32 devices in a mesh: section: 2 (over core), dp: 16 (over z, y, x).
Axes of the slice: x: 2, y: 2, z: 4, core: 2. Of those that a mesh axis runs over, the one named last changes fastest.
Arguments:
- inputs: bfloat16 [32, 128, 1024], P('dp'), may hold values from -6 to 6
- cotangent: bfloat16 [32, 128, 1024], P('dp'), may hold values from -6 to 6
- domain: int32 [32], P('dp'), may hold values from 0 to 15, as said below
- lengths: int32 [32], P('dp'), may hold values from 64 to 128
- steps_since_reset: int32 [1], replicated, may hold values from 0 to 49
- frozen_query_weight: bfloat16 [4, 1024, 3072], P('section', 'dp'), may hold values from -0.1875 to 0.1875
- frozen_output_weight: bfloat16 [4, 1024, 1024], P('section', 'dp'), may hold values from -0.75 to 0.75
- frozen_up_weight: bfloat16 [4, 1024, 4096], P('section', 'dp'), may hold values from -0.1875 to 0.1875
- frozen_down_weight: bfloat16 [4, 4096, 1024], P('section', 'dp'), may hold values from -0.09375 to 0.09375
- query_adapter_first: bfloat16 [4, 1024, 128], P('section'), may hold values from -0.1875 to 0.1875
- query_adapter_second: bfloat16 [4, 128, 3072], P('section'), may hold values from -0.5 to 0.5
- output_adapter_first: bfloat16 [4, 1024, 128], P('section'), may hold values from -0.1875 to 0.1875
- output_adapter_second: bfloat16 [4, 128, 1024], P('section'), may hold values from -2 to 2
- up_adapter_first: bfloat16 [4, 1024, 128], P('section'), may hold values from -0.1875 to 0.1875
- up_adapter_second: bfloat16 [4, 128, 4096], P('section'), may hold values from -0.5 to 0.5
- down_adapter_first: bfloat16 [4, 4096, 128], P('section'), may hold values from -0.09375 to 0.09375
- down_adapter_second: bfloat16 [4, 128, 1024], P('section'), may hold values from -0.5 to 0.5
- layer_norm_gain: float32 [4, 2, 1024], P('section'), may hold values from 0.5 to 1.5
- layer_norm_bias: float32 [4, 2, 1024], P('section'), may hold values from -1.5 to 1.5
Outputs:
- section_out: bfloat16 [2, 32, 128, 1024], P('section', 'dp')
- section_grad: float32 [2, 32, 128, 1024], P('section', 'dp')
- gradient_query_first: float32 [4, 1024, 128], P('section')
- gradient_query_second: float32 [4, 128, 3072], P('section')
- gradient_output_first: float32 [4, 1024, 128], P('section')
- gradient_output_second: float32 [4, 128, 1024], P('section')
- gradient_up_first: float32 [4, 1024, 128], P('section')
- gradient_up_second: float32 [4, 128, 4096], P('section')
- gradient_down_first: float32 [4, 4096, 128], P('section')
- gradient_down_second: float32 [4, 128, 1024], P('section')
- grad_norm_gain: float32 [4, 2, 1024], P('section')
- grad_norm_bias: float32 [4, 2, 1024], P('section')
- folded_query_weight: bfloat16 [4, 1024, 3072], P('section', 'dp')
- folded_output_weight: bfloat16 [4, 1024, 1024], P('section', 'dp')
- folded_up_weight: bfloat16 [4, 1024, 4096], P('section', 'dp')
- folded_down_weight: bfloat16 [4, 4096, 1024], P('section', 'dp')
- rms_stats: float32 [4, 3, 17], P('section')
The draws below stay inside these ranges and needn't reach their ends.
Inputs may be any that keep to these rules, and one draw needn't show every extreme that they name: `domain`: some domains may name no sequence.
All inputs are finite; a program needn't handle non-finite values.
Results may differ from the reference program's by a relative error of at most 0.022.
Values may be sent and summed in bfloat16 or wider, within the bound.
No kernel may reach another device: no remote copies, remote signals or barrier semaphores. Data moves between devices by JAX's collectives and lax.ppermute only.
A program may use at most 256 MiB of HBM per device.

```python
import jax
import jax.numpy as jnp
from jax import lax

MODEL_DIMENSION = 1024
HEADS = 16
HEAD_DIM = 64
FEEDFWD_UNITS = 4096
ROT = 16
ADAPTER_RANK = 128
DOMAINS = 16
LAYERS_SECTION = 2
SEQ = 128
WARM = 50
LAYER_TOTAL = 4
ROWS_DEV = 2
ROWS = 32


def draw_domain(key, part):
    first_key = jax.random.fold_in(key, 11)
    second_key = jax.random.fold_in(key, 23)
    unused_id = jax.random.randint(first_key, (), 1, DOMAINS - 1).astype(jnp.int32)
    raw_ids = jax.random.randint(second_key, (ROWS,), 0, DOMAINS - 1).astype(jnp.int32)
    shifted = raw_ids + (raw_ids >= unused_id).astype(jnp.int32)
    shifted = shifted.at[0].set(0)
    shifted = shifted.at[ROWS - 1].set(DOMAINS - 1)
    return shifted.astype(jnp.int32)


def touch_ends(drawn, rng, smallest, largest):
    spot = [jax.random.randint(jax.random.fold_in(rng, axis), (), 0, length) for axis, length in enumerate(drawn.shape)]
    widest = drawn.shape.index(max(drawn.shape))
    next_to = spot[:widest] + [(spot[widest] + 1) % drawn.shape[widest]] + spot[widest + 1:]
    return drawn.at[tuple(spot)].set(smallest).at[tuple(next_to)].set(largest)


def levels(rng, shape, cuts, least, top_value):
    def one(dim, parts):
        heights = jax.random.uniform(jax.random.fold_in(jax.random.fold_in(rng, 6), dim), (parts,), jnp.float32, least / len(cuts), top_value / len(cuts))
        return jnp.repeat(jnp.exp(heights), shape[dim] // parts).reshape((-1,) + (1,) * (len(shape) - dim - 1))

    factor_of = one(*cuts[0])
    for cut in cuts[1:]:
        factor_of = factor_of * one(*cut)
    return factor_of


def bell_draw(key, extent, scale, most, cuts=(), held_as=jnp.bfloat16):
    level = levels(key, extent, cuts, -0.22, 0.18) if cuts else 1.0
    entries = jax.random.normal(key, extent, jnp.float32) * scale * level
    return jnp.minimum(jnp.maximum(entries, -most), most).astype(held_as)


def setup_inputs(seed: int = 0) -> dict:
    seeds = jax.random.split(jax.random.key(seed), 20)
    return {
        "inputs": bell_draw(seeds[0], (ROWS, SEQ, MODEL_DIMENSION), 1.0, 6.0, ((0, 16),)),
        "cotangent": bell_draw(seeds[1], (ROWS, SEQ, MODEL_DIMENSION), 1.0, 6.0, ((0, 16),)),
        "domain": draw_domain(jax.random.fold_in(seeds[19], 71), 0),
        "lengths": touch_ends(jax.random.randint(seeds[3], (ROWS,), SEQ // 2, SEQ + 1), jax.random.fold_in(seeds[3], 1), SEQ // 2, SEQ).astype(jnp.int32),
        "steps_since_reset": jax.random.randint(seeds[4], (1,), 0, WARM).astype(jnp.int32),
        "frozen_query_weight": bell_draw(seeds[5], (LAYER_TOTAL, MODEL_DIMENSION, 3 * MODEL_DIMENSION), MODEL_DIMENSION ** -0.5, 0.1875, ((0, 2), (1, 16))),
        "frozen_output_weight": bell_draw(seeds[6], (LAYER_TOTAL, MODEL_DIMENSION, MODEL_DIMENSION), (MODEL_DIMENSION // 16) ** -0.5, 0.75, ((0, 2), (1, 16))),
        "frozen_up_weight": bell_draw(seeds[7], (LAYER_TOTAL, MODEL_DIMENSION, FEEDFWD_UNITS), MODEL_DIMENSION ** -0.5, 0.1875, ((0, 2), (1, 16))),
        "frozen_down_weight": bell_draw(seeds[8], (LAYER_TOTAL, FEEDFWD_UNITS, MODEL_DIMENSION), FEEDFWD_UNITS ** -0.5, 0.09375, ((0, 2), (1, 16))),
        "query_adapter_first": bell_draw(seeds[9], (LAYER_TOTAL, MODEL_DIMENSION, ADAPTER_RANK), MODEL_DIMENSION ** -0.5, 0.1875, ((0, 2),)),
        "query_adapter_second": bell_draw(seeds[10], (LAYER_TOTAL, ADAPTER_RANK, 3 * MODEL_DIMENSION), ADAPTER_RANK ** -0.5, 0.5, ((0, 2),)),
        "output_adapter_first": bell_draw(seeds[11], (LAYER_TOTAL, MODEL_DIMENSION, ADAPTER_RANK), MODEL_DIMENSION ** -0.5, 0.1875, ((0, 2),)),
        "output_adapter_second": bell_draw(seeds[12], (LAYER_TOTAL, ADAPTER_RANK, MODEL_DIMENSION), (ADAPTER_RANK // 16) ** -0.5, 2.0, ((0, 2),)),
        "up_adapter_first": bell_draw(seeds[13], (LAYER_TOTAL, MODEL_DIMENSION, ADAPTER_RANK), MODEL_DIMENSION ** -0.5, 0.1875, ((0, 2),)),
        "up_adapter_second": bell_draw(seeds[14], (LAYER_TOTAL, ADAPTER_RANK, FEEDFWD_UNITS), ADAPTER_RANK ** -0.5, 0.5, ((0, 2),)),
        "down_adapter_first": bell_draw(seeds[15], (LAYER_TOTAL, FEEDFWD_UNITS, ADAPTER_RANK), FEEDFWD_UNITS ** -0.5, 0.09375, ((0, 2),)),
        "down_adapter_second": bell_draw(seeds[16], (LAYER_TOTAL, ADAPTER_RANK, MODEL_DIMENSION), ADAPTER_RANK ** -0.5, 0.5, ((0, 2),)),
        "layer_norm_gain": jnp.clip(1.0 + 0.1 * jax.random.normal(seeds[17], (LAYER_TOTAL, 2, MODEL_DIMENSION), jnp.float32), 0.5, 1.5),
        "layer_norm_bias": bell_draw(seeds[18], (LAYER_TOTAL, 2, MODEL_DIMENSION), 0.3, 1.5, ((0, 2),), jnp.float32),
    }


@jax.custom_vjp
def low_rank_state(v):
    return lax.optimization_barrier(v.astype(jnp.bfloat16)).astype(jnp.float32)

@jax.custom_vjp
def low_rank_gradient(v):
    return v

def low_keep(v):
    return (low_rank_state(v), None)

def low_pass(kept, grad):
    return (grad,)

def back_keep(v):
    return (v, None)

def back_low(kept, grad):
    return (low_rank_state(grad),)
low_rank_state.defvjp(low_keep, low_pass)
low_rank_gradient.defvjp(back_keep, back_low)
adapter_scale = 0.5
norm_eps = 1e-05
peak_rate = 0.0002
masked_score = -1e+30

def precise_product(left, right):
    return jnp.matmul(left, right, precision=lax.Precision.HIGHEST)

def layer_norm(value, gain, bias):
    centred = value - lax.optimization_barrier(jnp.mean(value, axis=-1, keepdims=True))
    spread = lax.optimization_barrier(jnp.mean(centred * centred, axis=-1, keepdims=True))
    return centred * lax.rsqrt(spread + norm_eps) * gain + bias

def rotary(field):
    seq_len = field.shape[-3]
    half_rot = ROT // 2
    freqs = 10000.0 ** (-(jnp.arange(half_rot, dtype=jnp.float32) * 2.0 / ROT))
    angles = jnp.arange(seq_len, dtype=jnp.float32)[:, None] * freqs[None, :]
    cosine = jnp.concatenate([jnp.cos(angles), jnp.cos(angles)], -1)[:, None, :]
    sine = jnp.concatenate([jnp.sin(angles), jnp.sin(angles)], -1)[:, None, :]
    turned = field[..., :ROT]
    remain = field[..., ROT:]
    swapped = jnp.concatenate([-turned[..., half_rot:], turned[..., :half_rot]], -1)
    return jnp.concatenate([turned * cosine + swapped * sine, remain], -1)

def adapter_projection(saved_activations, dense_matmul, adapter_first_factor, adapter_second_factor):
    hidden_state = low_rank_gradient(low_rank_state(precise_product(saved_activations, adapter_first_factor)))
    return precise_product(saved_activations, dense_matmul) + adapter_scale * precise_product(hidden_state, adapter_second_factor)

def one_layer(residual, frozen, trainable_params, allowed, valid_mask):
    frozen_query_weight, frozen_output_weight, frozen_up_weight, frozen_down_weight = frozen
    query_first_factor, query_second_factor, output_first_factor, output_second_factor, up_first_factor, up_second_factor, down_first_factor, down_second_factor, gain, bias = trainable_params
    groups, seq_len, model_width = residual.shape
    attention_normed = low_rank_state(layer_norm(residual, gain[0], bias[0]))
    feed_normed = low_rank_state(layer_norm(residual, gain[1], bias[1]))
    combined_output = low_rank_gradient(adapter_projection(attention_normed, frozen_query_weight, query_first_factor, query_second_factor))
    combined_output = combined_output.reshape(groups, seq_len, 3, HEADS, HEAD_DIM)
    queries = low_rank_state(rotary(combined_output[:, :, 0]))
    key_heads = low_rank_state(rotary(combined_output[:, :, 1]))
    values = low_rank_state(combined_output[:, :, 2])
    scores = jnp.einsum('gqhd,gkhd->ghqk', queries, key_heads, precision=lax.Precision.HIGHEST) * HEAD_DIM ** (-0.5)
    scores = jnp.where(allowed, low_rank_gradient(scores), masked_score)
    probability = jax.nn.softmax(scores, axis=-1)
    merged_head_values = jnp.einsum('ghqk,gkhd->gqhd', low_rank_state(probability), values, precision=lax.Precision.HIGHEST)
    merged_head_values = low_rank_gradient(low_rank_state(merged_head_values.reshape(groups, seq_len, model_width)))
    attention_output = adapter_projection(merged_head_values, frozen_output_weight, output_first_factor, output_second_factor)
    upward_projection = low_rank_gradient(adapter_projection(feed_normed, frozen_up_weight, up_first_factor, up_second_factor))
    gelu_output = low_rank_gradient(low_rank_state(jax.nn.gelu(upward_projection, approximate=False)))
    feedforward_output = adapter_projection(gelu_output, frozen_down_weight, down_first_factor, down_second_factor)
    output = residual + low_rank_gradient(attention_output + feedforward_output)
    squared_values = jnp.stack([lax.optimization_barrier(jnp.sum(residual * residual, -1)), lax.optimization_barrier(jnp.sum(attention_output * attention_output, -1)), lax.optimization_barrier(jnp.sum(feedforward_output * feedforward_output, -1))], -1)
    row_sums = lax.optimization_barrier(jnp.sum(squared_values * valid_mask[..., None], axis=1))
    return (output, row_sums)

def forward(trainable_params, residual, probe, frozen, allowed, valid_mask):
    boundary = residual
    collected = []
    for layer_index in range(LAYER_TOTAL):
        if layer_index == LAYERS_SECTION:
            boundary = residual
            residual = low_rank_gradient(low_rank_state(residual) + probe)
        layer_frozen = tuple((matrix[layer_index] for matrix in frozen))
        layer_train = tuple((parameter[layer_index] for parameter in trainable_params))
        residual, row_sums = one_layer(residual, layer_frozen, layer_train, allowed, valid_mask)
        collected.append(row_sums)
    return (residual, (boundary, jnp.stack(collected, 1)))

def reference(inputs, cotangent, domain, lengths, steps_since_reset, frozen_query_weight, frozen_output_weight, frozen_up_weight, frozen_down_weight, query_adapter_first, query_adapter_second, output_adapter_first, output_adapter_second, up_adapter_first, up_adapter_second, down_adapter_first, down_adapter_second, layer_norm_gain, layer_norm_bias):
    frozen = tuple((matrix.astype(jnp.float32) for matrix in (frozen_query_weight, frozen_output_weight, frozen_up_weight, frozen_down_weight)))
    trainable_params = tuple((parameter.astype(jnp.float32) for parameter in (query_adapter_first, query_adapter_second, output_adapter_first, output_adapter_second, up_adapter_first, up_adapter_second, down_adapter_first, down_adapter_second, layer_norm_gain, layer_norm_bias)))
    group_rows = ROWS_DEV
    group_count = ROWS // group_rows
    positions = jnp.arange(SEQ)
    causal = positions[None, :] <= positions[:, None]

    def group_step(carry, item):
        group_inputs, group_cot, group_len = item
        valid_boolean_mask = positions[None, :] < group_len[:, None]
        allowed = causal[None, None] & valid_boolean_mask[:, None, None, :]
        valid_mask = valid_boolean_mask.astype(jnp.float32)
        probe = jnp.zeros(group_inputs.shape, jnp.float32)

        def run(train_params, start, probe_in):
            return forward(train_params, start, probe_in, frozen, allowed, valid_mask)
        final, pullback, (boundary, row_sums) = jax.vjp(run, trainable_params, group_inputs.astype(jnp.float32), probe, has_aux=True)
        grad_train, grad_input, grad_probe = pullback(group_cot.astype(jnp.float32) * valid_mask[..., None])
        carry = jax.tree.map(lambda total, extra: total + extra, carry, grad_train)
        return (carry, (boundary.astype(jnp.bfloat16), final.astype(jnp.bfloat16), grad_input, grad_probe, row_sums))
    zeros = jax.tree.map(jnp.zeros_like, trainable_params)
    items = (inputs.reshape(group_count, group_rows, SEQ, MODEL_DIMENSION), cotangent.reshape(group_count, group_rows, SEQ, MODEL_DIMENSION), lengths.reshape(group_count, group_rows))
    grads, (bounds, finals, grad_inputs, grad_probes, row_sums) = lax.scan(group_step, zeros, items)
    section_out = jnp.stack([bounds.reshape(ROWS, SEQ, MODEL_DIMENSION), finals.reshape(ROWS, SEQ, MODEL_DIMENSION)])
    section_grad = jnp.stack([grad_inputs.reshape(ROWS, SEQ, MODEL_DIMENSION), grad_probes.reshape(ROWS, SEQ, MODEL_DIMENSION)])
    row_sums = row_sums.reshape(ROWS, LAYER_TOTAL, 3)
    domain_table = (domain[:, None] == jnp.arange(DOMAINS)[None, :]).astype(jnp.float32)
    domain_sums = jnp.einsum('rn,rlq->lqn', domain_table, row_sums, precision=lax.Precision.HIGHEST)
    domain_counts = jnp.dot(lengths.astype(jnp.float32), domain_table, precision=lax.Precision.HIGHEST)
    all_sums = lax.optimization_barrier(jnp.sum(row_sums, axis=0))
    all_count = jnp.sum(lengths.astype(jnp.float32))
    rms_domain = jnp.sqrt(domain_sums / (jnp.maximum(domain_counts, 1.0) * MODEL_DIMENSION))
    rms_all = jnp.sqrt(all_sums / (all_count * MODEL_DIMENSION))
    rms_stats = jnp.concatenate([rms_domain, rms_all[..., None]], -1)
    rate = peak_rate * (steps_since_reset[0].astype(jnp.float32) + 1.0) / WARM

    def merge_adapter(dense_matmul, first_factor, second_factor, gradient_attention_normed, gradient_feed_normed):
        new_first = first_factor - rate * gradient_attention_normed
        new_second = second_factor - rate * gradient_feed_normed
        matrix_product = jnp.einsum('lkr,lrn->lkn', new_first, new_second, precision=lax.Precision.HIGHEST)
        return (dense_matmul + adapter_scale * matrix_product).astype(jnp.bfloat16)
    folded_query_weight = merge_adapter(frozen[0], trainable_params[0], trainable_params[1], grads[0], grads[1])
    folded_output_weight = merge_adapter(frozen[1], trainable_params[2], trainable_params[3], grads[2], grads[3])
    folded_up_weight = merge_adapter(frozen[2], trainable_params[4], trainable_params[5], grads[4], grads[5])
    folded_down_weight = merge_adapter(frozen[3], trainable_params[6], trainable_params[7], grads[6], grads[7])
    return (section_out, section_grad, grads[0], grads[1], grads[2], grads[3], grads[4], grads[5], grads[6], grads[7], grads[8], grads[9], folded_query_weight, folded_output_weight, folded_up_weight, folded_down_weight, rms_stats)
```

```python
from functools import partial

import jax
import jax.numpy as jnp
from jax import lax
from jax.experimental import pallas as pl
from jax.experimental.pallas import tpu as pltpu
from jax.sharding import PartitionSpec as P

HEADS = 16
HEAD_DIM = 64
ROT = 16
DOMAINS = 16
WARM = 50
RANK = 128
WIDE = 1024
UNITS = 12
HALF_UNITS = 6

adapter_scale = 0.5
norm_eps = 1e-05
peak_rate = 0.0002
masked_score = -1e30


def both_axes(value, pairs):
    return lax.ppermute(value, ("section", "dp"), pairs)


def flip_core(value):
    return lax.ppermute(value, "section", [(0, 1), (1, 0)])


def flip_place(value, mask):
    count = lax.axis_size("dp")
    return lax.ppermute(value, "dp", [(place, place ^ mask) for place in range(count)])


def split_units(matrices):
    query, output, upper, down = matrices
    rows = output.shape[0]
    return [
        query[:, :WIDE],
        query[:, WIDE : 2 * WIDE],
        query[:, 2 * WIDE :],
        output,
        upper[:, :WIDE],
        upper[:, WIDE : 2 * WIDE],
        upper[:, 2 * WIDE : 3 * WIDE],
        upper[:, 3 * WIDE :],
        down[:rows],
        down[rows : 2 * rows],
        down[2 * rows : 3 * rows],
        down[3 * rows :],
    ]


def gather_steps(piece, masks):
    held = piece[None]
    found = [0]
    for mask in masks:
        held = jnp.concatenate([held, flip_place(held, mask)], 0)
        found = found + [known ^ mask for known in found]
    return held, found


def assemble_kernel(info_ref, *refs):
    mine, theirs, outs = refs[:3], refs[3:6], refs[-4:]
    query_out, output_out, upper_out, down_out = outs
    rows = output_out.shape[0]

    def write(first, second):
        query_out[:, :WIDE] = first[0][0, 0]
        query_out[:, WIDE : 2 * WIDE] = first[0][0, 1]
        query_out[:, 2 * WIDE :] = first[1][0, 0]
        output_out[...] = first[1][0, 1]
        upper_out[:, :WIDE] = first[2][0, 0]
        upper_out[:, WIDE : 2 * WIDE] = first[2][0, 1]
        upper_out[:, 2 * WIDE : 3 * WIDE] = second[0][0, 0]
        upper_out[:, 3 * WIDE :] = second[0][0, 1]
        down_out[:rows] = second[1][0, 0]
        down_out[rows : 2 * rows] = second[1][0, 1]
        down_out[2 * rows : 3 * rows] = second[2][0, 0]
        down_out[3 * rows :] = second[2][0, 1]

    @pl.when(info_ref[0, 0] == 0)
    def _():
        write(mine, theirs)

    @pl.when(info_ref[0, 0] != 0)
    def _():
        write(theirs, mine)


def assemble(info, mine, theirs, rows, count, into):
    blocks = mine[0].shape[0]

    def source(part):
        return pl.BlockSpec((1, 2, rows, WIDE), lambda step, info_ref: (info_ref[2 + part, step], 0, 0, 0))

    def target(height, width):
        return pl.BlockSpec((height, width), lambda step, info_ref: (info_ref[1, step], 0))

    total = rows * count
    shapes = [(total, 3 * WIDE), (total, WIDE), (total, 4 * WIDE), (4 * total, WIDE)]
    extra = [] if into is None else list(into)
    size = 2 * 2 * UNITS * rows * WIDE * blocks
    return pl.pallas_call(
        assemble_kernel,
        out_shape=[jax.ShapeDtypeStruct(shape, jnp.bfloat16) for shape in shapes],
        grid_spec=pltpu.PrefetchScalarGridSpec(
            num_scalar_prefetch=1,
            grid=(blocks,),
            in_specs=[source(0), source(1), source(2)] * 2
            + [pl.BlockSpec(memory_space=pl.ANY)] * len(extra),
            out_specs=[target(rows, 3 * WIDE), target(rows, WIDE), target(rows, 4 * WIDE), target(4 * rows, WIDE)],
        ),
        input_output_aliases={7 + index: index for index in range(len(extra))},
        cost_estimate=pl.CostEstimate(flops=0, bytes_accessed=size, transcendentals=0),
        name="assemble",
    )(info, *mine, *theirs, *extra)


def rotations(masks):
    return [[masks[(start + index) % len(masks)] for index in range(len(masks))] for start in range(3)]


def gather_layer(matrices, core, stage, low, home, count, masks):
    half = count // 2
    units = split_units(matrices)
    rows = units[0].shape[0]
    first, second = jnp.stack(units[:HALF_UNITS]), jnp.stack(units[HALF_UNITS:])
    same = jnp.where(stage == 0, first, second)
    other = jnp.where(stage == 0, second, first)
    places = [(place // half, place) for place in range(count)]
    near = [(here * count + place, (1 - here) * count + place) for here, place in places]
    far = [((1 - here) * count + place, (1 - here) * count + (place ^ half)) for here, place in places]
    cross = [((1 - here) * count + place, here * count + (place ^ half)) for here, place in places]
    from_first = both_axes(other, near + far)
    from_second = both_axes(same, cross)
    own = jnp.where(home, same, from_first)
    partner = jnp.where(home, from_first, from_second)
    whole = None
    for which, block in enumerate((own, partner)):
        base = jnp.where(stage == which, 0, half)
        mine, theirs, rows_of = [], [], []
        order = None
        for part, turn in enumerate(rotations(masks)):
            held, found = gather_steps(block[2 * part : 2 * part + 2], turn)
            mine.append(held)
            theirs.append(flip_core(held))
            if order is None:
                order = found
            rows_of.append([found.index(mask) for mask in order])
        blocks = jnp.asarray(order, jnp.int32) ^ low
        info = jnp.stack(
            [jnp.full((half,), core, jnp.int32), blocks + base]
            + [jnp.asarray(row, jnp.int32) for row in rows_of]
        )
        whole = assemble(info, mine, theirs, rows, count, whole)
    return whole


def part_rows(total):
    first = (total // 3 + 7) // 8 * 8
    return [(0, first), (first, 2 * first), (2 * first, total)]


def reduce_section(parts, section, core, stage, low, count, masks):
    half = count // 2
    rounded = parts.astype(jnp.bfloat16)
    columns = parts.shape[1] // 2
    send = jnp.where(core == 0, rounded[:, columns:], rounded[:, :columns])
    keep = jnp.where(core == 0, parts[:, :columns], parts[:, columns:])
    held = (keep + flip_core(send).astype(jnp.float32)).astype(jnp.bfloat16)
    whole = []
    for (begin, end), turn in zip(part_rows(parts.shape[0]), rotations(masks)):
        slab = held[begin:end]
        for mask in turn:
            columns = slab.shape[1] // 2
            upper_side = (low & mask) != 0
            left, right = slab[:, :columns], slab[:, columns:]
            send = jnp.where(upper_side, left, right)
            keep = jnp.where(upper_side, right, left)
            slab = (keep.astype(jnp.float32) + flip_place(send, mask).astype(jnp.float32)).astype(jnp.bfloat16)
        across = flip_place(slab, half)
        slab = jnp.where(stage == section, slab, across)
        for mask in reversed(turn):
            upper_side = (low & mask) != 0
            there = flip_place(slab, mask)
            slab = jnp.concatenate(
                [jnp.where(upper_side, there, slab), jnp.where(upper_side, slab, there)], 1
            )
        whole.append(slab)
    here = jnp.concatenate(whole, 0)
    there = lax.ppermute(here, "section", [(1 - section, section)])
    return jnp.concatenate([here, there] if section == 0 else [there, here], 1)


def layer_norm(value, gain, bias):
    centred = value - jnp.mean(value, axis=-1, keepdims=True)
    spread = jnp.mean(centred * centred, axis=-1, keepdims=True)
    return centred * lax.rsqrt(spread + norm_eps) * gain + bias


def both_norms(value, gain_pair, bias_pair):
    return (
        layer_norm(value, gain_pair[0], bias_pair[0]),
        layer_norm(value, gain_pair[1], bias_pair[1]),
    )


def rotary(field):
    seq_len = field.shape[-3]
    half_rot = ROT // 2
    freqs = 10000.0 ** (-(jnp.arange(half_rot, dtype=jnp.float32) * 2.0 / ROT))
    angles = jnp.arange(seq_len, dtype=jnp.float32)[:, None] * freqs[None, :]
    cosine = jnp.concatenate([jnp.cos(angles), jnp.cos(angles)], -1)[:, None, :]
    sine = jnp.concatenate([jnp.sin(angles), jnp.sin(angles)], -1)[:, None, :]
    turned = field[..., :ROT]
    remain = field[..., ROT:]
    swapped = jnp.concatenate([-turned[..., half_rot:], turned[..., :half_rot]], -1)
    return jnp.concatenate([turned * cosine + swapped * sine, remain], -1)


def adapter_forward(saved_activations, dense_matmul, adapter_first_factor, adapter_second_factor):
    hidden_state = jnp.dot(
        saved_activations, adapter_first_factor, preferred_element_type=jnp.float32
    ).astype(jnp.bfloat16)
    final_result = jnp.dot(saved_activations, dense_matmul, preferred_element_type=jnp.float32)
    final_result = final_result + adapter_scale * jnp.dot(
        hidden_state, adapter_second_factor, preferred_element_type=jnp.float32
    )
    return (final_result, hidden_state)


def adapter_backward(
    gradient_layer_output,
    saved_activations,
    hidden_state,
    dense_matmul,
    adapter_first_factor,
    adapter_second_factor,
):
    gradient_hidden_state = (
        adapter_scale
        * jnp.einsum(
            "hfq,tq->hft",
            gradient_layer_output,
            adapter_second_factor,
            preferred_element_type=jnp.float32,
        )
    ).astype(jnp.bfloat16)
    gradient_feed_normed = adapter_scale * jnp.einsum(
        "rsm,rsn->mn", hidden_state, gradient_layer_output, preferred_element_type=jnp.float32
    )
    gradient_attention_normed = jnp.einsum(
        "rsm,rsk->mk", gradient_hidden_state, saved_activations, preferred_element_type=jnp.float32
    )
    grad_inputs = jnp.einsum(
        "rsn,kn->rsk", gradient_layer_output, dense_matmul, preferred_element_type=jnp.float32
    )
    grad_inputs = grad_inputs + jnp.einsum(
        "efj,lj->efl",
        gradient_hidden_state,
        adapter_first_factor,
        preferred_element_type=jnp.float32,
    )
    return (grad_inputs, gradient_attention_normed, gradient_feed_normed)


def attention_mask(valid_boolean_mask):
    seq_len = valid_boolean_mask.shape[-1]
    positions = jnp.arange(seq_len)
    causal = positions[None, :] <= positions[:, None]
    return causal[None, None] & valid_boolean_mask[:, None, None, :]


def layer_forward(residual, weights, valid_boolean_mask):
    (
        frozen_query_weight,
        frozen_output_weight,
        frozen_up_weight,
        frozen_down_weight,
        query_first_factor,
        query_second_factor,
        output_first_factor,
        output_second_factor,
        up_first_factor,
        up_second_factor,
        down_first_factor,
        down_second_factor,
        gain,
        bias,
    ) = weights
    row_count, seq_len, model_width = residual.shape
    attention_normed = layer_norm(residual, gain[0], bias[0]).astype(jnp.bfloat16)
    feed_normed = layer_norm(residual, gain[1], bias[1]).astype(jnp.bfloat16)
    combined_output, hidden_query_rank = adapter_forward(
        attention_normed, frozen_query_weight, query_first_factor, query_second_factor
    )
    combined_output = combined_output.reshape(row_count, seq_len, 3, HEADS, HEAD_DIM)
    queries = rotary(combined_output[:, :, 0]).astype(jnp.bfloat16)
    key_heads = rotary(combined_output[:, :, 1]).astype(jnp.bfloat16)
    values = combined_output[:, :, 2].astype(jnp.bfloat16)
    allowed = attention_mask(valid_boolean_mask)
    scores = jnp.einsum(
        "rqhd,rkhd->rhqk", queries, key_heads, preferred_element_type=jnp.float32
    ) * HEAD_DIM ** (-0.5)
    scores = jnp.where(allowed, scores, masked_score)
    top_score = jnp.max(scores, axis=-1, keepdims=True)
    expo_score = jnp.exp(scores - top_score)
    exp_total = jnp.sum(expo_score, axis=-1, keepdims=True)
    probability = expo_score / exp_total
    log_total = top_score + jnp.log(exp_total)
    merged_head_values = jnp.einsum(
        "rhqk,rkhd->rqhd",
        probability.astype(jnp.bfloat16),
        values,
        preferred_element_type=jnp.float32,
    )
    merged_head_values = merged_head_values.reshape(row_count, seq_len, model_width).astype(
        jnp.bfloat16
    )
    attention_output, hidden_output_rank = adapter_forward(
        merged_head_values, frozen_output_weight, output_first_factor, output_second_factor
    )
    upward_projection, hidden_up_rank = adapter_forward(
        feed_normed, frozen_up_weight, up_first_factor, up_second_factor
    )
    gelu_output = jax.nn.gelu(upward_projection, approximate=False).astype(jnp.bfloat16)
    feedforward_output, hidden_down_rank = adapter_forward(
        gelu_output, frozen_down_weight, down_first_factor, down_second_factor
    )
    output = residual + (attention_output + feedforward_output)
    squared_values = jnp.stack(
        [
            jnp.sum(residual * residual, -1),
            jnp.sum(attention_output * attention_output, -1),
            jnp.sum(feedforward_output * feedforward_output, -1),
        ],
        -1,
    )
    row_sums = jnp.einsum(
        "nx,nxo->no",
        valid_boolean_mask.astype(jnp.float32),
        squared_values,
        precision=lax.Precision.HIGHEST,
    )
    kept_state = (
        residual,
        queries,
        key_heads,
        values,
        log_total,
        merged_head_values,
        upward_projection,
        hidden_query_rank,
        hidden_output_rank,
        hidden_up_rank,
        hidden_down_rank,
    )
    return (output, kept_state, row_sums)


def layer_backward(gradient_layer_output, kept_state, weights, valid_boolean_mask):
    (
        frozen_query_weight,
        frozen_output_weight,
        frozen_up_weight,
        frozen_down_weight,
        query_first_factor,
        query_second_factor,
        output_first_factor,
        output_second_factor,
        up_first_factor,
        up_second_factor,
        down_first_factor,
        down_second_factor,
        gain,
        bias,
    ) = weights
    (
        residual,
        queries,
        key_heads,
        values,
        log_total,
        merged_head_values,
        upward_projection,
        hidden_query_rank,
        hidden_output_rank,
        hidden_up_rank,
        hidden_down_rank,
    ) = kept_state
    row_count, seq_len, model_width = residual.shape
    (attention_normed, feed_normed), norm_back = jax.vjp(both_norms, residual, gain, bias)
    attention_normed = attention_normed.astype(jnp.bfloat16)
    feed_normed = feed_normed.astype(jnp.bfloat16)
    grad_branch = gradient_layer_output.astype(jnp.bfloat16)
    gelu_output, gelu_back = jax.vjp(partial(jax.nn.gelu, approximate=False), upward_projection)
    gelu_output = gelu_output.astype(jnp.bfloat16)
    gradient_gelu_output, gradient_down_first, gradient_down_second = adapter_backward(
        grad_branch,
        gelu_output,
        hidden_down_rank,
        frozen_down_weight,
        down_first_factor,
        down_second_factor,
    )
    rounded_activated = lax.optimization_barrier(gradient_gelu_output.astype(jnp.bfloat16)).astype(
        jnp.float32
    )
    grad_upper = gelu_back(rounded_activated)[0].astype(jnp.bfloat16)
    gradient_feed_normed, gradient_up_first, gradient_up_second = adapter_backward(
        grad_upper, feed_normed, hidden_up_rank, frozen_up_weight, up_first_factor, up_second_factor
    )
    gradient_mixed_heads, gradient_output_first, gradient_output_second = adapter_backward(
        grad_branch,
        merged_head_values,
        hidden_output_rank,
        frozen_output_weight,
        output_first_factor,
        output_second_factor,
    )
    gradient_mixed_heads = gradient_mixed_heads.astype(jnp.bfloat16).reshape(
        row_count, seq_len, HEADS, HEAD_DIM
    )
    allowed = attention_mask(valid_boolean_mask)
    scale_factor = HEAD_DIM ** (-0.5)
    scores = (
        jnp.einsum("rqhd,rkhd->rhqk", queries, key_heads, preferred_element_type=jnp.float32)
        * scale_factor
    )
    probability = jnp.where(allowed, jnp.exp(scores - log_total), 0.0)
    grad_probs = jnp.einsum(
        "rqhd,rkhd->rhqk", gradient_mixed_heads, values, preferred_element_type=jnp.float32
    )
    grad_values = jnp.einsum(
        "rhqk,rqhd->rkhd",
        probability.astype(jnp.bfloat16),
        gradient_mixed_heads,
        preferred_element_type=jnp.float32,
    )
    grad_scores = probability * (
        grad_probs - jnp.sum(probability * grad_probs, axis=-1, keepdims=True)
    )
    grad_scores = grad_scores.astype(jnp.bfloat16)
    grad_queries = (
        jnp.einsum("rhqk,rkhd->rqhd", grad_scores, key_heads, preferred_element_type=jnp.float32)
        * scale_factor
    )
    grad_keys = (
        jnp.einsum("rhqk,rqhd->rkhd", grad_scores, queries, preferred_element_type=jnp.float32)
        * scale_factor
    )
    rotary_back = jax.vjp(rotary, jnp.zeros(grad_queries.shape, jnp.float32))[1]
    grad_joint = jnp.stack(
        [rotary_back(grad_queries)[0], rotary_back(grad_keys)[0], grad_values], 2
    )
    grad_joint = grad_joint.reshape(row_count, seq_len, 3 * model_width).astype(jnp.bfloat16)
    gradient_attention_normed, gradient_query_first, gradient_query_second = adapter_backward(
        grad_joint,
        attention_normed,
        hidden_query_rank,
        frozen_query_weight,
        query_first_factor,
        query_second_factor,
    )
    grad_residual, grad_gain, grad_bias = norm_back(
        (gradient_attention_normed, gradient_feed_normed)
    )
    layer_grads = (
        gradient_query_first,
        gradient_query_second,
        gradient_output_first,
        gradient_output_second,
        gradient_up_first,
        gradient_up_second,
        gradient_down_first,
        gradient_down_second,
        grad_gain,
        grad_bias,
    )
    return (gradient_layer_output + grad_residual, layer_grads)


def gradient_block(layer_grads, table):
    (
        query_first,
        query_second,
        output_first,
        output_second,
        up_first,
        up_second,
        down_first,
        down_second,
        gain,
        bias,
    ) = layer_grads
    main = jnp.concatenate(
        [query_first, output_first, up_first, down_first, query_second, output_second, up_second, down_second],
        1,
    )
    extra = jnp.concatenate([gain.reshape(1, -1), bias.reshape(1, -1), table.reshape(1, -1)], 1)
    extra = jnp.pad(extra, ((0, 7), (0, main.shape[1] - extra.shape[1])))
    return jnp.concatenate([main, extra], 0)


def unpack_gradients(block):
    offset = 0
    firsts = []
    for width in (1, 1, 1, 4):
        firsts.append(block[:RANK, offset : offset + width * WIDE].astype(jnp.float32).T)
        offset = offset + width * WIDE
    seconds = []
    for width in (3, 1, 4, 1):
        seconds.append(block[:RANK, offset : offset + width * WIDE].astype(jnp.float32))
        offset = offset + width * WIDE
    row = block[RANK].astype(jnp.float32)
    gain = row[: 2 * WIDE].reshape(2, WIDE)
    bias = row[2 * WIDE : 4 * WIDE].reshape(2, WIDE)
    table = row[4 * WIDE : 4 * WIDE + 3 * (DOMAINS + 1)].reshape(3, DOMAINS + 1)
    return [part for pair in zip(firsts, seconds) for part in pair] + [gain, bias, table]


def shards(
    inputs,
    cotangent,
    domain,
    lengths,
    steps_since_reset,
    frozen_query_weight,
    frozen_output_weight,
    frozen_up_weight,
    frozen_down_weight,
    query_adapter_first,
    query_adapter_second,
    output_adapter_first,
    output_adapter_second,
    up_adapter_first,
    up_adapter_second,
    down_adapter_first,
    down_adapter_second,
    layer_norm_gain,
    layer_norm_bias,
):
    core = lax.axis_index("section")
    place = lax.axis_index("dp")
    count = lax.axis_size("dp")
    half = count // 2
    stage = place // half
    low = place % half
    home = core == stage
    masks = [1 << bit for bit in range(half.bit_length() - 1)]
    frozen = (frozen_query_weight, frozen_output_weight, frozen_up_weight, frozen_down_weight)
    trained = (
        query_adapter_first,
        query_adapter_second,
        output_adapter_first,
        output_adapter_second,
        up_adapter_first,
        up_adapter_second,
        down_adapter_first,
        down_adapter_second,
        layer_norm_gain,
        layer_norm_bias,
    )
    local_layers = frozen_query_weight.shape[0]
    rows_dev, seq_len, model_width = inputs.shape
    span = frozen_output_weight.shape[1]

    dense = [
        gather_layer([matrix[layer] for matrix in frozen], core, stage, low, home, count, masks)
        for layer in range(local_layers)
    ]
    to_sibling = [
        ((index // half) * count + index, (1 - index // half) * count + index) for index in range(count)
    ]
    weights = []
    for layer in range(local_layers):
        adapters = tuple(
            jnp.where(home, parameter[layer], both_axes(parameter[layer], to_sibling))
            for parameter in trained
        )
        weights.append(tuple(dense[layer]) + adapters)

    away = [
        ((1 - index // half) * count + index, (index // half) * count + (index ^ half))
        for index in range(count)
    ]
    visiting = both_axes(jnp.where(stage == 0, cotangent, inputs), away)
    facts = jnp.stack([lengths, domain])
    facts = jnp.where(home, facts, both_axes(facts, away))
    group_lengths, group_domain = facts[0], facts[1]
    start = jnp.where(home, inputs, visiting).astype(jnp.float32)
    valid = jnp.arange(seq_len)[None, :] < group_lengths[:, None]
    end_grad = jnp.where(home, cotangent, visiting).astype(jnp.float32)
    end_grad = jnp.where(stage == 1, end_grad * valid[..., None].astype(jnp.float32), 0.0)
    table = (group_domain[:, None] == jnp.arange(DOMAINS)[None, :]).astype(jnp.float32)
    table = jnp.concatenate([table, jnp.ones((rows_dev, 1), jnp.float32)], 1)

    own_table = (domain[:, None] == jnp.arange(DOMAINS)[None, :]).astype(jnp.float32)
    own_table = jnp.concatenate([own_table, jnp.ones((rows_dev, 1), jnp.float32)], 1)
    counts = jnp.sum(own_table * lengths.astype(jnp.float32)[:, None], axis=0)
    for mask in masks + [half]:
        counts = counts + flip_place(counts, mask)

    def stage_forward(residual):
        kept, sums = [], []
        for layer in range(local_layers):
            residual, kept_state, row_sums = layer_forward(residual, weights[layer], valid)
            kept.append(kept_state)
            sums.append(row_sums)
        return residual, kept, sums

    def stage_backward(gradient, kept, section):
        blocks = [None] * local_layers
        for layer in reversed(range(local_layers)):
            gradient, layer_grads = layer_backward(gradient, kept[layer], weights[layer], valid)
            block = gradient_block(layer_grads, tables[layer])
            blocks[layer] = reduce_section(block, section, core, stage, low, count, masks)
        return gradient, blocks

    boundary, _, _ = stage_forward(start)
    boundary = boundary.astype(jnp.bfloat16)
    forward_pairs = [(index, index + half) for index in range(half)]
    received = lax.ppermute(boundary, "dp", forward_pairs)
    entry = jnp.where(stage == 0, start, received.astype(jnp.float32))
    final, kept, sums = stage_forward(entry)
    tables = [
        jnp.einsum("rq,rn->qn", row_sums, table, precision=lax.Precision.HIGHEST) for row_sums in sums
    ]
    final = final.astype(jnp.bfloat16)
    out_pairs = [(count + index + half, index + half) for index in range(half)]
    out_pairs = out_pairs + [(index + half, count + index) for index in range(half)]
    visiting = both_axes(jnp.where(core == 0, final, received), out_pairs)
    section_out = jnp.where(home, jnp.where(stage == 0, boundary, final), visiting)[None]

    gradient, late_blocks = stage_backward(end_grad, kept, 1)
    sent = gradient.astype(jnp.bfloat16)
    came_back = lax.ppermute(sent, "dp", [(after, before) for before, after in forward_pairs])
    gradient, early_blocks = stage_backward(
        jnp.where(stage == 0, came_back.astype(jnp.float32), 0.0), kept, 0
    )
    grad_pairs = [(index, count + index) for index in range(half)]
    grad_pairs = grad_pairs + [(count + index, index + half) for index in range(half)]
    visiting = both_axes(
        jnp.where(core == 0, came_back, gradient.astype(jnp.bfloat16)), grad_pairs
    ).astype(jnp.float32)
    section_grad = jnp.where(
        home, jnp.where(stage == 0, gradient, sent.astype(jnp.float32)), visiting
    )[None]

    unpacked = [
        unpack_gradients(jnp.where(core == 0, early, late))
        for early, late in zip(early_blocks, late_blocks)
    ]
    stacked = [jnp.stack([layer[index] for layer in unpacked]) for index in range(11)]
    table_sums = stacked.pop()
    bounded = jnp.concatenate([jnp.maximum(counts[:DOMAINS], 1.0), counts[DOMAINS:]])
    rms_stats = jnp.sqrt(table_sums / (bounded * model_width))
    rate = peak_rate * (steps_since_reset[0].astype(jnp.float32) + 1.0) / WARM

    def merge_adapter(matrix, first_factor, second_factor, first_grad, second_grad):
        row_span = matrix.shape[1]
        first_rows = lax.dynamic_slice_in_dim(
            first_factor, place * row_span, row_span, 1
        ).astype(jnp.float32) - rate * lax.dynamic_slice_in_dim(first_grad, place * row_span, row_span, 1)
        new_second = second_factor.astype(jnp.float32) - rate * second_grad
        product = jnp.einsum("lkr,lrn->lkn", first_rows, new_second, precision=lax.Precision.HIGHEST)
        return (matrix.astype(jnp.float32) + adapter_scale * product).astype(jnp.bfloat16)

    folded = [
        merge_adapter(
            frozen[index],
            trained[2 * index],
            trained[2 * index + 1],
            stacked[2 * index],
            stacked[2 * index + 1],
        )
        for index in range(4)
    ]
    return (section_out, section_grad, *stacked, *folded, rms_stats)


def solution(mesh):
    across = P("dp", None, None)
    copied = P("section", None, None)
    split = P("section", "dp", None)
    wide = P("section", "dp", None, None)
    return jax.shard_map(
        shards,
        mesh=mesh,
        in_specs=(across, across, P("dp"), P("dp"), P()) + (split,) * 4 + (copied,) * 10,
        out_specs=(wide, wide) + (copied,) * 10 + (split,) * 4 + (copied,),
        check_vma=False,
    )
```

```python
from functools import partial

import jax
import jax.numpy as jnp
from jax import lax
from jax.experimental import pallas as pl
from jax.experimental.pallas import tpu as pltpu
from jax.sharding import PartitionSpec as P

HEADS = 16
HEAD_DIM = 64
ROT = 16
DOMAINS = 16
WARM = 50
RANK = 128
WIDE = 1024
UNITS = 12
HALF_UNITS = 6

adapter_scale = 0.5
norm_eps = 1e-05
peak_rate = 0.0002
masked_score = -1e30


def both_axes(value, pairs):
    return lax.ppermute(value, ("section", "dp"), pairs)


def tie(value, *others):
    return lax.optimization_barrier((value, others))[0]


def flip_place(value, mask):
    count = lax.axis_size("dp")
    return lax.ppermute(value, "dp", [(place, place ^ mask) for place in range(count)])


def flip_core(value):
    return lax.ppermute(value, "section", [(0, 1), (1, 0)])


def split_units(matrices):
    query, output, upper, down = matrices
    rows = output.shape[0]
    return [
        query[:, :WIDE],
        query[:, WIDE : 2 * WIDE],
        query[:, 2 * WIDE :],
        output,
        upper[:, :WIDE],
        upper[:, WIDE : 2 * WIDE],
        upper[:, 2 * WIDE : 3 * WIDE],
        upper[:, 3 * WIDE :],
        down[:rows],
        down[rows : 2 * rows],
        down[2 * rows : 3 * rows],
        down[3 * rows :],
    ]


def rotations(masks):
    return [[masks[(start + index) % len(masks)] for index in range(len(masks))] for start in range(3)]


def assemble_kernel(info_ref, *refs):
    mine, theirs, outs = refs[:3], refs[3:6], refs[-4:]
    query_out, output_out, upper_out, down_out = outs
    rows = output_out.shape[0]

    def write(first, second):
        query_out[:, :WIDE] = first[0][0, 0]
        query_out[:, WIDE : 2 * WIDE] = first[0][0, 1]
        query_out[:, 2 * WIDE :] = first[1][0, 0]
        output_out[...] = first[1][0, 1]
        upper_out[:, :WIDE] = first[2][0, 0]
        upper_out[:, WIDE : 2 * WIDE] = first[2][0, 1]
        upper_out[:, 2 * WIDE : 3 * WIDE] = second[0][0, 0]
        upper_out[:, 3 * WIDE :] = second[0][0, 1]
        down_out[:rows] = second[1][0, 0]
        down_out[rows : 2 * rows] = second[1][0, 1]
        down_out[2 * rows : 3 * rows] = second[2][0, 0]
        down_out[3 * rows :] = second[2][0, 1]

    @pl.when(info_ref[0, 0] == 0)
    def _():
        write(mine, theirs)

    @pl.when(info_ref[0, 0] != 0)
    def _():
        write(theirs, mine)


def assemble(info, mine, theirs, rows, count, into):
    blocks = mine[0].shape[0]

    def source(part):
        return pl.BlockSpec((1, 2, rows, WIDE), lambda step, info_ref: (info_ref[2 + part, step], 0, 0, 0))

    def target(height, width):
        return pl.BlockSpec((height, width), lambda step, info_ref: (info_ref[1, step], 0))

    total = rows * count
    shapes = [(total, 3 * WIDE), (total, WIDE), (total, 4 * WIDE), (4 * total, WIDE)]
    extra = [] if into is None else list(into)
    size = 2 * 2 * UNITS * rows * WIDE * blocks
    return pl.pallas_call(
        assemble_kernel,
        out_shape=[jax.ShapeDtypeStruct(shape, jnp.bfloat16) for shape in shapes],
        grid_spec=pltpu.PrefetchScalarGridSpec(
            num_scalar_prefetch=1,
            grid=(blocks,),
            in_specs=[source(0), source(1), source(2)] * 2
            + [pl.BlockSpec(memory_space=pl.ANY)] * len(extra),
            out_specs=[target(rows, 3 * WIDE), target(rows, WIDE), target(rows, 4 * WIDE), target(4 * rows, WIDE)],
        ),
        input_output_aliases={7 + index: index for index in range(len(extra))},
        cost_estimate=pl.CostEstimate(flops=0, bytes_accessed=size, transcendentals=0),
        name="assemble",
    )(info, *mine, *theirs, *extra)


class Steps:
    def __init__(self):
        self.ended = ()

    def run(self, *moves):
        values = tuple(value for value, _ in moves)
        if self.ended:
            values = tie(values, *self.ended)
        self.ended = tuple(send(value) for value, (_, send) in zip(values, moves))
        return list(self.ended)


def pick_halves(matrices, stage):
    units = split_units(matrices)
    first, second = jnp.stack(units[:HALF_UNITS]), jnp.stack(units[HALF_UNITS:])
    return jnp.where(stage == 0, first, second), jnp.where(stage == 0, second, first)


class Gather:
    def __init__(self, block, masks):
        self.held = [block[2 * part : 2 * part + 2][None] for part in range(3)]
        self.found = [[0], [0], [0]]
        self.turns = rotations(masks)
        self.step = 0

    def moves(self):
        return [
            (self.held[part], partial(flip_place, mask=self.turns[part][self.step])) for part in range(3)
        ]

    def take(self, there):
        for part in range(3):
            self.held[part] = jnp.concatenate([self.held[part], there[part]], 0)
            mask = self.turns[part][self.step]
            self.found[part] = self.found[part] + [known ^ mask for known in self.found[part]]
        self.step = self.step + 1
        return there[3:]


def part_rows(total):
    first = (total // 3 + 15) // 16 * 16
    return [(0, first), (first, 2 * first), (2 * first, total)]


def side(value, which, axis=1):
    size = value.shape[axis] // 2
    return lax.dynamic_slice_in_dim(value, which * size, size, axis)


def total_of(first, second):
    return (first.astype(jnp.float32) + second.astype(jnp.float32)).astype(jnp.bfloat16)


class Scatter:
    def __init__(self, blocks, section, core, low, count, masks):
        middle = count // 2
        self.inside = [place for place in range(count) if place // middle == section]
        self.swap = [(here * count + place, (1 - here) * count + place) for here in range(2) for place in self.inside]
        self.blocks, self.core, self.low = blocks, core, low
        self.turns = rotations(masks)
        self.step = -1

    def moves(self):
        if self.step < 0:
            return [(side(block, 1 - self.core), partial(both_axes, pairs=self.swap)) for block in self.blocks]
        moves = []
        for slab, turn in zip(self.slabs, self.turns):
            mask = turn[self.step]
            pairs = [(place, place ^ mask) for place in self.inside]
            lower_side = ((self.low & mask) == 0).astype(jnp.int32)
            moves.append((side(slab, lower_side), partial(lax.ppermute, axis_name="dp", perm=pairs)))
        return moves

    def take(self, there):
        if self.step < 0:
            used = len(self.blocks)
            halves = [total_of(side(block, self.core), part) for block, part in zip(self.blocks, there)]
            self.slabs = [
                jnp.concatenate([part[begin:end] for part in halves], 0)
                for begin, end in part_rows(halves[0].shape[0])
            ]
        else:
            used = 3
            for part in range(3):
                upper_side = ((self.low & self.turns[part][self.step]) != 0).astype(jnp.int32)
                self.slabs[part] = total_of(side(self.slabs[part], upper_side), there[part])
        self.step = self.step + 1
        return there[used:]


def scatter_section(blocks, section, core, low, count, masks, steps):
    scatter = Scatter(blocks, section, core, low, count, masks)
    for step in range(len(masks) + 1):
        scatter.take(steps.run(*scatter.moves()))
    return scatter.slabs


class Spread:
    def __init__(self, slabs, section, masks, count, stage):
        middle = count // 2
        self.across = [(place, place ^ middle) for place in range(count) if place // middle == section]
        self.held, self.section, self.here = slabs, section, stage == section
        self.turns = [list(reversed(turn)) for turn in rotations(masks)]
        self.step = -1

    def done(self):
        return self.step > len(self.turns[0])

    def moves(self):
        if self.step < 0:
            return [(slab, partial(lax.ppermute, axis_name="dp", perm=self.across)) for slab in self.held]
        if self.step == len(self.turns[0]):
            pairs = [(1 - self.section, self.section)]
            return [(held, partial(lax.ppermute, axis_name="section", perm=pairs)) for held in self.held]
        return [(held, partial(flip_place, mask=turn[self.step])) for held, turn in zip(self.held, self.turns)]

    def take(self, there):
        if self.step < 0:
            self.held = [jnp.where(self.here, held, part)[None] for held, part in zip(self.held, there)]
        elif self.step == len(self.turns[0]):
            self.theirs = there[:3]
        else:
            self.held = [jnp.concatenate([held, part], 0) for held, part in zip(self.held, there)]
        self.step = self.step + 1
        return there[3:]


def place_kernel(section, layers, info_ref, *refs):
    mine, theirs, olds, outs = refs[:3], refs[3:6], refs[6:-layers], refs[-layers:]

    def write():
        for source, target in ((mine, section), (theirs, 1 - section)):
            begin = 0
            for slab in source:
                rows = slab.shape[1] // layers
                for layer in range(layers):
                    outs[layer][target, begin : begin + rows] = slab[0, layer * rows : (layer + 1) * rows]
                begin = begin + rows

    if not olds:
        write()
    else:
        pl.when(info_ref[0, 0] == section)(write)

        @pl.when(info_ref[0, 0] != section)
        def _():
            for old, out in zip(olds, outs):
                out[...] = old[...]


def place_section(section, core, low, masks, spread, olds, layers):
    mine, theirs = spread.held, spread.theirs
    pieces, _, columns = mine[0].shape
    rows = sum(slab.shape[1] for slab in mine) // layers
    step = jnp.arange(pieces, dtype=jnp.int32)
    info = [jnp.full((pieces,), core, jnp.int32), step]
    for turn in rotations(masks):
        here = sum(((low & mask) != 0).astype(jnp.int32) << (len(masks) - 1 - index) for index, mask in enumerate(turn))
        info.append(step ^ here)
    info = jnp.stack(info)

    def source(part):
        return pl.BlockSpec((1, mine[part].shape[1], columns), lambda step, info_ref: (info_ref[2 + part, step], 0, 0))

    target = pl.BlockSpec((2, rows, columns), lambda step, info_ref: (0, 0, info_ref[1, step]))
    shape = jax.ShapeDtypeStruct((2, rows, pieces * columns), jnp.bfloat16)
    return pl.pallas_call(
        partial(place_kernel, section, layers),
        out_shape=[shape] * layers,
        grid_spec=pltpu.PrefetchScalarGridSpec(
            num_scalar_prefetch=1,
            grid=(pieces,),
            in_specs=[source(0), source(1), source(2)] * 2 + [target] * len(olds or ()),
            out_specs=[target] * layers,
        ),
        cost_estimate=pl.CostEstimate(
            flops=0, bytes_accessed=8 * rows * pieces * columns * layers, transcendentals=0
        ),
        name="place",
    )(info, *mine, *theirs, *(olds or ()))


def finish_kernel(
    info_ref, rate_ref, g0_ref, g1_ref, counts_ref, aq_ref, ao_ref, au_ref, ad_ref, bq_ref, bo_ref, bu_ref, bd_ref,
    wq_ref, wo_ref, wu_ref, wd_ref,
    gaq, gbq, gao, gbo, gau, gbu, gad, gbd, gain_out, bias_out, fq, fo, fu, fd, rms_out,
):
    rate = rate_ref[0]

    def run(g_ref):
        per = g_ref.shape[2] // WIDE

        def columns(index, begin=0, end=RANK):
            return g_ref[index // per, begin:end, (index % per) * WIDE : (index % per + 1) * WIDE].astype(jnp.float32)

        def project(first_at, second_at, a_ref, b_ref, w_ref, ga, gb, folded):
            for index in range(ga.shape[1] // WIDE):
                ga[0, index * WIDE : (index + 1) * WIDE] = columns(first_at + index).T
            span = w_ref.shape[1]
            rows = pl.ds(pl.multiple_of(info_ref[0] * span, span), span)
            new_first = a_ref[0, rows].astype(jnp.float32) - rate * ga[0, rows]
            for index in range(gb.shape[2] // WIDE):
                lanes = slice(index * WIDE, (index + 1) * WIDE)
                grad = columns(second_at + index)
                gb[0, :, lanes] = grad
                new_second = b_ref[0, :, lanes].astype(jnp.float32) - rate * grad
                product = jnp.dot(new_first, new_second, precision=lax.Precision.HIGHEST)
                folded[0, :, lanes] = (
                    w_ref[0, :, lanes].astype(jnp.float32) + adapter_scale * product
                ).astype(jnp.bfloat16)

        project(0, 2, aq_ref, bq_ref, wq_ref, gaq, gbq, fq)
        project(1, 5, ao_ref, bo_ref, wo_ref, gao, gbo, fo)
        project(6, 11, au_ref, bu_ref, wu_ref, gau, gbu, fu)
        project(7, 15, ad_ref, bd_ref, wd_ref, gad, gbd, fd)
        extra = [columns(index, RANK, RANK + 8)[:1] for index in (0, 6, 1, 7)]
        gain_out[0] = jnp.concatenate(extra[:2], 0)
        bias_out[0] = jnp.concatenate(extra[2:], 0)
        sums = columns(8, RANK, RANK + 8)[:1]
        sums = jnp.concatenate([sums[:, 128 * index : 128 * (index + 1)] for index in range(3)], 0)
        rms_out[0] = jnp.sqrt(sums / counts_ref[...])

    @pl.when(pl.program_id(0) == 0)
    def _():
        run(g0_ref)

    @pl.when(pl.program_id(0) != 0)
    def _():
        run(g1_ref)


def finish(place, rate, blocks, counts, trained, frozen):
    firsts, seconds = trained[0:8:2], trained[1:8:2]
    layers = firsts[0].shape[0]

    def layer_block(value):
        return pl.BlockSpec((1,) + value.shape[1:], lambda step, *_: (step, 0, 0))

    shapes = []
    for first, second in zip(firsts, seconds):
        shapes.append(jax.ShapeDtypeStruct(first.shape, jnp.float32))
        shapes.append(jax.ShapeDtypeStruct(second.shape, jnp.float32))
    shapes += [jax.ShapeDtypeStruct((layers, 2, WIDE), jnp.float32)] * 2
    shapes += [jax.ShapeDtypeStruct(matrix.shape, jnp.bfloat16) for matrix in frozen]
    shapes += [jax.ShapeDtypeStruct((layers, 3, 128), jnp.float32)]
    keep = pl.BlockSpec(blocks[0].shape, lambda step, *_: (0, 0, 0))
    return pl.pallas_call(
        finish_kernel,
        out_shape=shapes,
        grid_spec=pltpu.PrefetchScalarGridSpec(
            num_scalar_prefetch=1,
            grid=(layers,),
            in_specs=[pl.BlockSpec(memory_space=pltpu.SMEM), keep, keep, pl.BlockSpec((1, 128), lambda step, *_: (0, 0))]
            + [layer_block(value) for value in firsts + seconds + frozen],
            out_specs=[layer_block(shape) for shape in shapes],
        ),
        compiler_params=pltpu.CompilerParams(vmem_limit_bytes=60 << 20),
        cost_estimate=pl.CostEstimate(flops=1 << 30, bytes_accessed=48 << 20, transcendentals=0),
        name="finish",
    )(place.reshape(1), rate.reshape(1), *blocks, counts, *firsts, *seconds, *frozen)


def mm(left, right):
    return jnp.dot(left, right, preferred_element_type=jnp.float32)


def mm_nt(left, right):
    return lax.dot_general(left, right, (((1,), (1,)), ((), ())), preferred_element_type=jnp.float32)


def mm_tn(left, right):
    return lax.dot_general(left, right, (((0,), (0,)), ((), ())), preferred_element_type=jnp.float32)


def half(value):
    return value.astype(jnp.bfloat16)


def normalize(value):
    centred = value - jnp.mean(value, axis=-1, keepdims=True)
    scale = lax.rsqrt(jnp.mean(centred * centred, axis=-1, keepdims=True) + norm_eps)
    return centred * scale, scale


def norm_gradient(grad, normal, scale, gain):
    pulled = grad * gain
    inner = pulled - jnp.mean(pulled, axis=-1, keepdims=True)
    return scale * (inner - normal * jnp.mean(pulled * normal, axis=-1, keepdims=True))


def rotary_tables(seq_len):
    half_rot = ROT // 2
    lane = jnp.arange(2 * HEAD_DIM) % HEAD_DIM
    freqs = 10000.0 ** (-((lane % half_rot).astype(jnp.float32) * 2.0 / ROT))
    angles = jnp.arange(seq_len, dtype=jnp.float32)[:, None] * freqs[None, :]
    turning = (lane < ROT)[None, :]
    cosine = jnp.where(turning, jnp.cos(angles), 1.0)
    ahead = jnp.where((lane < half_rot)[None, :], -jnp.sin(angles), 0.0)
    behind = jnp.where(turning & (lane >= half_rot)[None, :], jnp.sin(angles), 0.0)
    return jnp.stack([cosine, ahead, behind])


def tile_table(table, rows, columns):
    return jnp.concatenate([jnp.concatenate([table] * (columns // table.shape[1]), 1)] * rows, 0)


def turn(value, cosine, ahead, behind):
    width = value.shape[1]
    step = ROT // 2
    return value * cosine + pltpu.roll(value, width - step, 1) * ahead + pltpu.roll(value, step, 1) * behind


def turn_back(value, cosine, ahead, behind):
    width = value.shape[1]
    step = ROT // 2
    return value * cosine + pltpu.roll(value * ahead, step, 1) + pltpu.roll(value * behind, width - step, 1)


def stack_heads(pair):
    low = lax.broadcasted_iota(jnp.int32, pair.shape, 1) < HEAD_DIM
    zero = jnp.zeros_like(pair)
    return jnp.concatenate([jnp.where(low, pair, zero), jnp.where(low, zero, pair)], 0)


def merge_heads(stacked):
    rows = stacked.shape[0] // 2
    low = lax.broadcasted_iota(jnp.int32, (rows, stacked.shape[1]), 1) < HEAD_DIM
    return jnp.where(low, stacked[:rows], stacked[rows:])


def pair_softmax(query_stack, key_pair, limit):
    scores = mm_nt(query_stack, key_pair) * HEAD_DIM ** (-0.5)
    seq_len = key_pair.shape[0]
    row = lax.broadcasted_iota(jnp.int32, scores.shape, 0) % seq_len
    column = lax.broadcasted_iota(jnp.int32, scores.shape, 1)
    scores = jnp.where((column <= row) & (column < limit), scores, masked_score)
    grown = jnp.exp(scores - jnp.max(scores, axis=-1, keepdims=True))
    return grown / jnp.sum(grown, axis=-1, keepdims=True)


GROUP = 4 * HEAD_DIM
BLOCK = 512


def attention_forward_kernel(
    facts_ref, x_ref, norm_ref, table_ref, first_ref, wq_ref, wk_ref, wv_ref, bq_ref, bk_ref, bv_ref,
    wo_ref, ao_ref, bo_ref,
    q_out, k_out, v_out, mixed_out, midq_out, mido_out, att_out,
    a_scr, mid_scr,
):
    step = pl.program_id(0)
    seqs = x_ref.shape[0] // table_ref.shape[1]
    seq_len = table_ref.shape[1]

    @pl.when(step == 0)
    def _():
        normal, _ = normalize(x_ref[...])
        a_scr[...] = half(normal * norm_ref[0:1] + norm_ref[2:3])
        midq_out[...] = half(mm(a_scr[...], first_ref[...]))
        att_out[...] = jnp.zeros_like(att_out)
        mid_scr[...] = jnp.zeros_like(mid_scr)

    normed = a_scr[...]
    mid = midq_out[...]
    tables = [tile_table(table_ref[index], seqs, GROUP) for index in range(3)]
    query = mm(normed, wq_ref[...]) + adapter_scale * mm(mid, bq_ref[...])
    q_out[...] = half(turn(query, *tables))
    key = mm(normed, wk_ref[...]) + adapter_scale * mm(mid, bk_ref[...])
    k_out[...] = half(turn(key, *tables))
    v_out[...] = half(mm(normed, wv_ref[...]) + adapter_scale * mm(mid, bv_ref[...]))
    for seq in range(seqs):
        rows = slice(seq * seq_len, (seq + 1) * seq_len)
        for pair in range(GROUP // (2 * HEAD_DIM)):
            lanes = slice(pair * 2 * HEAD_DIM, (pair + 1) * 2 * HEAD_DIM)
            probability = pair_softmax(stack_heads(q_out[rows, lanes]), k_out[rows, lanes], facts_ref[0, seq])
            mixed_out[rows, lanes] = half(merge_heads(mm(half(probability), v_out[rows, lanes])))
    mixed = mixed_out[...]
    att_out[...] += mm(mixed, wo_ref[...])
    mid_scr[...] += mm(mixed, ao_ref[...])

    @pl.when(step == pl.num_programs(0) - 1)
    def _():
        mido_out[...] = half(mid_scr[...])
        att_out[...] += adapter_scale * mm(mido_out[...], bo_ref[...])


def whole(*shape):
    return pl.BlockSpec(shape, lambda step, facts_ref: (0,) * len(shape))


def fixed(height, width, down=0, right=0):
    return pl.BlockSpec((height, width), lambda step, facts_ref: (down, right))


def column_block(height, width, offset=0):
    return pl.BlockSpec((height, width), lambda step, facts_ref: (0, step + offset))


def row_block(height, width, offset=0):
    return pl.BlockSpec((height, width), lambda step, facts_ref: (step + offset, 0))


def kernel_call(kernel, name, steps, in_specs, out_specs, out_shape, scratch, flops, size, exps=0, aliases={}):
    return pl.pallas_call(
        kernel,
        out_shape=out_shape,
        grid_spec=pltpu.PrefetchScalarGridSpec(
            num_scalar_prefetch=1, grid=(steps,), in_specs=in_specs, out_specs=out_specs, scratch_shapes=scratch
        ),
        compiler_params=pltpu.CompilerParams(
            dimension_semantics=("arbitrary",), vmem_limit_bytes=48 << 20
        ),
        input_output_aliases=aliases,
        cost_estimate=pl.CostEstimate(flops=flops, bytes_accessed=size, transcendentals=exps),
        name=name,
    )


def shaped(shape, dtype=jnp.bfloat16):
    return jax.ShapeDtypeStruct(shape, dtype)


def attention_forward(residual, weights, norms, tables, facts):
    tokens, width = residual.shape
    groups = width // GROUP
    joint, output = weights[0], weights[1]
    firsts, seconds = weights[4:6]
    seq_len = tables.shape[1]
    return kernel_call(
        attention_forward_kernel,
        "attention_forward",
        groups,
        [
            whole(tokens, width),
            whole(4, width),
            whole(3, seq_len, 2 * HEAD_DIM),
            whole(width, RANK),
            column_block(width, GROUP),
            column_block(width, GROUP, groups),
            column_block(width, GROUP, 2 * groups),
            column_block(RANK, GROUP),
            column_block(RANK, GROUP, groups),
            column_block(RANK, GROUP, 2 * groups),
            row_block(GROUP, width),
            row_block(GROUP, RANK, groups),
            fixed(RANK, width, 0, 3),
        ],
        [column_block(tokens, GROUP)] * 4 + [whole(tokens, RANK), whole(tokens, RANK), whole(tokens, width)],
        [shaped((tokens, width))] * 4
        + [shaped((tokens, RANK)), shaped((tokens, RANK)), shaped((tokens, width), jnp.float32)],
        [pltpu.VMEM((tokens, width), jnp.bfloat16), pltpu.VMEM((tokens, RANK), jnp.float32)],
        2 * tokens * width * width * 4,
        2 * 5 * width * width + 12 * tokens * width,
    )(
        facts, residual, norms, tables, firsts, joint, joint, joint, seconds, seconds, seconds, output,
        firsts, seconds,
    )


def feed_forward_kernel(
    facts_ref, x_ref, norm_ref, att_ref, first_ref, wu_ref, bu_ref, wd_ref, ad_ref, bd_ref,
    act_out, slope_out, midu_out, midd_out, x_out, sums_out,
    a_scr, mid_scr,
):
    step = pl.program_id(0)

    @pl.when(step == 0)
    def _():
        normal, _ = normalize(x_ref[...])
        a_scr[...] = half(normal * norm_ref[1:2] + norm_ref[3:4])
        midu_out[...] = half(mm(a_scr[...], first_ref[...]))
        x_out[...] = jnp.zeros_like(x_out)
        mid_scr[...] = jnp.zeros_like(mid_scr)

    upper = mm(a_scr[...], wu_ref[...]) + adapter_scale * mm(midu_out[...], bu_ref[...])
    spread = 0.5 + 0.5 * lax.erf(upper * 0.5**0.5)
    density = jnp.exp(-0.5 * upper * upper) * (0.5 / jnp.pi) ** 0.5
    act_out[...] = half(upper * spread)
    slope_out[...] = half(spread + upper * density)
    active = act_out[...]
    x_out[...] += mm(active, wd_ref[...])
    mid_scr[...] += mm(active, ad_ref[...])

    @pl.when(step == pl.num_programs(0) - 1)
    def _():
        midd_out[...] = half(mid_scr[...])
        feed = x_out[...] + adapter_scale * mm(midd_out[...], bd_ref[...])
        attended = att_ref[...]
        residual = x_ref[...]
        x_out[...] = residual + (attended + feed)
        lane = lax.broadcasted_iota(jnp.int32, (1, 128), 1)
        seqs = facts_ref.shape[1]
        seq_len = residual.shape[0] // seqs
        row = lax.broadcasted_iota(jnp.int32, (seq_len, 1), 0)
        parts = []
        for part in (residual, attended, feed):
            squares = jnp.sum(part * part, axis=-1, keepdims=True)
            sums = jnp.zeros((1, 128), jnp.float32)
            for seq in range(seqs):
                valid = jnp.where(row < facts_ref[0, seq], squares[seq * seq_len : (seq + 1) * seq_len], 0.0)
                counted = (lane == facts_ref[1, seq]) | (lane == DOMAINS)
                sums = sums + jnp.where(counted, jnp.sum(valid), 0.0)
            parts.append(sums)
        sums_out[...] = jnp.concatenate(parts + [jnp.zeros((5, 128), jnp.float32)], 0)


def feed_forward(residual, attended, weights, norms, facts):
    tokens, width = residual.shape
    upper, down = weights[2], weights[3]
    firsts, seconds = weights[4:6]
    hidden = upper.shape[1]
    return kernel_call(
        feed_forward_kernel,
        "feed_forward",
        hidden // BLOCK,
        [
            whole(tokens, width),
            whole(4, width),
            whole(tokens, width),
            fixed(width, RANK, 2, 0),
            column_block(width, BLOCK),
            column_block(RANK, BLOCK, 4 * width // BLOCK),
            row_block(BLOCK, width),
            row_block(BLOCK, RANK, 3 * width // BLOCK),
            fixed(RANK, width, 0, 8),
        ],
        [column_block(tokens, BLOCK)] * 2
        + [whole(tokens, RANK), whole(tokens, RANK), whole(tokens, width), whole(8, 128)],
        [shaped((tokens, hidden))] * 2
        + [shaped((tokens, RANK))] * 2
        + [shaped((tokens, width), jnp.float32), shaped((8, 128), jnp.float32)],
        [pltpu.VMEM((tokens, width), jnp.bfloat16), pltpu.VMEM((tokens, RANK), jnp.float32)],
        2 * tokens * width * hidden * 2,
        4 * width * hidden + 4 * tokens * hidden + 12 * tokens * width,
        2 * tokens * hidden,
    )(facts, residual, norms, attended, firsts, upper, seconds, down, firsts, seconds)


def write_extra(block_out, grad, normal, sums):
    width = grad.shape[1]
    row = [jnp.sum(grad * normal, axis=0, keepdims=True), jnp.sum(grad, axis=0, keepdims=True)] + sums
    rest = block_out.shape[1] - sum(part.shape[1] for part in row)
    row = jnp.concatenate(row + [jnp.zeros((1, rest), jnp.float32)], 1)
    block_out[RANK:, :] = half(jnp.concatenate([row, jnp.zeros((7, row.shape[1]), jnp.float32)], 0))


def feed_backward_kernel(
    facts_ref, g_ref, x_ref, norm_ref, act_ref, slope_ref, midu_ref, midd_ref, sums_ref, wu_ref, wd_ref, au_ref,
    bu_ref, ad_ref, bd_ref,
    whole_out, gx_out,
    block_out, g_scr, gmd_scr, gmdt_scr, midut_scr, gmu_scr, sem,
):
    step = pl.program_id(0)
    width = x_ref.shape[1]
    hidden = pl.num_programs(0) * BLOCK

    @pl.when(step == 0)
    def _():
        g_scr[...] = half(g_ref[...])
        grad_mid = adapter_scale * mm_nt(g_scr[...], bd_ref[...])
        gmd_scr[...] = half(grad_mid)
        gmdt_scr[...] = half(half(grad_mid).astype(jnp.float32).T)
        midut_scr[...] = half(midu_ref[...].astype(jnp.float32).T)
        gx_out[...] = jnp.zeros_like(gx_out)
        gmu_scr[...] = jnp.zeros_like(gmu_scr)
        middt = half(midd_ref[...].astype(jnp.float32).T)
        block_out[:RANK, pl.ds(width + 2 * hidden, width)] = half(adapter_scale * mm(middt, g_scr[...]))

    grad_act = mm_nt(g_scr[...], wd_ref[...]) + mm_nt(gmd_scr[...], ad_ref[...])
    grad_up = half(half(grad_act).astype(jnp.float32) * slope_ref[...].astype(jnp.float32))
    first_at = pl.multiple_of(width + step * BLOCK, BLOCK)
    second_at = pl.multiple_of(width + hidden + step * BLOCK, BLOCK)
    block_out[:RANK, pl.ds(first_at, BLOCK)] = half(mm(gmdt_scr[...], act_ref[...]))
    block_out[:RANK, pl.ds(second_at, BLOCK)] = half(adapter_scale * mm(midut_scr[...], grad_up))
    gmu_scr[...] += mm_nt(grad_up, bu_ref[...])
    gx_out[...] += mm_nt(grad_up, wu_ref[...])

    @pl.when(step == pl.num_programs(0) - 1)
    def _():
        grad_mid = half(adapter_scale * gmu_scr[...])
        normal, scale = normalize(x_ref[...])
        normed = half(normal * norm_ref[1:2] + norm_ref[3:4])
        block_out[:RANK, :width] = half(mm(half(grad_mid.astype(jnp.float32).T), normed))
        grad = gx_out[...] + mm_nt(grad_mid, au_ref[...])
        write_extra(block_out, grad, normal, [sums_ref[index : index + 1] for index in range(3)])
        gather = pltpu.make_async_copy(
            block_out, whole_out.at[:, pl.ds(6 * width, block_out.shape[1])], sem
        )
        gather.start()
        gx_out[...] = g_ref[...] + norm_gradient(grad, normal, scale, norm_ref[1:2])
        gather.wait()


def feed_backward(gradient, residual, weights, norms, kept, facts):
    tokens, width = residual.shape
    upper, down = weights[2], weights[3]
    firsts, seconds = weights[4:6]
    active, slope, mid_u, mid_d, sums = kept
    hidden = upper.shape[1]
    return kernel_call(
        feed_backward_kernel,
        "feed_backward",
        hidden // BLOCK,
        [
            whole(tokens, width),
            whole(tokens, width),
            whole(4, width),
            column_block(tokens, BLOCK),
            column_block(tokens, BLOCK),
            whole(tokens, RANK),
            whole(tokens, RANK),
            whole(8, 128),
            column_block(width, BLOCK),
            row_block(BLOCK, width),
            fixed(width, RANK, 2, 0),
            column_block(RANK, BLOCK, 4 * width // BLOCK),
            row_block(BLOCK, RANK, 3 * width // BLOCK),
            fixed(RANK, width, 0, 8),
        ],
        [pl.BlockSpec(memory_space=pl.ANY), whole(tokens, width)],
        [shaped((RANK + 8, 16 * width)), shaped((tokens, width), jnp.float32)],
        [
            pltpu.VMEM((RANK + 8, 2 * width + 2 * hidden), jnp.bfloat16),
            pltpu.VMEM((tokens, width), jnp.bfloat16),
            pltpu.VMEM((tokens, RANK), jnp.bfloat16),
            pltpu.VMEM((RANK, tokens), jnp.bfloat16),
            pltpu.VMEM((RANK, tokens), jnp.bfloat16),
            pltpu.VMEM((tokens, RANK), jnp.float32),
            pltpu.SemaphoreType.DMA,
        ],
        2 * tokens * width * hidden * 2,
        4 * width * hidden + 4 * tokens * hidden + 16 * tokens * width,
    )(
        facts, gradient, residual, norms, active, slope, mid_u, mid_d, sums, upper, down, firsts, seconds,
        firsts, seconds,
    )


def attention_backward_kernel(
    facts_ref, g_ref, gx_ref, x_ref, norm_ref, table_ref, q_ref, k_ref, v_ref, mixed_ref, midq_ref, mido_ref,
    wq_ref, wk_ref, wv_ref, aq_ref, bq_ref, bk_ref, bv_ref, wo_ref, ao_ref, bo_ref, feed_block_ref,
    whole_out, gx_out,
    block_out, g_scr, gmo_scr, gmot_scr, midqt_scr, gmq_scr, acc_scr, gq_scr, gk_scr, gv_scr, sem,
):
    step = pl.program_id(0)
    width = x_ref.shape[1]
    seq_len = table_ref.shape[1]
    seqs = x_ref.shape[0] // seq_len
    scale_factor = HEAD_DIM ** (-0.5)

    @pl.when(step == 0)
    def _():
        g_scr[...] = half(g_ref[...])
        grad_mid = half(adapter_scale * mm_nt(g_scr[...], bo_ref[...]))
        gmo_scr[...] = grad_mid
        gmot_scr[...] = half(grad_mid.astype(jnp.float32).T)
        midqt_scr[...] = half(midq_ref[...].astype(jnp.float32).T)
        acc_scr[...] = jnp.zeros_like(acc_scr)
        gmq_scr[...] = jnp.zeros_like(gmq_scr)
        midot = half(mido_ref[...].astype(jnp.float32).T)
        block_out[:RANK, pl.ds(5 * width, width)] = half(adapter_scale * mm(midot, g_scr[...]))

    grad_mixed = half(mm_nt(g_scr[...], wo_ref[...]) + mm_nt(gmo_scr[...], ao_ref[...]))
    first_at = pl.multiple_of(width + step * GROUP, GROUP)
    block_out[:RANK, pl.ds(first_at, GROUP)] = half(mm(gmot_scr[...], mixed_ref[...]))
    for seq in range(seqs):
        rows = slice(seq * seq_len, (seq + 1) * seq_len)
        for pair in range(GROUP // (2 * HEAD_DIM)):
            lanes = slice(pair * 2 * HEAD_DIM, (pair + 1) * 2 * HEAD_DIM)
            query_stack = stack_heads(q_ref[rows, lanes])
            key_pair = k_ref[rows, lanes]
            probability = pair_softmax(query_stack, key_pair, facts_ref[0, seq])
            grad_stack = stack_heads(grad_mixed[rows, lanes])
            grad_prob = mm_nt(grad_stack, v_ref[rows, lanes])
            gv_scr[rows, lanes] = half(mm_tn(half(probability), grad_stack))
            inner = jnp.sum(probability * grad_prob, axis=-1, keepdims=True)
            grad_scores = half(probability * (grad_prob - inner))
            gq_scr[rows, lanes] = merge_heads(mm(grad_scores, key_pair)) * scale_factor
            gk_scr[rows, lanes] = mm_tn(grad_scores, query_stack) * scale_factor
    tables = [tile_table(table_ref[index], seqs, GROUP) for index in range(3)]
    joint = (half(turn_back(gq_scr[...], *tables)), half(turn_back(gk_scr[...], *tables)), gv_scr[...])
    mid = midqt_scr[...]
    for index, (grad, w_ref, b_ref) in enumerate(zip(joint, (wq_ref, wk_ref, wv_ref), (bq_ref, bk_ref, bv_ref))):
        second_at = pl.multiple_of((2 + index) * width + step * GROUP, GROUP)
        block_out[:RANK, pl.ds(second_at, GROUP)] = half(adapter_scale * mm(mid, grad))
        gmq_scr[...] += mm_nt(grad, b_ref[...])
        acc_scr[...] += mm_nt(grad, w_ref[...])

    @pl.when(step == pl.num_programs(0) - 1)
    def _():
        grad_mid = half(adapter_scale * gmq_scr[...])
        normal, scale = normalize(x_ref[...])
        normed = half(normal * norm_ref[0:1] + norm_ref[2:3])
        block_out[:RANK, :width] = half(mm(half(grad_mid.astype(jnp.float32).T), normed))
        grad = acc_scr[...] + mm_nt(grad_mid, aq_ref[...])
        write_extra(block_out, grad, normal, [])
        gather = pltpu.make_async_copy(block_out, whole_out.at[:, pl.ds(0, block_out.shape[1])], sem)
        gather.start()
        gx_out[...] = gx_ref[...] + norm_gradient(grad, normal, scale, norm_ref[0:1])
        gather.wait()


def attention_backward(gradient, grad_feed, feed_block, residual, weights, norms, tables, kept, facts):
    tokens, width = residual.shape
    groups = width // GROUP
    joint, output = weights[0], weights[1]
    firsts, seconds = weights[4:6]
    queries, keys, values, mixed, mid_q, mid_o = kept
    seq_len = tables.shape[1]
    block = column_block(tokens, GROUP)
    return kernel_call(
        attention_backward_kernel,
        "attention_backward",
        groups,
        [
            whole(tokens, width),
            whole(tokens, width),
            whole(tokens, width),
            whole(4, width),
            whole(3, seq_len, 2 * HEAD_DIM),
            block,
            block,
            block,
            block,
            whole(tokens, RANK),
            whole(tokens, RANK),
            column_block(width, GROUP),
            column_block(width, GROUP, groups),
            column_block(width, GROUP, 2 * groups),
            whole(width, RANK),
            column_block(RANK, GROUP),
            column_block(RANK, GROUP, groups),
            column_block(RANK, GROUP, 2 * groups),
            row_block(GROUP, width),
            row_block(GROUP, RANK, groups),
            fixed(RANK, width, 0, 3),
            pl.BlockSpec(memory_space=pl.ANY),
        ],
        [pl.BlockSpec(memory_space=pl.ANY), whole(tokens, width)],
        [shaped((RANK + 8, 16 * width)), shaped((tokens, width), jnp.float32)],
        [
            pltpu.VMEM((RANK + 8, 6 * width), jnp.bfloat16),
            pltpu.VMEM((tokens, width), jnp.bfloat16),
            pltpu.VMEM((tokens, RANK), jnp.bfloat16),
            pltpu.VMEM((RANK, tokens), jnp.bfloat16),
            pltpu.VMEM((RANK, tokens), jnp.bfloat16),
            pltpu.VMEM((tokens, RANK), jnp.float32),
            pltpu.VMEM((tokens, width), jnp.float32),
            pltpu.VMEM((tokens, GROUP), jnp.float32),
            pltpu.VMEM((tokens, GROUP), jnp.float32),
            pltpu.VMEM((tokens, GROUP), jnp.bfloat16),
            pltpu.SemaphoreType.DMA,
        ],
        2 * tokens * width * width * 4,
        2 * 5 * width * width + 24 * tokens * width,
        aliases={22: 0},
    )(
        facts, gradient, grad_feed, residual, norms, tables, queries, keys, values, mixed, mid_q, mid_o, joint,
        joint, joint, firsts, seconds, seconds, seconds, output, firsts, seconds, feed_block,
    )


def layer_forward(residual, weights, tables, facts):
    norms = weights[6]
    *kept_attention, attended = attention_forward(residual, weights, norms, tables, facts)
    *kept_feed, output, sums = feed_forward(residual, attended, weights, norms, facts)
    return output, (residual, kept_attention, kept_feed + [sums])


def layer_backward(gradient, kept, weights, tables, facts):
    residual, kept_attention, kept_feed = kept
    norms = weights[6]
    feed_block, grad_feed = feed_backward(gradient, residual, weights, norms, kept_feed, facts)
    block, grad_input = attention_backward(
        gradient, grad_feed, feed_block, residual, weights, norms, tables, kept_attention, facts
    )
    return grad_input, block


def gather_plan(gathers, turns):
    if (gathers, turns) == (4, 3):
        return [[0, 2], [0], [0, 1], [1, 2], [1, 3], [2, 3], [3], []]
    return [
        [index for index in range(gathers) if index <= step < index + turns] for step in range(gathers + turns)
    ]


def shards(
    inputs,
    cotangent,
    domain,
    lengths,
    steps_since_reset,
    frozen_query_weight,
    frozen_output_weight,
    frozen_up_weight,
    frozen_down_weight,
    query_adapter_first,
    query_adapter_second,
    output_adapter_first,
    output_adapter_second,
    up_adapter_first,
    up_adapter_second,
    down_adapter_first,
    down_adapter_second,
    layer_norm_gain,
    layer_norm_bias,
):
    core = lax.axis_index("section")
    place = lax.axis_index("dp")
    count = lax.axis_size("dp")
    middle = count // 2
    stage = place // middle
    low = place % middle
    home = core == stage
    masks = [1 << bit for bit in range(middle.bit_length() - 1)]
    frozen = (frozen_query_weight, frozen_output_weight, frozen_up_weight, frozen_down_weight)
    trained = (
        query_adapter_first,
        query_adapter_second,
        output_adapter_first,
        output_adapter_second,
        up_adapter_first,
        up_adapter_second,
        down_adapter_first,
        down_adapter_second,
    )
    local_layers = frozen_query_weight.shape[0]
    rows_dev, seq_len, model_width = inputs.shape
    tokens = rows_dev * seq_len
    rows = frozen_output_weight.shape[1]

    places = [(index // middle, index) for index in range(count)]
    to_sibling = [(here * count + index, (1 - here) * count + index) for here, index in places]
    to_far = [((1 - here) * count + index, (1 - here) * count + (index ^ middle)) for here, index in places]
    to_cross = [((1 - here) * count + index, here * count + (index ^ middle)) for here, index in places]
    halves = [pick_halves([matrix[layer] for matrix in frozen], stage) for layer in range(local_layers)]
    packed = [
        (
            jnp.concatenate([factor[layer] for factor in trained[0::2]], 0),
            jnp.concatenate([factor[layer] for factor in trained[1::2]], 1),
            jnp.concatenate([layer_norm_gain[layer], layer_norm_bias[layer]], 0),
        )
        for layer in range(local_layers)
    ]
    sibling, far, cross = [
        partial(both_axes, pairs=pairs) for pairs in (to_sibling, to_far, to_cross)
    ]
    steps = Steps()
    near = steps.run(*[(other, sibling) for _, other in halves])
    apart = []
    for same, other in halves:
        same, other = tie((same, other), *(near + apart[-1:]))
        apart.append((far(other), cross(same)))
    gathers = []
    for layer in range(local_layers):
        gathers.append(Gather(jnp.where(home, halves[layer][0], near[layer]), masks))
        gathers.append(Gather(jnp.where(home, *apart[layer]), masks))
    plan = gather_plan(len(gathers), len(masks))
    visiting = jnp.where(stage == 0, cotangent, inputs)
    facts = jnp.stack([lengths, domain])
    weights = [None] * local_layers
    swapped = [None] * len(gathers)
    ready = []
    for number, active in enumerate(plan):
        moves = [move for index in active for move in gathers[index].moves()]
        moves = moves + [(held, flip_core) for index in ready for held in gathers[index].held]
        if number == 0:
            moves.append((facts, cross))
        if number == 1:
            moves = moves + [(part, sibling) for part in packed[0]]
        if number == 3:
            moves.append((visiting, cross))
            moves = moves + [(part, sibling) for layer in packed[1:] for part in layer]
        there = steps.run(*moves)
        for index in active:
            gathers[index].take(there[:3])
            there = there[3:]
        for index in ready:
            swapped[index] = there[:3]
            there = there[3:]
        ready = [index for index in active if gathers[index].step == len(masks)]
        if number == 0:
            facts = jnp.where(home, facts, there[0])
        if number == 1:
            packed[0] = [jnp.where(home, here, far_part) for here, far_part in zip(packed[0], there)]
        if number == 3:
            visiting, there = there[0], there[1:]
            for layer in range(1, local_layers):
                packed[layer] = [jnp.where(home, here, far_part) for here, far_part in zip(packed[layer], there)]
                there = there[3:]
    for layer in range(local_layers):
        dense = None
        for which in range(2):
            gather = gathers[2 * layer + which]
            base = jnp.where(stage == which, 0, middle)
            order = gather.found[0]
            info = jnp.stack(
                [jnp.full((middle,), core, jnp.int32), (jnp.asarray(order, jnp.int32) ^ low) + base]
                + [jnp.asarray([known.index(mask) for mask in order], jnp.int32) for known in gather.found]
            )
            dense = assemble(info, gather.held, swapped[2 * layer + which], rows, count, dense)
        weights[layer] = tuple(dense) + tuple(packed[layer])
    start = jnp.where(home, inputs, visiting).astype(jnp.float32).reshape(tokens, model_width)
    valid = jnp.arange(seq_len)[None, :] < facts[0][:, None]
    end_grad = jnp.where(home, cotangent, visiting).astype(jnp.float32)
    end_grad = jnp.where(stage == 1, end_grad * valid[..., None].astype(jnp.float32), 0.0)
    end_grad = end_grad.reshape(tokens, model_width)
    tables = rotary_tables(seq_len)

    def stage_forward(residual):
        kept = []
        for layer in range(local_layers):
            residual, kept_state = layer_forward(residual, weights[layer], tables, facts)
            kept.append(kept_state)
        return residual, kept

    boundary, _ = stage_forward(start)
    boundary = boundary.astype(jnp.bfloat16)
    forward_pairs = [(index, index + middle) for index in range(middle)]
    received = lax.ppermute(boundary, "dp", forward_pairs)
    entry = jnp.where(stage == 0, start, received.astype(jnp.float32))
    final, kept = stage_forward(entry)
    final = final.astype(jnp.bfloat16)

    gradient = end_grad
    late = [None] * local_layers
    for layer in reversed(range(local_layers)):
        gradient, late[layer] = layer_backward(gradient, kept[layer], weights[layer], tables, facts)
    sent = gradient.astype(jnp.bfloat16)
    came_back = lax.ppermute(sent, "dp", [(after, before) for before, after in forward_pairs])
    steps = Steps()
    late_slabs = scatter_section(late, 1, core, low, count, masks, steps)

    gradient = jnp.where(stage == 0, came_back.astype(jnp.float32), 0.0)
    blocks, slabs = [None] * local_layers, [None] * local_layers
    for layer in reversed(range(local_layers)):
        gradient, blocks[layer] = layer_backward(gradient, kept[layer], weights[layer], tables, facts)
        if layer:
            slabs[layer] = scatter_section([blocks[layer]], 0, core, low, count, masks, steps)

    first = Spread(late_slabs, 1, masks, count, stage)
    second = Spread(sum(slabs[1:], []), 0, masks, count, stage)
    third = Scatter([blocks[0]], 0, core, low, count, masks)
    there = steps.run(*third.moves(), *first.moves(), *second.moves())
    there = third.take(there)
    second.take(first.take(there))
    for step in range(len(masks)):
        there = steps.run(*third.moves())
        third.take(there)
    third = Spread(third.slabs, 0, masks, count, stage)
    for step in range(len(masks) + 2):
        groups = [first, second, third] if step else [third, first, second]
        groups = [group for group in groups if not group.done()]
        there = steps.run(*[move for group in groups for move in group.moves()])
        for group in groups:
            there = group.take(there)
    placed = place_section(1, core, low, masks, first, None, local_layers)
    old = placed[1:]
    upper_placed = place_section(0, core, low, masks, second, old, local_layers - 1)
    lower_placed = place_section(0, core, low, masks, third, placed[:1], 1)
    blocks = lower_placed + upper_placed

    out_pairs = [(count + index + middle, index + middle) for index in range(middle)]
    out_pairs = out_pairs + [(index + middle, count + index) for index in range(middle)]
    visiting = both_axes(jnp.where(core == 0, final, received), out_pairs)
    section_out = jnp.where(home, jnp.where(stage == 0, boundary, final), visiting)
    section_out = section_out.reshape(1, rows_dev, seq_len, model_width)
    grad_pairs = [(index, count + index) for index in range(middle)]
    grad_pairs = grad_pairs + [(count + index, index + middle) for index in range(middle)]
    visiting = both_axes(jnp.where(core == 0, came_back, gradient.astype(jnp.bfloat16)), grad_pairs)
    section_grad = jnp.where(
        home, jnp.where(stage == 0, gradient, sent.astype(jnp.float32)), visiting.astype(jnp.float32)
    )
    section_grad = section_grad.reshape(1, rows_dev, seq_len, model_width)

    lane = jnp.arange(128)
    counted = (domain[:, None] == lane[None, :]) | (lane == DOMAINS)[None, :]
    counts = jnp.sum(jnp.where(counted, lengths.astype(jnp.float32)[:, None], 0.0), axis=0, keepdims=True)
    counts = tie(counts, final)
    for mask in masks + [middle]:
        counts = counts + flip_place(counts, mask)
    counts = jnp.maximum(counts, 1.0) * model_width
    rate = peak_rate * (steps_since_reset[0].astype(jnp.float32) + 1.0) / WARM
    *outputs, rms = finish(place, rate, blocks, counts, trained, frozen)
    return (section_out, section_grad, *outputs, rms[:, :, : DOMAINS + 1])


def solution(mesh):
    across = P("dp", None, None)
    copied = P("section", None, None)
    split = P("section", "dp", None)
    wide = P("section", "dp", None, None)
    return jax.shard_map(
        shards,
        mesh=mesh,
        in_specs=(across, across, P("dp"), P("dp"), P()) + (split,) * 4 + (copied,) * 10,
        out_specs=(wide, wide) + (copied,) * 10 + (split,) * 4 + (copied,),
        check_vma=False,
    )
```

```python
from functools import partial

import jax
import jax.numpy as jnp
from jax import lax
from jax.experimental import pallas as pl
from jax.experimental.pallas import tpu as pltpu
from jax.sharding import PartitionSpec as P

HEADS = 16
HEAD_DIM = 64
ROT = 16
DOMAINS = 16
WARM = 50
RANK = 128
WIDE = 1024
UNITS = 12
HALF_UNITS = 6

adapter_scale = 0.5
norm_eps = 1e-05
peak_rate = 0.0002
masked_score = -1e30


def both_axes(value, pairs):
    return lax.ppermute(value, ("section", "dp"), pairs)


def tie(value, *others):
    return lax.optimization_barrier((value, others))[0]


def flip_place(value, mask):
    count = lax.axis_size("dp")
    return lax.ppermute(value, "dp", [(place, place ^ mask) for place in range(count)])


def flip_core(value):
    return lax.ppermute(value, "section", [(0, 1), (1, 0)])


def pack_kernel(info_ref, query_ref, output_ref, upper_ref, down_ref, keep_ref, send_ref):
    rows = output_ref.shape[1]

    def write(first, second):
        for layer in range(output_ref.shape[0]):
            first[layer, 0] = query_ref[layer, :, :WIDE]
            first[layer, 1] = query_ref[layer, :, WIDE : 2 * WIDE]
            first[layer, 2] = query_ref[layer, :, 2 * WIDE :]
            first[layer, 3] = output_ref[layer]
            first[layer, 4] = upper_ref[layer, :, :WIDE]
            first[layer, 5] = upper_ref[layer, :, WIDE : 2 * WIDE]
            second[layer, 0] = upper_ref[layer, :, 2 * WIDE : 3 * WIDE]
            second[layer, 1] = upper_ref[layer, :, 3 * WIDE :]
            for index in range(4):
                second[layer, 2 + index] = down_ref[layer, index * rows : (index + 1) * rows]

    @pl.when(info_ref[0] == 0)
    def _():
        write(keep_ref, send_ref)

    @pl.when(info_ref[0] != 0)
    def _():
        write(send_ref, keep_ref)


def pack_halves(core, frozen):
    layers, rows = frozen[1].shape[:2]
    shape = jax.ShapeDtypeStruct((layers, HALF_UNITS, rows, WIDE), jnp.bfloat16)
    vmem = pl.BlockSpec(memory_space=pltpu.VMEM)
    return pl.pallas_call(
        pack_kernel,
        out_shape=[shape, shape],
        in_specs=[pl.BlockSpec(memory_space=pltpu.SMEM)] + [vmem] * 4,
        out_specs=[vmem, vmem],
        compiler_params=pltpu.CompilerParams(vmem_limit_bytes=32 << 20),
        cost_estimate=pl.CostEstimate(
            flops=0, bytes_accessed=8 * HALF_UNITS * layers * rows * WIDE, transcendentals=0
        ),
        name="pack",
    )(core.reshape(1), *frozen)


def rotations(masks):
    return [[masks[(start + index) % len(masks)] for index in range(len(masks))] for start in range(3)]


def assemble_kernel(layout, info_ref, mine, theirs, *refs):
    count = len({layer for layer, _ in layout})
    outs, token_out, sem = refs[-4 * count - 2 : -2], refs[-2], refs[-1]
    token_out[...] = jnp.zeros_like(token_out)
    first_layer = min(layer for layer, _ in layout)
    rows = mine.shape[2]

    def targets(half_index, layer, part, place):
        query_out, output_out, upper_out, down_out = outs[4 * (layer - first_layer) : 4 * (layer - first_layer) + 4]
        at = pl.multiple_of(place * rows, rows)
        down_at = pl.multiple_of(place * 4 * rows, rows)

        def columns(out, index):
            return out.at[pl.ds(at, rows), pl.ds(index * WIDE, WIDE)]

        def down(index):
            return down_out.at[pl.ds(down_at + index * rows, rows)]

        return [
            [(columns(query_out, 0), columns(query_out, 1)), (columns(query_out, 2), columns(output_out, 0)),
             (columns(upper_out, 0), columns(upper_out, 1))],
            [(columns(upper_out, 2), columns(upper_out, 3)), (down(0), down(1)), (down(2), down(3))],
        ][half_index][part]

    def run(first, second):
        copies = []
        for block, (layer, part) in enumerate(layout):
            for half_index, source in enumerate((first, second)):
                for unit, target in enumerate(targets(half_index, layer, part, info_ref[1 + block])):
                    where = sem.at[block, half_index * 2 + unit]
                    copies.append(pltpu.make_async_copy(source.at[block, unit], target, where))
                    copies[-1].start()
        for copy in copies:
            copy.wait()

    @pl.when(info_ref[0] == 0)
    def _():
        run(mine, theirs)

    @pl.when(info_ref[0] != 0)
    def _():
        run(theirs, mine)


def assemble(info, layout, mine, theirs, count, into):
    rows = mine.shape[2]
    total = rows * count
    layers = sorted({layer for layer, _ in layout})
    shapes = [(total, 3 * WIDE), (total, WIDE), (total, 4 * WIDE), (4 * total, WIDE)] * len(layers)
    extra = [matrix for layer in layers for matrix in (into[layer] or ())]
    anywhere = pl.BlockSpec(memory_space=pltpu.HBM)
    aliases, index = {}, 3
    for position, layer in enumerate(layers):
        if into[layer]:
            for matrix in range(4):
                aliases[index] = 4 * position + matrix
                index = index + 1
    made = pl.pallas_call(
        partial(assemble_kernel, tuple(layout)),
        out_shape=[jax.ShapeDtypeStruct(shape, jnp.bfloat16) for shape in shapes]
        + [jax.ShapeDtypeStruct((8, 128), jnp.float32)],
        in_specs=[pl.BlockSpec(memory_space=pltpu.SMEM)]
        + [pl.BlockSpec(memory_space=pltpu.VMEM)] * 2
        + [anywhere] * len(extra),
        out_specs=[anywhere] * len(shapes) + [pl.BlockSpec(memory_space=pltpu.VMEM)],
        scratch_shapes=[pltpu.SemaphoreType.DMA((len(layout), 4))],
        input_output_aliases=aliases,
        compiler_params=pltpu.CompilerParams(vmem_limit_bytes=60 << 20),
        cost_estimate=pl.CostEstimate(flops=0, bytes_accessed=12 * mine.size, transcendentals=0),
        name="assemble",
    )(info, mine, theirs, *extra)
    for position, layer in enumerate(layers):
        into[layer] = made[4 * position : 4 * position + 4]
    return made[-1]


def copy_kernel(plans, *refs):
    inputs, outs = refs[: -len(plans)], refs[-len(plans) :]
    for plan, out in zip(plans, outs):
        at = 0
        for source, begin, size in plan:
            out[at : at + size] = inputs[source][begin : begin + size]
            at = at + size


def copy_blocks(arrays, plans, after):
    tail = arrays[0].shape[1:]
    vmem = pl.BlockSpec(memory_space=pltpu.VMEM)
    shapes = [jax.ShapeDtypeStruct((sum(size for _, _, size in plan),) + tail, jnp.bfloat16) for plan in plans]
    moved = 4 * sum(shape.size for shape in shapes)
    return pl.pallas_call(
        partial(copy_kernel, tuple(tuple(plan) for plan in plans)),
        out_shape=shapes,
        in_specs=[vmem] * len(arrays) + [pl.BlockSpec(memory_space=pl.ANY)] * len(after),
        out_specs=[vmem] * len(shapes),
        compiler_params=pltpu.CompilerParams(vmem_limit_bytes=40 << 20),
        cost_estimate=pl.CostEstimate(flops=0, bytes_accessed=moved, transcendentals=0),
        name="collect",
    )(*arrays, *after)


class Gather:
    def __init__(self, layer, which, block, masks):
        self.layer, self.which = layer, which
        block = block.reshape((3, 2) + block.shape[1:])
        self.block = block
        self.held = [[(block, part, 1)] for part in range(3)]
        self.found = [[0], [0], [0]]
        self.turns = rotations(masks)
        self.step = 0


class Store:
    def __init__(self):
        self.arrays = []

    def index(self, array):
        for position, known in enumerate(self.arrays):
            if known is array:
                return position
        self.arrays.append(array)
        return len(self.arrays) - 1


def gather_step(active, masks, fresh, extra, after):
    store = Store()
    plans, lists = [], []
    for mask in masks:
        entries = [
            (gather, part) for gather in active for part in range(3) if gather.turns[part][gather.step] == mask
        ]
        if entries:
            plans.append(
                [
                    (store.index(array), begin, size)
                    for gather, part in entries
                    for array, begin, size in gather.held[part]
                ]
            )
            lists.append((mask, entries))
    if fresh:
        plans.append([(store.index(array), begin, size) for array, begin, size, _, _, _ in fresh])
    after = [value for value in after if all(value is not known for known in store.arrays)]
    values = list(copy_blocks(store.arrays, plans, after)) + [value for value, _ in extra]
    there = []
    for value, (mask, _) in zip(values, lists):
        there.append(flip_place(value, mask))
    collected = values[len(lists)] if fresh else None
    swapped = flip_core(collected) if fresh else None
    results = [send(value) for value, (_, send) in zip(values[len(plans) :], extra)]
    came = []
    for (mask, entries), value in zip(lists, there):
        begin = 0
        for gather, part in entries:
            size = sum(amount for _, _, amount in gather.held[part])
            known = [place ^ gather.turns[part][gather.step] for place in gather.found[part]]
            gather.held[part] = gather.held[part] + [(value, begin, size)]
            gather.found[part] = gather.found[part] + known
            came.append((value, begin, size, gather, part, known))
            begin = begin + size
    for gather in active:
        gather.step = gather.step + 1
    return there, came, collected, swapped, results


def pieces_by_place(block, pieces):
    if pieces == block.shape[0]:
        return block
    split = pieces // block.shape[0]
    columns = block.shape[2] // split
    block = block.reshape(block.shape[0], block.shape[1], split, columns).transpose(0, 2, 1, 3)
    return block.reshape(pieces, block.shape[2], columns)


def places_to_blocks(pieces, blocks):
    if pieces.shape[0] == blocks:
        return pieces
    split = pieces.shape[0] // blocks
    rows, columns = pieces.shape[1:]
    return pieces.reshape(blocks, split, rows, columns).transpose(0, 2, 1, 3).reshape(blocks, rows, split * columns)


def exchange(value, count):
    middle = count // 2
    groups = [[half_index * middle + index for index in range(middle)] for half_index in range(2)]
    return lax.all_to_all(value, "dp", 0, 0, axis_index_groups=groups)


def swap_halves(block, section, core, count):
    middle = count // 2
    inside = [place for place in range(count) if place // middle == section]
    swap = [(here * count + place, (1 - here) * count + place) for here in range(2) for place in inside]
    size = block.shape[0] // 2
    there = both_axes(lax.dynamic_slice_in_dim(block, (1 - core) * size, size, 0), swap)
    here = lax.dynamic_slice_in_dim(block, core * size, size, 0)
    return (here.astype(jnp.float32) + there.astype(jnp.float32)).astype(jnp.bfloat16)


def sum_halves(halves, count):
    pieces = [pieces_by_place(part, count // 2) for part in halves]
    pieces = pieces[0] if len(pieces) == 1 else jnp.concatenate(pieces, 1)
    return jnp.sum(exchange(pieces, count).astype(jnp.float32), axis=0).astype(jnp.bfloat16)


def scatter_section(blocks, section, core, count):
    return sum_halves([swap_halves(block, section, core, count) for block in blocks], count)


def cross_section(piece, section, stage, count):
    middle = count // 2
    across = [(place, place ^ middle) for place in range(count) if place // middle == section]
    return jnp.where(stage == section, piece, lax.ppermute(piece, "dp", across))


def spread_section(piece, section, count):
    middle = count // 2
    spread = exchange(jnp.broadcast_to(piece[None], (middle,) + piece.shape), count)
    here = places_to_blocks(spread, 8)
    there = lax.ppermute(here, "section", [(1 - section, section)])
    return (here, there) if section == 0 else (there, here)


def finish_kernel(
    offsets, info_ref, rate_ref, early0_ref, early1_ref, late0_ref, late1_ref, counts_ref,
    aq_ref, ao_ref, au_ref, ad_ref, bq_ref, bo_ref, bu_ref, bd_ref, wq_ref, wo_ref, wu_ref, wd_ref, *refs,
):
    gaq, gbq, gao, gbo, gau, gbu, gad, gbd, gain_out, bias_out, fq, fo, fu, fd, rms_out, g_ref, sem = refs[-17:]
    rate = rate_ref[0]
    size, height = early0_ref.shape[0], g_ref.shape[1]

    def fetch(sources, begin):
        copies = [
            pltpu.make_async_copy(
                source.at[:, pl.ds(begin, height)], g_ref.at[pl.ds(index * size, size)], sem.at[index]
            )
            for index, source in enumerate(sources)
        ]
        for copy in copies:
            copy.start()
        for copy in copies:
            copy.wait()

    @pl.when(info_ref[1] == 0)
    def _():
        fetch((early0_ref, early1_ref), offsets[0])

    @pl.when(info_ref[1] != 0)
    def _():
        fetch((late0_ref, late1_ref), offsets[1])

    def run():
        def columns(index, begin=0, end=RANK):
            return g_ref[index, begin:end].astype(jnp.float32)

        def project(first_at, second_at, a_ref, b_ref, w_ref, ga, gb, folded):
            for index in range(ga.shape[1] // WIDE):
                ga[0, index * WIDE : (index + 1) * WIDE] = columns(first_at + index).T
            span = w_ref.shape[1]
            rows = pl.ds(pl.multiple_of(info_ref[0] * span, span), span)
            new_first = a_ref[0, rows].astype(jnp.float32) - rate * ga[0, rows]
            for index in range(gb.shape[2] // WIDE):
                lanes = slice(index * WIDE, (index + 1) * WIDE)
                grad = columns(second_at + index)
                gb[0, :, lanes] = grad
                new_second = b_ref[0, :, lanes].astype(jnp.float32) - rate * grad
                product = jnp.dot(new_first, new_second, precision=lax.Precision.HIGHEST)
                folded[0, :, lanes] = (
                    w_ref[0, :, lanes].astype(jnp.float32) + adapter_scale * product
                ).astype(jnp.bfloat16)

        project(0, 2, aq_ref, bq_ref, wq_ref, gaq, gbq, fq)
        project(1, 5, ao_ref, bo_ref, wo_ref, gao, gbo, fo)
        project(6, 11, au_ref, bu_ref, wu_ref, gau, gbu, fu)
        project(7, 15, ad_ref, bd_ref, wd_ref, gad, gbd, fd)
        extra = [columns(index, RANK, RANK + 8)[:1] for index in (0, 6, 1, 7)]
        gain_out[0] = jnp.concatenate(extra[:2], 0)
        bias_out[0] = jnp.concatenate(extra[2:], 0)
        sums = columns(8, RANK, RANK + 8)[:1]
        sums = jnp.concatenate([sums[:, 128 * index : 128 * (index + 1)] for index in range(3)], 0)
        rms_out[0] = jnp.sqrt(sums / counts_ref[...])

    run()


def finish(place, core, rate, early, late, offsets, layer, counts, trained, frozen, into):
    firsts, seconds = trained[0:8:2], trained[1:8:2]
    layers = firsts[0].shape[0]

    def layer_block(value):
        return pl.BlockSpec((1,) + value.shape[1:], lambda step, *_: (layer, 0, 0))

    shapes = []
    for first, second in zip(firsts, seconds):
        shapes.append(jax.ShapeDtypeStruct(first.shape, jnp.float32))
        shapes.append(jax.ShapeDtypeStruct(second.shape, jnp.float32))
    shapes += [jax.ShapeDtypeStruct((layers, 2, WIDE), jnp.float32)] * 2
    shapes += [jax.ShapeDtypeStruct(matrix.shape, jnp.bfloat16) for matrix in frozen]
    shapes += [jax.ShapeDtypeStruct((layers, 3, 128), jnp.float32)]
    keep = pl.BlockSpec(memory_space=pl.ANY)
    extra = [] if into is None else list(into)
    return pl.pallas_call(
        partial(finish_kernel, offsets),
        out_shape=shapes,
        grid_spec=pltpu.PrefetchScalarGridSpec(
            num_scalar_prefetch=1,
            grid=(1,),
            in_specs=[pl.BlockSpec(memory_space=pltpu.SMEM)]
            + [keep] * 4
            + [pl.BlockSpec((1, 128), lambda step, *_: (0, 0))]
            + [layer_block(value) for value in firsts + seconds + frozen]
            + [keep] * len(extra),
            out_specs=[layer_block(shape) for shape in shapes],
            scratch_shapes=[pltpu.VMEM((16, RANK + 8, WIDE), jnp.bfloat16), pltpu.SemaphoreType.DMA((2,))],
        ),
        input_output_aliases={19 + index: index for index in range(len(extra))},
        compiler_params=pltpu.CompilerParams(vmem_limit_bytes=60 << 20),
        cost_estimate=pl.CostEstimate(flops=1 << 29, bytes_accessed=24 << 20, transcendentals=0),
        name="finish",
    )(jnp.stack([place, core]), rate.reshape(1), *early, *late, counts, *firsts, *seconds, *frozen, *extra)


def mm(left, right):
    return jnp.dot(left, right, preferred_element_type=jnp.float32)


def mm_nt(left, right):
    return lax.dot_general(left, right, (((1,), (1,)), ((), ())), preferred_element_type=jnp.float32)


def mm_tn(left, right):
    return lax.dot_general(left, right, (((0,), (0,)), ((), ())), preferred_element_type=jnp.float32)


def half(value):
    return value.astype(jnp.bfloat16)


def normalize(value):
    centred = value - jnp.mean(value, axis=-1, keepdims=True)
    scale = lax.rsqrt(jnp.mean(centred * centred, axis=-1, keepdims=True) + norm_eps)
    return centred * scale, scale


def norm_gradient(grad, normal, scale, gain):
    pulled = grad * gain
    inner = pulled - jnp.mean(pulled, axis=-1, keepdims=True)
    return scale * (inner - normal * jnp.mean(pulled * normal, axis=-1, keepdims=True))


def rotary_tables(seq_len):
    half_rot = ROT // 2
    lane = jnp.arange(2 * HEAD_DIM) % HEAD_DIM
    freqs = 10000.0 ** (-((lane % half_rot).astype(jnp.float32) * 2.0 / ROT))
    angles = jnp.arange(seq_len, dtype=jnp.float32)[:, None] * freqs[None, :]
    turning = (lane < ROT)[None, :]
    cosine = jnp.where(turning, jnp.cos(angles), 1.0)
    ahead = jnp.where((lane < half_rot)[None, :], -jnp.sin(angles), 0.0)
    behind = jnp.where(turning & (lane >= half_rot)[None, :], jnp.sin(angles), 0.0)
    return jnp.stack([cosine, ahead, behind])


def tile_table(table, rows, columns):
    return jnp.concatenate([jnp.concatenate([table] * (columns // table.shape[1]), 1)] * rows, 0)


def turn(value, cosine, ahead, behind):
    width = value.shape[1]
    step = ROT // 2
    return value * cosine + pltpu.roll(value, width - step, 1) * ahead + pltpu.roll(value, step, 1) * behind


def turn_back(value, cosine, ahead, behind):
    width = value.shape[1]
    step = ROT // 2
    return value * cosine + pltpu.roll(value * ahead, step, 1) + pltpu.roll(value * behind, width - step, 1)


def stack_heads(pair):
    low = lax.broadcasted_iota(jnp.int32, pair.shape, 1) < HEAD_DIM
    zero = jnp.zeros_like(pair)
    return jnp.concatenate([jnp.where(low, pair, zero), jnp.where(low, zero, pair)], 0)


def merge_heads(stacked):
    rows = stacked.shape[0] // 2
    low = lax.broadcasted_iota(jnp.int32, (rows, stacked.shape[1]), 1) < HEAD_DIM
    return jnp.where(low, stacked[:rows], stacked[rows:])


def pair_softmax(query_stack, key_pair, limit):
    scores = mm_nt(query_stack, key_pair) * HEAD_DIM ** (-0.5)
    seq_len = key_pair.shape[0]
    row = lax.broadcasted_iota(jnp.int32, scores.shape, 0) % seq_len
    column = lax.broadcasted_iota(jnp.int32, scores.shape, 1)
    scores = jnp.where((column <= row) & (column < limit), scores, masked_score)
    grown = jnp.exp(scores - jnp.max(scores, axis=-1, keepdims=True))
    return grown / jnp.sum(grown, axis=-1, keepdims=True)


GROUP = 4 * HEAD_DIM
BLOCK = 512


def attention_forward_kernel(
    facts_ref, x_ref, norm_ref, table_ref, first_ref, wq_ref, wk_ref, wv_ref, bq_ref, bk_ref, bv_ref,
    wo_ref, ao_ref, bo_ref,
    q_out, k_out, v_out, mixed_out, midq_out, mido_out, att_out,
    a_scr, mid_scr,
):
    step = pl.program_id(0)
    seqs = x_ref.shape[0] // table_ref.shape[1]
    seq_len = table_ref.shape[1]

    @pl.when(step == 0)
    def _():
        normal, _ = normalize(x_ref[...])
        a_scr[...] = half(normal * norm_ref[0:1] + norm_ref[2:3])
        midq_out[...] = half(mm(a_scr[...], first_ref[...]))
        att_out[...] = jnp.zeros_like(att_out)
        mid_scr[...] = jnp.zeros_like(mid_scr)

    normed = a_scr[...]
    mid = midq_out[...]
    tables = [tile_table(table_ref[index], seqs, GROUP) for index in range(3)]
    query = mm(normed, wq_ref[...]) + adapter_scale * mm(mid, bq_ref[...])
    q_out[...] = half(turn(query, *tables))
    key = mm(normed, wk_ref[...]) + adapter_scale * mm(mid, bk_ref[...])
    k_out[...] = half(turn(key, *tables))
    v_out[...] = half(mm(normed, wv_ref[...]) + adapter_scale * mm(mid, bv_ref[...]))
    for seq in range(seqs):
        rows = slice(seq * seq_len, (seq + 1) * seq_len)
        for pair in range(GROUP // (2 * HEAD_DIM)):
            lanes = slice(pair * 2 * HEAD_DIM, (pair + 1) * 2 * HEAD_DIM)
            probability = pair_softmax(stack_heads(q_out[rows, lanes]), k_out[rows, lanes], facts_ref[0, seq])
            mixed_out[rows, lanes] = half(merge_heads(mm(half(probability), v_out[rows, lanes])))
    mixed = mixed_out[...]
    att_out[...] += mm(mixed, wo_ref[...])
    mid_scr[...] += mm(mixed, ao_ref[...])

    @pl.when(step == pl.num_programs(0) - 1)
    def _():
        mido_out[...] = half(mid_scr[...])
        att_out[...] += adapter_scale * mm(mido_out[...], bo_ref[...])


def whole(*shape):
    return pl.BlockSpec(shape, lambda step, facts_ref: (0,) * len(shape))


def fixed(height, width, down=0, right=0):
    return pl.BlockSpec((height, width), lambda step, facts_ref: (down, right))


def layer_fixed(layer, height, width, down=0, right=0):
    return pl.BlockSpec((None, height, width), lambda step, facts_ref: (layer, down, right))


def layer_columns(layer, height, width, offset=0):
    return pl.BlockSpec((None, height, width), lambda step, facts_ref: (layer, 0, step + offset))


def layer_rows(layer, height, width, offset=0):
    return pl.BlockSpec((None, height, width), lambda step, facts_ref: (layer, step + offset, 0))


def column_block(height, width, offset=0):
    return pl.BlockSpec((height, width), lambda step, facts_ref: (0, step + offset))


def row_block(height, width, offset=0):
    return pl.BlockSpec((height, width), lambda step, facts_ref: (step + offset, 0))


def kernel_call(kernel, name, steps, in_specs, out_specs, out_shape, scratch, flops, size, exps=0, aliases={}):
    return pl.pallas_call(
        kernel,
        out_shape=out_shape,
        grid_spec=pltpu.PrefetchScalarGridSpec(
            num_scalar_prefetch=1, grid=(steps,), in_specs=in_specs, out_specs=out_specs, scratch_shapes=scratch
        ),
        compiler_params=pltpu.CompilerParams(
            dimension_semantics=("arbitrary",), vmem_limit_bytes=48 << 20
        ),
        input_output_aliases=aliases,
        cost_estimate=pl.CostEstimate(flops=flops, bytes_accessed=size, transcendentals=exps),
        name=name,
    )


def shaped(shape, dtype=jnp.bfloat16):
    return jax.ShapeDtypeStruct(shape, dtype)


def attention_forward(residual, weights, norms, tables, facts):
    tokens, width = residual.shape
    groups = width // GROUP
    joint, output = weights[0], weights[1]
    firsts, seconds, _, layer = weights[4:8]
    seq_len = tables.shape[1]
    return kernel_call(
        attention_forward_kernel,
        "attention_forward",
        groups,
        [
            whole(tokens, width),
            whole(4, width),
            whole(3, seq_len, 2 * HEAD_DIM),
            layer_fixed(layer, width, RANK),
            column_block(width, GROUP),
            column_block(width, GROUP, groups),
            column_block(width, GROUP, 2 * groups),
            layer_columns(layer, RANK, GROUP),
            layer_columns(layer, RANK, GROUP, groups),
            layer_columns(layer, RANK, GROUP, 2 * groups),
            row_block(GROUP, width),
            layer_rows(layer, GROUP, RANK, groups),
            layer_fixed(layer, RANK, width, 0, 3),
        ],
        [column_block(tokens, GROUP)] * 4 + [whole(tokens, RANK), whole(tokens, RANK), whole(tokens, width)],
        [shaped((tokens, width))] * 4
        + [shaped((tokens, RANK)), shaped((tokens, RANK)), shaped((tokens, width), jnp.float32)],
        [pltpu.VMEM((tokens, width), jnp.bfloat16), pltpu.VMEM((tokens, RANK), jnp.float32)],
        2 * tokens * width * width * 4,
        2 * 5 * width * width + 12 * tokens * width,
    )(
        facts, residual, norms, tables, firsts, joint, joint, joint, seconds, seconds, seconds, output,
        firsts, seconds,
    )


def feed_forward_kernel(
    facts_ref, x_ref, norm_ref, att_ref, first_ref, wu_ref, bu_ref, wd_ref, ad_ref, bd_ref,
    act_out, slope_out, midu_out, midd_out, x_out, sums_out,
    a_scr, mid_scr,
):
    step = pl.program_id(0)

    @pl.when(step == 0)
    def _():
        normal, _ = normalize(x_ref[...])
        a_scr[...] = half(normal * norm_ref[1:2] + norm_ref[3:4])
        midu_out[...] = half(mm(a_scr[...], first_ref[...]))
        x_out[...] = jnp.zeros_like(x_out)
        mid_scr[...] = jnp.zeros_like(mid_scr)

    upper = mm(a_scr[...], wu_ref[...]) + adapter_scale * mm(midu_out[...], bu_ref[...])
    spread = 0.5 + 0.5 * lax.erf(upper * 0.5**0.5)
    density = jnp.exp(-0.5 * upper * upper) * (0.5 / jnp.pi) ** 0.5
    act_out[...] = half(upper * spread)
    slope_out[...] = half(spread + upper * density)
    active = act_out[...]
    x_out[...] += mm(active, wd_ref[...])
    mid_scr[...] += mm(active, ad_ref[...])

    @pl.when(step == pl.num_programs(0) - 1)
    def _():
        midd_out[...] = half(mid_scr[...])
        feed = x_out[...] + adapter_scale * mm(midd_out[...], bd_ref[...])
        attended = att_ref[...]
        residual = x_ref[...]
        x_out[...] = residual + (attended + feed)
        lane = lax.broadcasted_iota(jnp.int32, (1, 128), 1)
        seqs = facts_ref.shape[1]
        seq_len = residual.shape[0] // seqs
        row = lax.broadcasted_iota(jnp.int32, (seq_len, 1), 0)
        parts = []
        for part in (residual, attended, feed):
            squares = jnp.sum(part * part, axis=-1, keepdims=True)
            sums = jnp.zeros((1, 128), jnp.float32)
            for seq in range(seqs):
                valid = jnp.where(row < facts_ref[0, seq], squares[seq * seq_len : (seq + 1) * seq_len], 0.0)
                counted = (lane == facts_ref[1, seq]) | (lane == DOMAINS)
                sums = sums + jnp.where(counted, jnp.sum(valid), 0.0)
            parts.append(sums)
        sums_out[...] = jnp.concatenate(parts + [jnp.zeros((5, 128), jnp.float32)], 0)


def feed_forward(residual, attended, weights, norms, facts):
    tokens, width = residual.shape
    upper, down = weights[2], weights[3]
    firsts, seconds, _, layer = weights[4:8]
    hidden = upper.shape[1]
    return kernel_call(
        feed_forward_kernel,
        "feed_forward",
        hidden // BLOCK,
        [
            whole(tokens, width),
            whole(4, width),
            whole(tokens, width),
            layer_fixed(layer, width, RANK, 2, 0),
            column_block(width, BLOCK),
            layer_columns(layer, RANK, BLOCK, 4 * width // BLOCK),
            row_block(BLOCK, width),
            layer_rows(layer, BLOCK, RANK, 3 * width // BLOCK),
            layer_fixed(layer, RANK, width, 0, 8),
        ],
        [column_block(tokens, BLOCK)] * 2
        + [whole(tokens, RANK), whole(tokens, RANK), whole(tokens, width), whole(8, 128)],
        [shaped((tokens, hidden))] * 2
        + [shaped((tokens, RANK))] * 2
        + [shaped((tokens, width), jnp.float32), shaped((8, 128), jnp.float32)],
        [pltpu.VMEM((tokens, width), jnp.bfloat16), pltpu.VMEM((tokens, RANK), jnp.float32)],
        2 * tokens * width * hidden * 2,
        4 * width * hidden + 4 * tokens * hidden + 12 * tokens * width,
        2 * tokens * hidden,
    )(facts, residual, norms, attended, firsts, upper, seconds, down, firsts, seconds)


def write_extra(block_out, grad, normal, sums):
    width = grad.shape[1]
    row = [jnp.sum(grad * normal, axis=0, keepdims=True), jnp.sum(grad, axis=0, keepdims=True)] + sums
    rest = block_out.shape[1] - sum(part.shape[1] for part in row)
    row = jnp.concatenate(row + [jnp.zeros((1, rest), jnp.float32)], 1)
    block_out[RANK:, :] = half(jnp.concatenate([row, jnp.zeros((7, row.shape[1]), jnp.float32)], 0))


def block_copies(block_out, whole_out, first, sem):
    width = whole_out.shape[2]
    copies = []
    for index in range(block_out.shape[1] // width):
        source = block_out.at[:, pl.ds(index * width, width)]
        copies.append(pltpu.make_async_copy(source, whole_out.at[first + index], sem.at[index]))
        copies[-1].start()
    return copies


def feed_backward_kernel(
    facts_ref, g_ref, x_ref, norm_ref, act_ref, slope_ref, midu_ref, midd_ref, sums_ref, wu_ref, wd_ref, au_ref,
    bu_ref, ad_ref, bd_ref,
    whole_out, gx_out,
    block_out, g_scr, gmd_scr, gmdt_scr, midut_scr, gmu_scr, sem,
):
    step = pl.program_id(0)
    width = x_ref.shape[1]
    hidden = pl.num_programs(0) * BLOCK

    @pl.when(step == 0)
    def _():
        g_scr[...] = half(g_ref[...])
        grad_mid = adapter_scale * mm_nt(g_scr[...], bd_ref[...])
        gmd_scr[...] = half(grad_mid)
        gmdt_scr[...] = half(half(grad_mid).astype(jnp.float32).T)
        midut_scr[...] = half(midu_ref[...].astype(jnp.float32).T)
        gx_out[...] = jnp.zeros_like(gx_out)
        gmu_scr[...] = jnp.zeros_like(gmu_scr)
        middt = half(midd_ref[...].astype(jnp.float32).T)
        block_out[:RANK, pl.ds(width + 2 * hidden, width)] = half(adapter_scale * mm(middt, g_scr[...]))

    grad_act = mm_nt(g_scr[...], wd_ref[...]) + mm_nt(gmd_scr[...], ad_ref[...])
    grad_up = half(half(grad_act).astype(jnp.float32) * slope_ref[...].astype(jnp.float32))
    first_at = pl.multiple_of(width + step * BLOCK, BLOCK)
    second_at = pl.multiple_of(width + hidden + step * BLOCK, BLOCK)
    block_out[:RANK, pl.ds(first_at, BLOCK)] = half(mm(gmdt_scr[...], act_ref[...]))
    block_out[:RANK, pl.ds(second_at, BLOCK)] = half(adapter_scale * mm(midut_scr[...], grad_up))
    gmu_scr[...] += mm_nt(grad_up, bu_ref[...])
    gx_out[...] += mm_nt(grad_up, wu_ref[...])

    @pl.when(step == pl.num_programs(0) - 1)
    def _():
        grad_mid = half(adapter_scale * gmu_scr[...])
        normal, scale = normalize(x_ref[...])
        normed = half(normal * norm_ref[1:2] + norm_ref[3:4])
        block_out[:RANK, :width] = half(mm(half(grad_mid.astype(jnp.float32).T), normed))
        grad = gx_out[...] + mm_nt(grad_mid, au_ref[...])
        write_extra(block_out, grad, normal, [sums_ref[index : index + 1] for index in range(3)])
        gather = block_copies(block_out, whole_out, 6, sem)
        gx_out[...] = g_ref[...] + norm_gradient(grad, normal, scale, norm_ref[1:2])
        for copy in gather:
            copy.wait()


def feed_backward(gradient, residual, weights, norms, kept, facts):
    tokens, width = residual.shape
    upper, down = weights[2], weights[3]
    firsts, seconds, _, layer = weights[4:8]
    active, slope, mid_u, mid_d, sums = kept
    hidden = upper.shape[1]
    return kernel_call(
        feed_backward_kernel,
        "feed_backward",
        hidden // BLOCK,
        [
            whole(tokens, width),
            whole(tokens, width),
            whole(4, width),
            column_block(tokens, BLOCK),
            column_block(tokens, BLOCK),
            whole(tokens, RANK),
            whole(tokens, RANK),
            whole(8, 128),
            column_block(width, BLOCK),
            row_block(BLOCK, width),
            layer_fixed(layer, width, RANK, 2, 0),
            layer_columns(layer, RANK, BLOCK, 4 * width // BLOCK),
            layer_rows(layer, BLOCK, RANK, 3 * width // BLOCK),
            layer_fixed(layer, RANK, width, 0, 8),
        ],
        [pl.BlockSpec(memory_space=pl.ANY), whole(tokens, width)],
        [shaped((16, RANK + 8, width)), shaped((tokens, width), jnp.float32)],
        [
            pltpu.VMEM((RANK + 8, 2 * width + 2 * hidden), jnp.bfloat16),
            pltpu.VMEM((tokens, width), jnp.bfloat16),
            pltpu.VMEM((tokens, RANK), jnp.bfloat16),
            pltpu.VMEM((RANK, tokens), jnp.bfloat16),
            pltpu.VMEM((RANK, tokens), jnp.bfloat16),
            pltpu.VMEM((tokens, RANK), jnp.float32),
            pltpu.SemaphoreType.DMA((10,)),
        ],
        2 * tokens * width * hidden * 2,
        4 * width * hidden + 4 * tokens * hidden + 16 * tokens * width,
    )(
        facts, gradient, residual, norms, active, slope, mid_u, mid_d, sums, upper, down, firsts, seconds,
        firsts, seconds,
    )


def attention_backward_kernel(
    facts_ref, g_ref, gx_ref, x_ref, norm_ref, table_ref, q_ref, k_ref, v_ref, mixed_ref, midq_ref, mido_ref,
    wq_ref, wk_ref, wv_ref, aq_ref, bq_ref, bk_ref, bv_ref, wo_ref, ao_ref, bo_ref, feed_block_ref,
    whole_out, gx_out,
    block_out, g_scr, gmo_scr, gmot_scr, midqt_scr, gmq_scr, acc_scr, gq_scr, gk_scr, gv_scr, sem,
):
    step = pl.program_id(0)
    width = x_ref.shape[1]
    seq_len = table_ref.shape[1]
    seqs = x_ref.shape[0] // seq_len
    scale_factor = HEAD_DIM ** (-0.5)

    @pl.when(step == 0)
    def _():
        g_scr[...] = half(g_ref[...])
        grad_mid = half(adapter_scale * mm_nt(g_scr[...], bo_ref[...]))
        gmo_scr[...] = grad_mid
        gmot_scr[...] = half(grad_mid.astype(jnp.float32).T)
        midqt_scr[...] = half(midq_ref[...].astype(jnp.float32).T)
        acc_scr[...] = jnp.zeros_like(acc_scr)
        gmq_scr[...] = jnp.zeros_like(gmq_scr)
        midot = half(mido_ref[...].astype(jnp.float32).T)
        block_out[:RANK, pl.ds(5 * width, width)] = half(adapter_scale * mm(midot, g_scr[...]))

    grad_mixed = half(mm_nt(g_scr[...], wo_ref[...]) + mm_nt(gmo_scr[...], ao_ref[...]))
    first_at = pl.multiple_of(width + step * GROUP, GROUP)
    block_out[:RANK, pl.ds(first_at, GROUP)] = half(mm(gmot_scr[...], mixed_ref[...]))
    for seq in range(seqs):
        rows = slice(seq * seq_len, (seq + 1) * seq_len)
        for pair in range(GROUP // (2 * HEAD_DIM)):
            lanes = slice(pair * 2 * HEAD_DIM, (pair + 1) * 2 * HEAD_DIM)
            query_stack = stack_heads(q_ref[rows, lanes])
            key_pair = k_ref[rows, lanes]
            probability = pair_softmax(query_stack, key_pair, facts_ref[0, seq])
            grad_stack = stack_heads(grad_mixed[rows, lanes])
            grad_prob = mm_nt(grad_stack, v_ref[rows, lanes])
            gv_scr[rows, lanes] = half(mm_tn(half(probability), grad_stack))
            inner = jnp.sum(probability * grad_prob, axis=-1, keepdims=True)
            grad_scores = half(probability * (grad_prob - inner))
            gq_scr[rows, lanes] = merge_heads(mm(grad_scores, key_pair)) * scale_factor
            gk_scr[rows, lanes] = mm_tn(grad_scores, query_stack) * scale_factor
    tables = [tile_table(table_ref[index], seqs, GROUP) for index in range(3)]
    joint = (half(turn_back(gq_scr[...], *tables)), half(turn_back(gk_scr[...], *tables)), gv_scr[...])
    mid = midqt_scr[...]
    for index, (grad, w_ref, b_ref) in enumerate(zip(joint, (wq_ref, wk_ref, wv_ref), (bq_ref, bk_ref, bv_ref))):
        second_at = pl.multiple_of((2 + index) * width + step * GROUP, GROUP)
        block_out[:RANK, pl.ds(second_at, GROUP)] = half(adapter_scale * mm(mid, grad))
        gmq_scr[...] += mm_nt(grad, b_ref[...])
        acc_scr[...] += mm_nt(grad, w_ref[...])

    @pl.when(step == pl.num_programs(0) - 1)
    def _():
        grad_mid = half(adapter_scale * gmq_scr[...])
        normal, scale = normalize(x_ref[...])
        normed = half(normal * norm_ref[0:1] + norm_ref[2:3])
        block_out[:RANK, :width] = half(mm(half(grad_mid.astype(jnp.float32).T), normed))
        grad = acc_scr[...] + mm_nt(grad_mid, aq_ref[...])
        write_extra(block_out, grad, normal, [])
        gather = block_copies(block_out, whole_out, 0, sem)
        gx_out[...] = gx_ref[...] + norm_gradient(grad, normal, scale, norm_ref[0:1])
        for copy in gather:
            copy.wait()


def attention_backward(gradient, grad_feed, feed_block, residual, weights, norms, tables, kept, facts):
    tokens, width = residual.shape
    groups = width // GROUP
    joint, output = weights[0], weights[1]
    firsts, seconds, _, layer = weights[4:8]
    queries, keys, values, mixed, mid_q, mid_o = kept
    seq_len = tables.shape[1]
    block = column_block(tokens, GROUP)
    return kernel_call(
        attention_backward_kernel,
        "attention_backward",
        groups,
        [
            whole(tokens, width),
            whole(tokens, width),
            whole(tokens, width),
            whole(4, width),
            whole(3, seq_len, 2 * HEAD_DIM),
            block,
            block,
            block,
            block,
            whole(tokens, RANK),
            whole(tokens, RANK),
            column_block(width, GROUP),
            column_block(width, GROUP, groups),
            column_block(width, GROUP, 2 * groups),
            layer_fixed(layer, width, RANK),
            layer_columns(layer, RANK, GROUP),
            layer_columns(layer, RANK, GROUP, groups),
            layer_columns(layer, RANK, GROUP, 2 * groups),
            row_block(GROUP, width),
            layer_rows(layer, GROUP, RANK, groups),
            layer_fixed(layer, RANK, width, 0, 3),
            pl.BlockSpec(memory_space=pl.ANY),
        ],
        [pl.BlockSpec(memory_space=pl.ANY), whole(tokens, width)],
        [shaped((16, RANK + 8, width)), shaped((tokens, width), jnp.float32)],
        [
            pltpu.VMEM((RANK + 8, 6 * width), jnp.bfloat16),
            pltpu.VMEM((tokens, width), jnp.bfloat16),
            pltpu.VMEM((tokens, RANK), jnp.bfloat16),
            pltpu.VMEM((RANK, tokens), jnp.bfloat16),
            pltpu.VMEM((RANK, tokens), jnp.bfloat16),
            pltpu.VMEM((tokens, RANK), jnp.float32),
            pltpu.VMEM((tokens, width), jnp.float32),
            pltpu.VMEM((tokens, GROUP), jnp.float32),
            pltpu.VMEM((tokens, GROUP), jnp.float32),
            pltpu.VMEM((tokens, GROUP), jnp.bfloat16),
            pltpu.SemaphoreType.DMA((6,)),
        ],
        2 * tokens * width * width * 4,
        2 * 5 * width * width + 24 * tokens * width,
        aliases={22: 0},
    )(
        facts, gradient, grad_feed, residual, norms, tables, queries, keys, values, mixed, mid_q, mid_o, joint,
        joint, joint, firsts, seconds, seconds, seconds, output, firsts, seconds, feed_block,
    )


def layer_forward(residual, weights, tables, facts):
    norms = weights[6]
    *kept_attention, attended = attention_forward(residual, weights, norms, tables, facts)
    *kept_feed, output, sums = feed_forward(residual, attended, weights, norms, facts)
    return output, (residual, kept_attention, kept_feed + [sums])


def layer_backward(gradient, kept, weights, tables, facts, after=()):
    residual, kept_attention, kept_feed = kept
    norms = weights[6]
    feed_block, grad_feed = feed_backward(gradient, residual, weights, norms, kept_feed, facts)
    if after:
        grad_feed = tie(grad_feed, *after)
    block, grad_input = attention_backward(
        gradient, grad_feed, feed_block, residual, weights, norms, tables, kept_attention, facts
    )
    return grad_input, block


def gather_plan(gathers, turns):
    if (gathers, turns) == (4, 3):
        return [[0, 2], [0, 2], [0, 1], [2, 1], [1, 3], [3], [3]]
    order = [0, 2, 1, 3]
    return [[order[step // turns]] for step in range(gathers * turns)]


def shards(
    inputs,
    cotangent,
    domain,
    lengths,
    steps_since_reset,
    frozen_query_weight,
    frozen_output_weight,
    frozen_up_weight,
    frozen_down_weight,
    query_adapter_first,
    query_adapter_second,
    output_adapter_first,
    output_adapter_second,
    up_adapter_first,
    up_adapter_second,
    down_adapter_first,
    down_adapter_second,
    layer_norm_gain,
    layer_norm_bias,
):
    core = lax.axis_index("section")
    place = lax.axis_index("dp")
    count = lax.axis_size("dp")
    middle = count // 2
    stage = place // middle
    low = place % middle
    home = core == stage
    masks = [1 << bit for bit in range(middle.bit_length() - 1)]
    frozen = (frozen_query_weight, frozen_output_weight, frozen_up_weight, frozen_down_weight)
    trained = (
        query_adapter_first,
        query_adapter_second,
        output_adapter_first,
        output_adapter_second,
        up_adapter_first,
        up_adapter_second,
        down_adapter_first,
        down_adapter_second,
    )
    local_layers = frozen_query_weight.shape[0]
    rows_dev, seq_len, model_width = inputs.shape
    tokens = rows_dev * seq_len

    places = [(index // middle, index) for index in range(count)]
    to_sibling = [(here * count + index, (1 - here) * count + index) for here, index in places]
    to_cross = [((1 - here) * count + index, here * count + (index ^ middle)) for here, index in places]
    sibling, cross = [partial(both_axes, pairs=pairs) for pairs in (to_sibling, to_cross)]

    same, other = pack_halves(core, frozen)
    swapped = flip_core(other)
    own = jnp.where(home, same, swapped)
    leaving = jnp.where(home, swapped, same)
    partner = [flip_place(leaving[0], middle)]
    for layer in range(1, local_layers):
        partner.append(flip_place(tie(leaving[layer], partner[-1]), middle))
    gathers = []
    for layer in range(local_layers):
        gathers.append(Gather(layer, 0, own[layer], masks))
        gathers.append(Gather(layer, 1, partner[layer], masks))
    plan = gather_plan(len(gathers), len(masks)) + [[]]
    dense = [None] * local_layers
    facts = jnp.stack([lengths, domain])
    norms = jnp.concatenate([layer_norm_gain, layer_norm_bias], 1)
    facts = jnp.where(home, facts, cross(facts))
    norms = jnp.where(home, norms, sibling(norms))
    packed = [
        jnp.concatenate([factor for factor in trained[0::2]], 1),
        jnp.concatenate([factor for factor in trained[1::2]], 2),
    ]
    visiting = jnp.where(stage == 0, cotangent, inputs)
    tables = rotary_tables(seq_len)
    ended, fresh, started, waiting = (), [], set(), []
    bases = [jnp.where(stage == which, 0, middle) for which in range(2)]
    for number, active in enumerate(plan):
        for index in active:
            if index not in started:
                started.add(index)
                gather = gathers[index]
                fresh = fresh + [(gather.block, part, 1, gather, part, [0]) for part in range(3)]
        extra = []
        if number < 2:
            extra.append((packed[number], sibling))
        if number == 4:
            extra.append((visiting, cross))
        moving = fresh if number >= 2 else []
        there, came, collected, swapped, results = gather_step(
            [gathers[index] for index in active], masks, moving, extra, ended
        )
        fresh = came if moving else fresh + came
        if number < 2:
            packed[number] = jnp.where(home, packed[number], results[0])
        if number == 4:
            visiting = results[0]
        marks = [assemble(*waiting.pop(0), count, dense)] if waiting and number < len(plan) - 1 else []
        ended = tuple(there) + tuple(results) + tuple(marks)
        if moving:
            ended = ended + (swapped,)
            layout = [(gather.layer, part) for _, _, size, gather, part, _ in moving for _ in range(size)]
            places_of = [
                (known ^ low) + bases[gather.which] for _, _, _, gather, _, found in moving for known in found
            ]
            info = jnp.stack([core] + places_of)
            waiting.append((info, layout, collected, swapped))
    for item in waiting:
        assemble(*item, count, dense)
    weights = [tuple(dense[layer]) + (packed[0], packed[1], norms[layer], layer) for layer in range(local_layers)]
    start = jnp.where(home, inputs, visiting).astype(jnp.float32).reshape(tokens, model_width)
    valid = jnp.arange(seq_len)[None, :] < facts[0][:, None]
    end_grad = jnp.where(home, cotangent, visiting).astype(jnp.float32)
    end_grad = jnp.where(stage == 1, end_grad * valid[..., None].astype(jnp.float32), 0.0)
    end_grad = end_grad.reshape(tokens, model_width)
    def stage_forward(residual):
        kept = []
        for layer in range(local_layers):
            residual, kept_state = layer_forward(residual, weights[layer], tables, facts)
            kept.append(kept_state)
        return residual, kept

    boundary, _ = stage_forward(start)
    boundary = boundary.astype(jnp.bfloat16)
    forward_pairs = [(index, index + middle) for index in range(middle)]
    received = lax.ppermute(boundary, "dp", forward_pairs)
    entry = jnp.where(stage == 0, start, received.astype(jnp.float32))
    final, kept = stage_forward(entry)
    final = final.astype(jnp.bfloat16)

    gradient = end_grad
    late = [None] * local_layers
    for layer in reversed(range(local_layers)):
        gradient, late[layer] = layer_backward(gradient, kept[layer], weights[layer], tables, facts)
    sent = gradient.astype(jnp.bfloat16)
    came_back = lax.ppermute(sent, "dp", [(after, before) for before, after in forward_pairs])
    late_halves = tie([swap_halves(block, 1, core, count) for block in late], came_back)
    late_piece = sum_halves(late_halves, count)

    gradient = jnp.where(stage == 0, came_back.astype(jnp.float32), 0.0)
    pieces = [None] * local_layers
    last = late_piece
    for layer in reversed(range(local_layers)):
        gradient, block = layer_backward(gradient, kept[layer], weights[layer], tables, facts)
        halves = swap_halves(block, 0, core, count)
        pieces[layer] = last = sum_halves([tie(halves, last)], count)
    late_piece = cross_section(tie(late_piece, pieces[local_layers - 1]), 1, stage, count)
    early_piece = cross_section(jnp.concatenate(pieces, 0), 0, stage, count)
    late_whole = spread_section(tie(late_piece, last), 1, count)
    early_whole = spread_section(tie(early_piece, late_whole[1]), 0, count)

    out_pairs = [(count + index + middle, index + middle) for index in range(middle)]
    out_pairs = out_pairs + [(index + middle, count + index) for index in range(middle)]
    visiting = both_axes(jnp.where(core == 0, final, received), out_pairs)
    section_out = jnp.where(home, jnp.where(stage == 0, boundary, final), visiting)
    section_out = section_out.reshape(1, rows_dev, seq_len, model_width)
    grad_pairs = [(index, count + index) for index in range(middle)]
    grad_pairs = grad_pairs + [(count + index, index + middle) for index in range(middle)]
    visiting = both_axes(jnp.where(core == 0, came_back, gradient.astype(jnp.bfloat16)), grad_pairs)
    section_grad = jnp.where(
        home, jnp.where(stage == 0, gradient, sent.astype(jnp.float32)), visiting.astype(jnp.float32)
    )
    section_grad = section_grad.reshape(1, rows_dev, seq_len, model_width)

    lane = jnp.arange(128)
    counted = (domain[:, None] == lane[None, :]) | (lane == DOMAINS)[None, :]
    counts = jnp.sum(jnp.where(counted, lengths.astype(jnp.float32)[:, None], 0.0), axis=0, keepdims=True)
    counts = tie(counts, final)
    for mask in masks + [middle]:
        counts = counts + flip_place(counts, mask)
    counts = jnp.maximum(counts, 1.0) * model_width
    rate = peak_rate * (steps_since_reset[0].astype(jnp.float32) + 1.0) / WARM
    outputs = None
    for layer in reversed(range(local_layers)):
        offsets = (layer * (RANK + 8),) * 2
        outputs = finish(
            place, core, rate, early_whole, late_whole, offsets, layer, counts, trained, frozen, outputs
        )
    *outputs, rms = outputs
    return (section_out, section_grad, *outputs, rms[:, :, : DOMAINS + 1])


def solution(mesh):
    across = P("dp", None, None)
    copied = P("section", None, None)
    split = P("section", "dp", None)
    wide = P("section", "dp", None, None)
    return jax.shard_map(
        shards,
        mesh=mesh,
        in_specs=(across, across, P("dp"), P("dp"), P()) + (split,) * 4 + (copied,) * 10,
        out_specs=(wide, wide) + (copied,) * 10 + (split,) * 4 + (copied,),
        check_vma=False,
    )
```

```python
from functools import partial

import jax
import jax.numpy as jnp
from jax import lax
from jax.experimental import pallas as pl
from jax.experimental.pallas import tpu as pltpu
from jax.sharding import PartitionSpec as P

HEADS = 16
HEAD_DIM = 64
ROT = 16
DOMAINS = 16
WARM = 50
RANK = 128
WIDE = 1024
UNITS = 12
HALF_UNITS = 6

adapter_scale = 0.5
norm_eps = 1e-05
peak_rate = 0.0002
masked_score = -1e30


def both_axes(value, pairs):
    return lax.ppermute(value, ("section", "dp"), pairs)


def tie(value, *others):
    return lax.optimization_barrier((value, others))[0]


def flip_place(value, mask):
    count = lax.axis_size("dp")
    return lax.ppermute(value, "dp", [(place, place ^ mask) for place in range(count)])


def flip_core(value):
    return lax.ppermute(value, "section", [(0, 1), (1, 0)])


def pack_kernel(info_ref, query_ref, output_ref, upper_ref, down_ref, keep_ref, send_ref):
    rows = output_ref.shape[1]

    def write(first, second):
        for layer in range(output_ref.shape[0]):
            first[layer, 0] = query_ref[layer, :, :WIDE]
            first[layer, 1] = query_ref[layer, :, WIDE : 2 * WIDE]
            first[layer, 2] = query_ref[layer, :, 2 * WIDE :]
            first[layer, 3] = output_ref[layer]
            first[layer, 4] = upper_ref[layer, :, :WIDE]
            first[layer, 5] = upper_ref[layer, :, WIDE : 2 * WIDE]
            second[layer, 0] = upper_ref[layer, :, 2 * WIDE : 3 * WIDE]
            second[layer, 1] = upper_ref[layer, :, 3 * WIDE :]
            for index in range(4):
                second[layer, 2 + index] = down_ref[layer, index * rows : (index + 1) * rows]

    @pl.when(info_ref[0] == 0)
    def _():
        write(keep_ref, send_ref)

    @pl.when(info_ref[0] != 0)
    def _():
        write(send_ref, keep_ref)


def pack_halves(core, frozen):
    layers, rows = frozen[1].shape[:2]
    shape = jax.ShapeDtypeStruct((layers, HALF_UNITS, rows, WIDE), jnp.bfloat16)
    vmem = pl.BlockSpec(memory_space=pltpu.VMEM)
    return pl.pallas_call(
        pack_kernel,
        out_shape=[shape, shape],
        in_specs=[pl.BlockSpec(memory_space=pltpu.SMEM)] + [vmem] * 4,
        out_specs=[vmem, vmem],
        compiler_params=pltpu.CompilerParams(vmem_limit_bytes=32 << 20),
        cost_estimate=pl.CostEstimate(
            flops=0, bytes_accessed=8 * HALF_UNITS * layers * rows * WIDE, transcendentals=0
        ),
        name="pack",
    )(core.reshape(1), *frozen)


def pack_adapters_kernel(*refs):
    sources, (first_out, second_out) = refs[:8], refs[-2:]
    at = 0
    for source in sources[0::2]:
        first_out[:, at : at + source.shape[1]] = source[...]
        at = at + source.shape[1]
    at = 0
    for source in sources[1::2]:
        second_out[:, :, at : at + source.shape[2]] = source[...]
        at = at + source.shape[2]


def pack_adapters(trained, *after):
    layers = trained[0].shape[0]
    height = sum(factor.shape[1] for factor in trained[0::2])
    width = sum(factor.shape[2] for factor in trained[1::2])
    shapes = [
        jax.ShapeDtypeStruct((layers, height, RANK), jnp.bfloat16),
        jax.ShapeDtypeStruct((layers, RANK, width), jnp.bfloat16),
    ]

    def layer_block(value):
        return pl.BlockSpec((1,) + value.shape[1:], lambda step: (step, 0, 0))

    return pl.pallas_call(
        pack_adapters_kernel,
        out_shape=shapes,
        grid=(layers,),
        in_specs=[layer_block(factor) for factor in trained] + [pl.BlockSpec(memory_space=pl.ANY)] * len(after),
        out_specs=[layer_block(shape) for shape in shapes],
        compiler_params=pltpu.CompilerParams(vmem_limit_bytes=30 << 20),
        cost_estimate=pl.CostEstimate(flops=0, bytes_accessed=4 * RANK * layers * (height + width), transcendentals=0),
        name="pack_adapters",
    )(*trained, *after)


def rotations(masks):
    return [[masks[(start + index) % len(masks)] for index in range(len(masks))] for start in range(3)]


def assemble_kernel(layout, info_ref, mine, theirs, *refs):
    count = len({layer for layer, _ in layout})
    outs, token_out, sem = refs[-4 * count - 2 : -2], refs[-2], refs[-1]
    token_out[...] = jnp.zeros_like(token_out)
    first_layer = min(layer for layer, _ in layout)
    rows = mine.shape[2]

    def targets(half_index, layer, part, place):
        query_out, output_out, upper_out, down_out = outs[4 * (layer - first_layer) : 4 * (layer - first_layer) + 4]
        at = pl.multiple_of(place * rows, rows)
        down_at = pl.multiple_of(place * 4 * rows, rows)

        def columns(out, index):
            return out.at[pl.ds(at, rows), pl.ds(index * WIDE, WIDE)]

        def down(index):
            return down_out.at[pl.ds(down_at + index * rows, rows)]

        return [
            [(columns(query_out, 0), columns(query_out, 1)), (columns(query_out, 2), columns(output_out, 0)),
             (columns(upper_out, 0), columns(upper_out, 1))],
            [(columns(upper_out, 2), columns(upper_out, 3)), (down(0), down(1)), (down(2), down(3))],
        ][half_index][part]

    def run(first, second):
        copies = []
        for block, (layer, part) in enumerate(layout):
            for half_index, source in enumerate((first, second)):
                for unit, target in enumerate(targets(half_index, layer, part, info_ref[1 + block])):
                    where = sem.at[block, half_index * 2 + unit]
                    copies.append(pltpu.make_async_copy(source.at[block, unit], target, where))
                    copies[-1].start()
        for copy in copies:
            copy.wait()

    @pl.when(info_ref[0] == 0)
    def _():
        run(mine, theirs)

    @pl.when(info_ref[0] != 0)
    def _():
        run(theirs, mine)


def assemble(info, layout, mine, theirs, count, into):
    rows = mine.shape[2]
    total = rows * count
    layers = sorted({layer for layer, _ in layout})
    shapes = [(total, 3 * WIDE), (total, WIDE), (total, 4 * WIDE), (4 * total, WIDE)] * len(layers)
    extra = [matrix for layer in layers for matrix in (into[layer] or ())]
    anywhere = pl.BlockSpec(memory_space=pltpu.HBM)
    aliases, index = {}, 3
    for position, layer in enumerate(layers):
        if into[layer]:
            for matrix in range(4):
                aliases[index] = 4 * position + matrix
                index = index + 1
    made = pl.pallas_call(
        partial(assemble_kernel, tuple(layout)),
        out_shape=[jax.ShapeDtypeStruct(shape, jnp.bfloat16) for shape in shapes]
        + [jax.ShapeDtypeStruct((8, 128), jnp.float32)],
        in_specs=[pl.BlockSpec(memory_space=pltpu.SMEM)]
        + [pl.BlockSpec(memory_space=pltpu.VMEM)] * 2
        + [anywhere] * len(extra),
        out_specs=[anywhere] * len(shapes) + [pl.BlockSpec(memory_space=pltpu.VMEM)],
        scratch_shapes=[pltpu.SemaphoreType.DMA((len(layout), 4))],
        input_output_aliases=aliases,
        compiler_params=pltpu.CompilerParams(vmem_limit_bytes=60 << 20),
        cost_estimate=pl.CostEstimate(flops=0, bytes_accessed=12 * mine.size, transcendentals=0),
        name="assemble",
    )(info, mine, theirs, *extra)
    for position, layer in enumerate(layers):
        into[layer] = made[4 * position : 4 * position + 4]
    return made[-1]


def copy_kernel(plans, *refs):
    inputs, outs = refs[: -len(plans)], refs[-len(plans) :]
    for plan, out in zip(plans, outs):
        at = 0
        for source, begin, size in plan:
            out[at : at + size] = inputs[source][begin : begin + size]
            at = at + size


def copy_blocks(arrays, plans, after):
    tail = arrays[0].shape[1:]
    vmem = pl.BlockSpec(memory_space=pltpu.VMEM)
    shapes = [jax.ShapeDtypeStruct((sum(size for _, _, size in plan),) + tail, jnp.bfloat16) for plan in plans]
    moved = 4 * sum(shape.size for shape in shapes)
    return pl.pallas_call(
        partial(copy_kernel, tuple(tuple(plan) for plan in plans)),
        out_shape=shapes,
        in_specs=[vmem] * len(arrays) + [pl.BlockSpec(memory_space=pl.ANY)] * len(after),
        out_specs=[vmem] * len(shapes),
        compiler_params=pltpu.CompilerParams(vmem_limit_bytes=40 << 20),
        cost_estimate=pl.CostEstimate(flops=0, bytes_accessed=moved, transcendentals=0),
        name="collect",
    )(*arrays, *after)


class Gather:
    def __init__(self, layer, which, block, masks):
        self.layer, self.which = layer, which
        block = block.reshape((3, 2) + block.shape[1:])
        self.block = block
        self.held = [[(block, part, 1)] for part in range(3)]
        self.found = [[0], [0], [0]]
        self.turns = rotations(masks)
        self.step = 0


class Store:
    def __init__(self):
        self.arrays = []

    def index(self, array):
        for position, known in enumerate(self.arrays):
            if known is array:
                return position
        self.arrays.append(array)
        return len(self.arrays) - 1


def gather_step(active, masks, fresh, extra, after):
    store = Store()
    plans, lists = [], []
    for mask in masks:
        entries = [
            (gather, part) for gather in active for part in range(3) if gather.turns[part][gather.step] == mask
        ]
        if entries:
            plans.append(
                [
                    (store.index(array), begin, size)
                    for gather, part in entries
                    for array, begin, size in gather.held[part]
                ]
            )
            lists.append((mask, entries))
    if fresh:
        plans.append([(store.index(array), begin, size) for array, begin, size, _, _, _ in fresh])
    after = [value for value in after if all(value is not known for known in store.arrays)]
    values = list(copy_blocks(store.arrays, plans, after)) + [value for value, _ in extra]
    there = []
    for value, (mask, _) in zip(values, lists):
        there.append(flip_place(value, mask))
    collected = values[len(lists)] if fresh else None
    swapped = flip_core(collected) if fresh else None
    results = [send(value) for value, (_, send) in zip(values[len(plans) :], extra)]
    came = []
    for (mask, entries), value in zip(lists, there):
        begin = 0
        for gather, part in entries:
            size = sum(amount for _, _, amount in gather.held[part])
            known = [place ^ gather.turns[part][gather.step] for place in gather.found[part]]
            gather.held[part] = gather.held[part] + [(value, begin, size)]
            gather.found[part] = gather.found[part] + known
            came.append((value, begin, size, gather, part, known))
            begin = begin + size
    for gather in active:
        gather.step = gather.step + 1
    return there, came, collected, swapped, results


def pieces_by_place(block, pieces):
    if pieces == block.shape[0]:
        return block
    split = pieces // block.shape[0]
    columns = block.shape[2] // split
    block = block.reshape(block.shape[0], block.shape[1], split, columns).transpose(0, 2, 1, 3)
    return block.reshape(pieces, block.shape[2], columns)


def places_to_blocks(pieces, blocks):
    if pieces.shape[0] == blocks:
        return pieces
    split = pieces.shape[0] // blocks
    rows, columns = pieces.shape[1:]
    return pieces.reshape(blocks, split, rows, columns).transpose(0, 2, 1, 3).reshape(blocks, rows, split * columns)


def exchange(value, count):
    middle = count // 2
    groups = [[half_index * middle + index for index in range(middle)] for half_index in range(2)]
    return lax.all_to_all(value, "dp", 0, 0, axis_index_groups=groups)


def swap_halves(block, section, core, count):
    middle = count // 2
    inside = [place for place in range(count) if place // middle == section]
    swap = [(here * count + place, (1 - here) * count + place) for here in range(2) for place in inside]
    size = block.shape[0] // 2
    there = both_axes(lax.dynamic_slice_in_dim(block, (1 - core) * size, size, 0), swap)
    here = lax.dynamic_slice_in_dim(block, core * size, size, 0)
    return (here.astype(jnp.float32) + there.astype(jnp.float32)).astype(jnp.bfloat16)


def sum_halves(halves, count):
    pieces = [pieces_by_place(part, count // 2) for part in halves]
    pieces = pieces[0] if len(pieces) == 1 else jnp.concatenate(pieces, 1)
    return jnp.sum(exchange(pieces, count).astype(jnp.float32), axis=0).astype(jnp.bfloat16)


def scatter_section(blocks, section, core, count):
    return sum_halves([swap_halves(block, section, core, count) for block in blocks], count)


def cross_section(piece, section, stage, count):
    middle = count // 2
    across = [(place, place ^ middle) for place in range(count) if place // middle == section]
    return jnp.where(stage == section, piece, lax.ppermute(piece, "dp", across))


def spread_section(piece, section, count):
    middle = count // 2
    spread = exchange(jnp.broadcast_to(piece[None], (middle,) + piece.shape), count)
    here = places_to_blocks(spread, 8)
    there = lax.ppermute(here, "section", [(1 - section, section)])
    return (here, there) if section == 0 else (there, here)


def finish_kernel(
    info_ref, rate_ref, early0_ref, early1_ref, late0_ref, late1_ref, counts_ref,
    aq_ref, ao_ref, au_ref, ad_ref, bq_ref, bo_ref, bu_ref, bd_ref, wq_ref, wo_ref, wu_ref, wd_ref, *refs,
):
    gaq, gbq, gao, gbo, gau, gbu, gad, gbd, gain_out, bias_out, fq, fo, fu, fd, rms_out, g_ref, sem = refs[-17:]
    rate = rate_ref[0]
    size, height = early0_ref.shape[0], g_ref.shape[1]

    def fetch(sources, begin):
        copies = [
            pltpu.make_async_copy(
                source.at[:, pl.ds(begin, height)], g_ref.at[pl.ds(index * size, size)], sem.at[index]
            )
            for index, source in enumerate(sources)
        ]
        for copy in copies:
            copy.start()
        for copy in copies:
            copy.wait()

    @pl.when(info_ref[1] == 0)
    def _():
        fetch((early0_ref, early1_ref), pl.program_id(0) * height)

    @pl.when(info_ref[1] != 0)
    def _():
        fetch((late0_ref, late1_ref), pl.program_id(0) * height)

    def run():
        def columns(index, begin=0, end=RANK):
            return g_ref[index, begin:end].astype(jnp.float32)

        def project(first_at, second_at, a_ref, b_ref, w_ref, ga, gb, folded):
            for index in range(ga.shape[1] // WIDE):
                ga[0, index * WIDE : (index + 1) * WIDE] = columns(first_at + index).T
            span = w_ref.shape[1]
            rows = pl.ds(pl.multiple_of(info_ref[0] * span, span), span)
            new_first = a_ref[0, rows].astype(jnp.float32) - rate * ga[0, rows]
            for index in range(gb.shape[2] // WIDE):
                lanes = slice(index * WIDE, (index + 1) * WIDE)
                grad = columns(second_at + index)
                gb[0, :, lanes] = grad
                new_second = b_ref[0, :, lanes].astype(jnp.float32) - rate * grad
                product = jnp.dot(new_first, new_second, precision=lax.Precision.HIGHEST)
                folded[0, :, lanes] = (
                    w_ref[0, :, lanes].astype(jnp.float32) + adapter_scale * product
                ).astype(jnp.bfloat16)

        project(0, 2, aq_ref, bq_ref, wq_ref, gaq, gbq, fq)
        project(1, 5, ao_ref, bo_ref, wo_ref, gao, gbo, fo)
        project(6, 11, au_ref, bu_ref, wu_ref, gau, gbu, fu)
        project(7, 15, ad_ref, bd_ref, wd_ref, gad, gbd, fd)
        extra = [columns(index, RANK, RANK + 8)[:1] for index in (0, 6, 1, 7)]
        gain_out[0] = jnp.concatenate(extra[:2], 0)
        bias_out[0] = jnp.concatenate(extra[2:], 0)
        sums = columns(8, RANK, RANK + 8)[:1]
        sums = jnp.concatenate([sums[:, 128 * index : 128 * (index + 1)] for index in range(3)], 0)
        rms_out[0] = jnp.sqrt(sums / counts_ref[...])

    run()


def finish(place, core, rate, early, late, counts, trained, frozen):
    firsts, seconds = trained[0:8:2], trained[1:8:2]
    layers = firsts[0].shape[0]

    def layer_block(value):
        return pl.BlockSpec((1,) + value.shape[1:], lambda step, *_: (step, 0, 0))

    shapes = []
    for first, second in zip(firsts, seconds):
        shapes.append(jax.ShapeDtypeStruct(first.shape, jnp.float32))
        shapes.append(jax.ShapeDtypeStruct(second.shape, jnp.float32))
    shapes += [jax.ShapeDtypeStruct((layers, 2, WIDE), jnp.float32)] * 2
    shapes += [jax.ShapeDtypeStruct(matrix.shape, jnp.bfloat16) for matrix in frozen]
    shapes += [jax.ShapeDtypeStruct((layers, 3, 128), jnp.float32)]
    keep = pl.BlockSpec(memory_space=pl.ANY)
    return pl.pallas_call(
        finish_kernel,
        out_shape=shapes,
        grid_spec=pltpu.PrefetchScalarGridSpec(
            num_scalar_prefetch=1,
            grid=(layers,),
            in_specs=[pl.BlockSpec(memory_space=pltpu.SMEM)]
            + [keep] * 4
            + [pl.BlockSpec((1, 128), lambda step, *_: (0, 0))]
            + [layer_block(value) for value in firsts + seconds + frozen],
            out_specs=[layer_block(shape) for shape in shapes],
            scratch_shapes=[pltpu.VMEM((16, RANK + 8, WIDE), jnp.bfloat16), pltpu.SemaphoreType.DMA((2,))],
        ),
        compiler_params=pltpu.CompilerParams(vmem_limit_bytes=60 << 20),
        cost_estimate=pl.CostEstimate(flops=1 << 29, bytes_accessed=24 << 20, transcendentals=0),
        name="finish",
    )(jnp.stack([place, core]), rate.reshape(1), *early, *late, counts, *firsts, *seconds, *frozen)


def mm(left, right):
    return jnp.dot(left, right, preferred_element_type=jnp.float32)


def mm_nt(left, right):
    return lax.dot_general(left, right, (((1,), (1,)), ((), ())), preferred_element_type=jnp.float32)


def mm_tn(left, right):
    return lax.dot_general(left, right, (((0,), (0,)), ((), ())), preferred_element_type=jnp.float32)


def half(value):
    return value.astype(jnp.bfloat16)


def normalize(value):
    centred = value - jnp.mean(value, axis=-1, keepdims=True)
    scale = lax.rsqrt(jnp.mean(centred * centred, axis=-1, keepdims=True) + norm_eps)
    return centred * scale, scale


def norm_gradient(grad, normal, scale, gain):
    pulled = grad * gain
    inner = pulled - jnp.mean(pulled, axis=-1, keepdims=True)
    return scale * (inner - normal * jnp.mean(pulled * normal, axis=-1, keepdims=True))


def rotary_tables(seq_len):
    half_rot = ROT // 2
    lane = jnp.arange(2 * HEAD_DIM) % HEAD_DIM
    freqs = 10000.0 ** (-((lane % half_rot).astype(jnp.float32) * 2.0 / ROT))
    angles = jnp.arange(seq_len, dtype=jnp.float32)[:, None] * freqs[None, :]
    turning = (lane < ROT)[None, :]
    cosine = jnp.where(turning, jnp.cos(angles), 1.0)
    ahead = jnp.where((lane < half_rot)[None, :], -jnp.sin(angles), 0.0)
    behind = jnp.where(turning & (lane >= half_rot)[None, :], jnp.sin(angles), 0.0)
    return jnp.stack([cosine, ahead, behind])


def tile_table(table, rows, columns):
    return jnp.concatenate([jnp.concatenate([table] * (columns // table.shape[1]), 1)] * rows, 0)


def turn(value, cosine, ahead, behind):
    width = value.shape[1]
    step = ROT // 2
    return value * cosine + pltpu.roll(value, width - step, 1) * ahead + pltpu.roll(value, step, 1) * behind


def turn_back(value, cosine, ahead, behind):
    width = value.shape[1]
    step = ROT // 2
    return value * cosine + pltpu.roll(value * ahead, step, 1) + pltpu.roll(value * behind, width - step, 1)


def stack_heads(pair):
    low = lax.broadcasted_iota(jnp.int32, pair.shape, 1) < HEAD_DIM
    zero = jnp.zeros_like(pair)
    return jnp.concatenate([jnp.where(low, pair, zero), jnp.where(low, zero, pair)], 0)


def merge_heads(stacked):
    rows = stacked.shape[0] // 2
    low = lax.broadcasted_iota(jnp.int32, (rows, stacked.shape[1]), 1) < HEAD_DIM
    return jnp.where(low, stacked[:rows], stacked[rows:])


def pair_softmax(query_stack, key_pair, limit):
    scores = mm_nt(query_stack, key_pair) * HEAD_DIM ** (-0.5)
    seq_len = key_pair.shape[0]
    row = lax.broadcasted_iota(jnp.int32, scores.shape, 0) % seq_len
    column = lax.broadcasted_iota(jnp.int32, scores.shape, 1)
    scores = jnp.where((column <= row) & (column < limit), scores, masked_score)
    grown = jnp.exp(scores - jnp.max(scores, axis=-1, keepdims=True))
    return grown / jnp.sum(grown, axis=-1, keepdims=True)


GROUP = 4 * HEAD_DIM
BLOCK = 512


def attention_forward_kernel(
    facts_ref, x_ref, norm_ref, table_ref, first_ref, wq_ref, wk_ref, wv_ref, bq_ref, bk_ref, bv_ref,
    wo_ref, ao_ref, bo_ref, *refs,
):
    q_out, k_out, v_out, mixed_out, midq_out, mido_out, att_out, a_scr, mid_scr = refs[-9:]
    step = pl.program_id(0)
    seqs = x_ref.shape[0] // table_ref.shape[1]
    seq_len = table_ref.shape[1]

    @pl.when(step == 0)
    def _():
        normal, _ = normalize(x_ref[...])
        a_scr[...] = half(normal * norm_ref[0:1] + norm_ref[2:3])
        midq_out[...] = half(mm(a_scr[...], first_ref[...]))
        att_out[...] = jnp.zeros_like(att_out)
        mid_scr[...] = jnp.zeros_like(mid_scr)

    normed = a_scr[...]
    mid = midq_out[...]
    tables = [tile_table(table_ref[index], seqs, GROUP) for index in range(3)]
    query = mm(normed, wq_ref[...]) + adapter_scale * mm(mid, bq_ref[...])
    q_out[...] = half(turn(query, *tables))
    key = mm(normed, wk_ref[...]) + adapter_scale * mm(mid, bk_ref[...])
    k_out[...] = half(turn(key, *tables))
    v_out[...] = half(mm(normed, wv_ref[...]) + adapter_scale * mm(mid, bv_ref[...]))
    for seq in range(seqs):
        rows = slice(seq * seq_len, (seq + 1) * seq_len)
        for pair in range(GROUP // (2 * HEAD_DIM)):
            lanes = slice(pair * 2 * HEAD_DIM, (pair + 1) * 2 * HEAD_DIM)
            probability = pair_softmax(stack_heads(q_out[rows, lanes]), k_out[rows, lanes], facts_ref[0, seq])
            mixed_out[rows, lanes] = half(merge_heads(mm(half(probability), v_out[rows, lanes])))
    mixed = mixed_out[...]
    att_out[...] += mm(mixed, wo_ref[...])
    mid_scr[...] += mm(mixed, ao_ref[...])

    @pl.when(step == pl.num_programs(0) - 1)
    def _():
        mido_out[...] = half(mid_scr[...])
        att_out[...] += adapter_scale * mm(mido_out[...], bo_ref[...])


def whole(*shape):
    return pl.BlockSpec(shape, lambda step, facts_ref: (0,) * len(shape))


def fixed(height, width, down=0, right=0):
    return pl.BlockSpec((height, width), lambda step, facts_ref: (down, right))


def layer_fixed(layer, height, width, down=0, right=0):
    return pl.BlockSpec((None, height, width), lambda step, facts_ref: (layer, down, right))


def layer_columns(layer, height, width, offset=0):
    return pl.BlockSpec((None, height, width), lambda step, facts_ref: (layer, 0, step + offset))


def layer_rows(layer, height, width, offset=0):
    return pl.BlockSpec((None, height, width), lambda step, facts_ref: (layer, step + offset, 0))


def column_block(height, width, offset=0):
    return pl.BlockSpec((height, width), lambda step, facts_ref: (0, step + offset))


def row_block(height, width, offset=0):
    return pl.BlockSpec((height, width), lambda step, facts_ref: (step + offset, 0))


def kernel_call(kernel, name, steps, in_specs, out_specs, out_shape, scratch, flops, size, exps=0, aliases={}):
    return pl.pallas_call(
        kernel,
        out_shape=out_shape,
        grid_spec=pltpu.PrefetchScalarGridSpec(
            num_scalar_prefetch=1, grid=(steps,), in_specs=in_specs, out_specs=out_specs, scratch_shapes=scratch
        ),
        compiler_params=pltpu.CompilerParams(
            dimension_semantics=("arbitrary",), vmem_limit_bytes=48 << 20
        ),
        input_output_aliases=aliases,
        cost_estimate=pl.CostEstimate(flops=flops, bytes_accessed=size, transcendentals=exps),
        name=name,
    )


def shaped(shape, dtype=jnp.bfloat16):
    return jax.ShapeDtypeStruct(shape, dtype)


def attention_forward(residual, weights, norms, tables, facts, after):
    tokens, width = residual.shape
    groups = width // GROUP
    joint, output = weights[0], weights[1]
    firsts, seconds, _, layer = weights[4:8]
    seq_len = tables.shape[1]
    return kernel_call(
        attention_forward_kernel,
        "attention_forward",
        groups,
        [
            whole(tokens, width),
            whole(4, width),
            whole(3, seq_len, 2 * HEAD_DIM),
            layer_fixed(layer, width, RANK),
            column_block(width, GROUP),
            column_block(width, GROUP, groups),
            column_block(width, GROUP, 2 * groups),
            layer_columns(layer, RANK, GROUP),
            layer_columns(layer, RANK, GROUP, groups),
            layer_columns(layer, RANK, GROUP, 2 * groups),
            row_block(GROUP, width),
            layer_rows(layer, GROUP, RANK, groups),
            layer_fixed(layer, RANK, width, 0, 3),
        ]
        + [pl.BlockSpec(memory_space=pl.ANY)] * len(after),
        [column_block(tokens, GROUP)] * 4 + [whole(tokens, RANK), whole(tokens, RANK), whole(tokens, width)],
        [shaped((tokens, width))] * 4
        + [shaped((tokens, RANK)), shaped((tokens, RANK)), shaped((tokens, width), jnp.float32)],
        [pltpu.VMEM((tokens, width), jnp.bfloat16), pltpu.VMEM((tokens, RANK), jnp.float32)],
        2 * tokens * width * width * 4,
        2 * 5 * width * width + 12 * tokens * width,
    )(
        facts, residual, norms, tables, firsts, joint, joint, joint, seconds, seconds, seconds, output,
        firsts, seconds, *after,
    )


def feed_forward_kernel(
    facts_ref, x_ref, norm_ref, att_ref, first_ref, wu_ref, bu_ref, wd_ref, ad_ref, bd_ref,
    act_out, slope_out, midu_out, midd_out, x_out, sums_out,
    a_scr, mid_scr,
):
    step = pl.program_id(0)

    @pl.when(step == 0)
    def _():
        normal, _ = normalize(x_ref[...])
        a_scr[...] = half(normal * norm_ref[1:2] + norm_ref[3:4])
        midu_out[...] = half(mm(a_scr[...], first_ref[...]))
        x_out[...] = jnp.zeros_like(x_out)
        mid_scr[...] = jnp.zeros_like(mid_scr)

    upper = mm(a_scr[...], wu_ref[...]) + adapter_scale * mm(midu_out[...], bu_ref[...])
    spread = 0.5 + 0.5 * lax.erf(upper * 0.5**0.5)
    density = jnp.exp(-0.5 * upper * upper) * (0.5 / jnp.pi) ** 0.5
    act_out[...] = half(upper * spread)
    slope_out[...] = half(spread + upper * density)
    active = act_out[...]
    x_out[...] += mm(active, wd_ref[...])
    mid_scr[...] += mm(active, ad_ref[...])

    @pl.when(step == pl.num_programs(0) - 1)
    def _():
        midd_out[...] = half(mid_scr[...])
        feed = x_out[...] + adapter_scale * mm(midd_out[...], bd_ref[...])
        attended = att_ref[...]
        residual = x_ref[...]
        x_out[...] = residual + (attended + feed)
        lane = lax.broadcasted_iota(jnp.int32, (1, 128), 1)
        seqs = facts_ref.shape[1]
        seq_len = residual.shape[0] // seqs
        row = lax.broadcasted_iota(jnp.int32, (seq_len, 1), 0)
        parts = []
        for part in (residual, attended, feed):
            squares = jnp.sum(part * part, axis=-1, keepdims=True)
            sums = jnp.zeros((1, 128), jnp.float32)
            for seq in range(seqs):
                valid = jnp.where(row < facts_ref[0, seq], squares[seq * seq_len : (seq + 1) * seq_len], 0.0)
                counted = (lane == facts_ref[1, seq]) | (lane == DOMAINS)
                sums = sums + jnp.where(counted, jnp.sum(valid), 0.0)
            parts.append(sums)
        sums_out[...] = jnp.concatenate(parts + [jnp.zeros((5, 128), jnp.float32)], 0)


def feed_forward(residual, attended, weights, norms, facts):
    tokens, width = residual.shape
    upper, down = weights[2], weights[3]
    firsts, seconds, _, layer = weights[4:8]
    hidden = upper.shape[1]
    return kernel_call(
        feed_forward_kernel,
        "feed_forward",
        hidden // BLOCK,
        [
            whole(tokens, width),
            whole(4, width),
            whole(tokens, width),
            layer_fixed(layer, width, RANK, 2, 0),
            column_block(width, BLOCK),
            layer_columns(layer, RANK, BLOCK, 4 * width // BLOCK),
            row_block(BLOCK, width),
            layer_rows(layer, BLOCK, RANK, 3 * width // BLOCK),
            layer_fixed(layer, RANK, width, 0, 8),
        ],
        [column_block(tokens, BLOCK)] * 2
        + [whole(tokens, RANK), whole(tokens, RANK), whole(tokens, width), whole(8, 128)],
        [shaped((tokens, hidden))] * 2
        + [shaped((tokens, RANK))] * 2
        + [shaped((tokens, width), jnp.float32), shaped((8, 128), jnp.float32)],
        [pltpu.VMEM((tokens, width), jnp.bfloat16), pltpu.VMEM((tokens, RANK), jnp.float32)],
        2 * tokens * width * hidden * 2,
        4 * width * hidden + 4 * tokens * hidden + 12 * tokens * width,
        2 * tokens * hidden,
    )(facts, residual, norms, attended, firsts, upper, seconds, down, firsts, seconds)


def write_extra(block_out, grad, normal, sums):
    width = grad.shape[1]
    row = [jnp.sum(grad * normal, axis=0, keepdims=True), jnp.sum(grad, axis=0, keepdims=True)] + sums
    rest = block_out.shape[1] - sum(part.shape[1] for part in row)
    row = jnp.concatenate(row + [jnp.zeros((1, rest), jnp.float32)], 1)
    block_out[RANK:, :] = half(jnp.concatenate([row, jnp.zeros((7, row.shape[1]), jnp.float32)], 0))


def block_copies(block_out, whole_out, first, sem):
    width = whole_out.shape[2]
    copies = []
    for index in range(block_out.shape[1] // width):
        source = block_out.at[:, pl.ds(index * width, width)]
        copies.append(pltpu.make_async_copy(source, whole_out.at[first + index], sem.at[index]))
        copies[-1].start()
    return copies


def feed_backward_kernel(
    facts_ref, g_ref, x_ref, norm_ref, act_ref, slope_ref, midu_ref, midd_ref, sums_ref, wu_ref, wd_ref, au_ref,
    bu_ref, ad_ref, bd_ref,
    whole_out, gx_out,
    block_out, g_scr, gmd_scr, gmdt_scr, midut_scr, gmu_scr, sem,
):
    step = pl.program_id(0)
    width = x_ref.shape[1]
    hidden = pl.num_programs(0) * BLOCK

    @pl.when(step == 0)
    def _():
        g_scr[...] = half(g_ref[...])
        grad_mid = adapter_scale * mm_nt(g_scr[...], bd_ref[...])
        gmd_scr[...] = half(grad_mid)
        gmdt_scr[...] = half(half(grad_mid).astype(jnp.float32).T)
        midut_scr[...] = half(midu_ref[...].astype(jnp.float32).T)
        gx_out[...] = jnp.zeros_like(gx_out)
        gmu_scr[...] = jnp.zeros_like(gmu_scr)
        middt = half(midd_ref[...].astype(jnp.float32).T)
        block_out[:RANK, pl.ds(width + 2 * hidden, width)] = half(adapter_scale * mm(middt, g_scr[...]))

    grad_act = mm_nt(g_scr[...], wd_ref[...]) + mm_nt(gmd_scr[...], ad_ref[...])
    grad_up = half(half(grad_act).astype(jnp.float32) * slope_ref[...].astype(jnp.float32))
    first_at = pl.multiple_of(width + step * BLOCK, BLOCK)
    second_at = pl.multiple_of(width + hidden + step * BLOCK, BLOCK)
    block_out[:RANK, pl.ds(first_at, BLOCK)] = half(mm(gmdt_scr[...], act_ref[...]))
    block_out[:RANK, pl.ds(second_at, BLOCK)] = half(adapter_scale * mm(midut_scr[...], grad_up))
    gmu_scr[...] += mm_nt(grad_up, bu_ref[...])
    gx_out[...] += mm_nt(grad_up, wu_ref[...])

    @pl.when(step == pl.num_programs(0) - 1)
    def _():
        grad_mid = half(adapter_scale * gmu_scr[...])
        normal, scale = normalize(x_ref[...])
        normed = half(normal * norm_ref[1:2] + norm_ref[3:4])
        block_out[:RANK, :width] = half(mm(half(grad_mid.astype(jnp.float32).T), normed))
        grad = gx_out[...] + mm_nt(grad_mid, au_ref[...])
        write_extra(block_out, grad, normal, [sums_ref[index : index + 1] for index in range(3)])
        gather = block_copies(block_out, whole_out, 6, sem)
        gx_out[...] = g_ref[...] + norm_gradient(grad, normal, scale, norm_ref[1:2])
        for copy in gather:
            copy.wait()


def feed_backward(gradient, residual, weights, norms, kept, facts):
    tokens, width = residual.shape
    upper, down = weights[2], weights[3]
    firsts, seconds, _, layer = weights[4:8]
    active, slope, mid_u, mid_d, sums = kept
    hidden = upper.shape[1]
    return kernel_call(
        feed_backward_kernel,
        "feed_backward",
        hidden // BLOCK,
        [
            whole(tokens, width),
            whole(tokens, width),
            whole(4, width),
            column_block(tokens, BLOCK),
            column_block(tokens, BLOCK),
            whole(tokens, RANK),
            whole(tokens, RANK),
            whole(8, 128),
            column_block(width, BLOCK),
            row_block(BLOCK, width),
            layer_fixed(layer, width, RANK, 2, 0),
            layer_columns(layer, RANK, BLOCK, 4 * width // BLOCK),
            layer_rows(layer, BLOCK, RANK, 3 * width // BLOCK),
            layer_fixed(layer, RANK, width, 0, 8),
        ],
        [pl.BlockSpec(memory_space=pl.ANY), whole(tokens, width)],
        [shaped((16, RANK + 8, width)), shaped((tokens, width), jnp.float32)],
        [
            pltpu.VMEM((RANK + 8, 2 * width + 2 * hidden), jnp.bfloat16),
            pltpu.VMEM((tokens, width), jnp.bfloat16),
            pltpu.VMEM((tokens, RANK), jnp.bfloat16),
            pltpu.VMEM((RANK, tokens), jnp.bfloat16),
            pltpu.VMEM((RANK, tokens), jnp.bfloat16),
            pltpu.VMEM((tokens, RANK), jnp.float32),
            pltpu.SemaphoreType.DMA((10,)),
        ],
        2 * tokens * width * hidden * 2,
        4 * width * hidden + 4 * tokens * hidden + 16 * tokens * width,
    )(
        facts, gradient, residual, norms, active, slope, mid_u, mid_d, sums, upper, down, firsts, seconds,
        firsts, seconds,
    )


def attention_backward_kernel(
    facts_ref, g_ref, gx_ref, x_ref, norm_ref, table_ref, q_ref, k_ref, v_ref, mixed_ref, midq_ref, mido_ref,
    wq_ref, wk_ref, wv_ref, aq_ref, bq_ref, bk_ref, bv_ref, wo_ref, ao_ref, bo_ref, feed_block_ref, *refs,
):
    whole_out, gx_out = refs[-13:-11]
    block_out, g_scr, gmo_scr, gmot_scr, midqt_scr, gmq_scr, acc_scr, gq_scr, gk_scr, gv_scr, sem = refs[-11:]
    step = pl.program_id(0)
    width = x_ref.shape[1]
    seq_len = table_ref.shape[1]
    seqs = x_ref.shape[0] // seq_len
    scale_factor = HEAD_DIM ** (-0.5)

    @pl.when(step == 0)
    def _():
        g_scr[...] = half(g_ref[...])
        grad_mid = half(adapter_scale * mm_nt(g_scr[...], bo_ref[...]))
        gmo_scr[...] = grad_mid
        gmot_scr[...] = half(grad_mid.astype(jnp.float32).T)
        midqt_scr[...] = half(midq_ref[...].astype(jnp.float32).T)
        acc_scr[...] = jnp.zeros_like(acc_scr)
        gmq_scr[...] = jnp.zeros_like(gmq_scr)
        midot = half(mido_ref[...].astype(jnp.float32).T)
        block_out[:RANK, pl.ds(5 * width, width)] = half(adapter_scale * mm(midot, g_scr[...]))

    grad_mixed = half(mm_nt(g_scr[...], wo_ref[...]) + mm_nt(gmo_scr[...], ao_ref[...]))
    first_at = pl.multiple_of(width + step * GROUP, GROUP)
    block_out[:RANK, pl.ds(first_at, GROUP)] = half(mm(gmot_scr[...], mixed_ref[...]))
    for seq in range(seqs):
        rows = slice(seq * seq_len, (seq + 1) * seq_len)
        for pair in range(GROUP // (2 * HEAD_DIM)):
            lanes = slice(pair * 2 * HEAD_DIM, (pair + 1) * 2 * HEAD_DIM)
            query_stack = stack_heads(q_ref[rows, lanes])
            key_pair = k_ref[rows, lanes]
            probability = pair_softmax(query_stack, key_pair, facts_ref[0, seq])
            grad_stack = stack_heads(grad_mixed[rows, lanes])
            grad_prob = mm_nt(grad_stack, v_ref[rows, lanes])
            gv_scr[rows, lanes] = half(mm_tn(half(probability), grad_stack))
            inner = jnp.sum(probability * grad_prob, axis=-1, keepdims=True)
            grad_scores = half(probability * (grad_prob - inner))
            gq_scr[rows, lanes] = merge_heads(mm(grad_scores, key_pair)) * scale_factor
            gk_scr[rows, lanes] = mm_tn(grad_scores, query_stack) * scale_factor
    tables = [tile_table(table_ref[index], seqs, GROUP) for index in range(3)]
    joint = (half(turn_back(gq_scr[...], *tables)), half(turn_back(gk_scr[...], *tables)), gv_scr[...])
    mid = midqt_scr[...]
    for index, (grad, w_ref, b_ref) in enumerate(zip(joint, (wq_ref, wk_ref, wv_ref), (bq_ref, bk_ref, bv_ref))):
        second_at = pl.multiple_of((2 + index) * width + step * GROUP, GROUP)
        block_out[:RANK, pl.ds(second_at, GROUP)] = half(adapter_scale * mm(mid, grad))
        gmq_scr[...] += mm_nt(grad, b_ref[...])
        acc_scr[...] += mm_nt(grad, w_ref[...])

    @pl.when(step == pl.num_programs(0) - 1)
    def _():
        grad_mid = half(adapter_scale * gmq_scr[...])
        normal, scale = normalize(x_ref[...])
        normed = half(normal * norm_ref[0:1] + norm_ref[2:3])
        block_out[:RANK, :width] = half(mm(half(grad_mid.astype(jnp.float32).T), normed))
        grad = acc_scr[...] + mm_nt(grad_mid, aq_ref[...])
        write_extra(block_out, grad, normal, [])
        gather = block_copies(block_out, whole_out, 0, sem)
        gx_out[...] = gx_ref[...] + norm_gradient(grad, normal, scale, norm_ref[0:1])
        for copy in gather:
            copy.wait()


def attention_backward(gradient, grad_feed, feed_block, residual, weights, norms, tables, kept, facts, after):
    tokens, width = residual.shape
    groups = width // GROUP
    joint, output = weights[0], weights[1]
    firsts, seconds, _, layer = weights[4:8]
    queries, keys, values, mixed, mid_q, mid_o = kept
    seq_len = tables.shape[1]
    block = column_block(tokens, GROUP)
    return kernel_call(
        attention_backward_kernel,
        "attention_backward",
        groups,
        [
            whole(tokens, width),
            whole(tokens, width),
            whole(tokens, width),
            whole(4, width),
            whole(3, seq_len, 2 * HEAD_DIM),
            block,
            block,
            block,
            block,
            whole(tokens, RANK),
            whole(tokens, RANK),
            column_block(width, GROUP),
            column_block(width, GROUP, groups),
            column_block(width, GROUP, 2 * groups),
            layer_fixed(layer, width, RANK),
            layer_columns(layer, RANK, GROUP),
            layer_columns(layer, RANK, GROUP, groups),
            layer_columns(layer, RANK, GROUP, 2 * groups),
            row_block(GROUP, width),
            layer_rows(layer, GROUP, RANK, groups),
            layer_fixed(layer, RANK, width, 0, 3),
            pl.BlockSpec(memory_space=pl.ANY),
        ]
        + [pl.BlockSpec(memory_space=pl.ANY)] * len(after),
        [pl.BlockSpec(memory_space=pl.ANY), whole(tokens, width)],
        [shaped((16, RANK + 8, width)), shaped((tokens, width), jnp.float32)],
        [
            pltpu.VMEM((RANK + 8, 6 * width), jnp.bfloat16),
            pltpu.VMEM((tokens, width), jnp.bfloat16),
            pltpu.VMEM((tokens, RANK), jnp.bfloat16),
            pltpu.VMEM((RANK, tokens), jnp.bfloat16),
            pltpu.VMEM((RANK, tokens), jnp.bfloat16),
            pltpu.VMEM((tokens, RANK), jnp.float32),
            pltpu.VMEM((tokens, width), jnp.float32),
            pltpu.VMEM((tokens, GROUP), jnp.float32),
            pltpu.VMEM((tokens, GROUP), jnp.float32),
            pltpu.VMEM((tokens, GROUP), jnp.bfloat16),
            pltpu.SemaphoreType.DMA((6,)),
        ],
        2 * tokens * width * width * 4,
        2 * 5 * width * width + 24 * tokens * width,
        aliases={22: 0},
    )(
        facts, gradient, grad_feed, residual, norms, tables, queries, keys, values, mixed, mid_q, mid_o, joint,
        joint, joint, firsts, seconds, seconds, seconds, output, firsts, seconds, feed_block, *after,
    )


def layer_forward(residual, weights, tables, facts, after=()):
    norms = weights[6]
    *kept_attention, attended = attention_forward(residual, weights, norms, tables, facts, after)
    *kept_feed, output, sums = feed_forward(residual, attended, weights, norms, facts)
    return output, (residual, kept_attention, kept_feed + [sums])


def layer_backward(gradient, kept, weights, tables, facts, after=()):
    residual, kept_attention, kept_feed = kept
    norms = weights[6]
    feed_block, grad_feed = feed_backward(gradient, residual, weights, norms, kept_feed, facts)
    block, grad_input = attention_backward(
        gradient, grad_feed, feed_block, residual, weights, norms, tables, kept_attention, facts, after
    )
    return grad_input, block


def gather_plan(gathers, turns):
    if (gathers, turns) == (4, 3):
        return [[0, 2], [0, 2], [0, 1], [2, 1], [1, 3], [3], [3]]
    order = [0, 2, 1, 3]
    return [[order[step // turns]] for step in range(gathers * turns)]


def shards(
    inputs,
    cotangent,
    domain,
    lengths,
    steps_since_reset,
    frozen_query_weight,
    frozen_output_weight,
    frozen_up_weight,
    frozen_down_weight,
    query_adapter_first,
    query_adapter_second,
    output_adapter_first,
    output_adapter_second,
    up_adapter_first,
    up_adapter_second,
    down_adapter_first,
    down_adapter_second,
    layer_norm_gain,
    layer_norm_bias,
):
    core = lax.axis_index("section")
    place = lax.axis_index("dp")
    count = lax.axis_size("dp")
    middle = count // 2
    stage = place // middle
    low = place % middle
    home = core == stage
    masks = [1 << bit for bit in range(middle.bit_length() - 1)]
    frozen = (frozen_query_weight, frozen_output_weight, frozen_up_weight, frozen_down_weight)
    trained = (
        query_adapter_first,
        query_adapter_second,
        output_adapter_first,
        output_adapter_second,
        up_adapter_first,
        up_adapter_second,
        down_adapter_first,
        down_adapter_second,
    )
    local_layers = frozen_query_weight.shape[0]
    rows_dev, seq_len, model_width = inputs.shape
    tokens = rows_dev * seq_len

    places = [(index // middle, index) for index in range(count)]
    to_sibling = [(here * count + index, (1 - here) * count + index) for here, index in places]
    to_cross = [((1 - here) * count + index, here * count + (index ^ middle)) for here, index in places]
    sibling, cross = [partial(both_axes, pairs=pairs) for pairs in (to_sibling, to_cross)]

    same, other = pack_halves(core, frozen)
    swapped_units = flip_core(other)
    own = jnp.where(home, same, swapped_units)
    leaving = jnp.where(home, swapped_units, same)
    partner = [flip_place(leaving[0], middle)]
    for layer in range(1, local_layers):
        partner.append(flip_place(tie(leaving[layer], partner[-1]), middle))
    gathers = []
    for layer in range(local_layers):
        gathers.append(Gather(layer, 0, own[layer], masks))
        gathers.append(Gather(layer, 1, partner[layer], masks))
    plan = gather_plan(len(gathers), len(masks)) + [[]]
    dense = [None] * local_layers
    facts = jnp.stack([lengths, domain])
    norms = jnp.concatenate([layer_norm_gain, layer_norm_bias], 1)
    facts = jnp.where(home, facts, cross(facts))
    norms = jnp.where(home, norms, sibling(norms))
    visiting = jnp.where(stage == 0, cotangent, inputs)
    tables = rotary_tables(seq_len)
    ended, fresh, started, waiting = (), [], set(), []
    bases = [jnp.where(stage == which, 0, middle) for which in range(2)]
    for number, active in enumerate(plan):
        if number == len(plan) - 1:
            start = jnp.where(home, inputs, visiting).astype(jnp.float32).reshape(tokens, model_width)
            while waiting and min(layer for layer, _ in waiting[0][1]) == 0:
                assemble(*waiting.pop(0), count, dense)
            first_weights = tuple(dense[0]) + (packed[0], packed[1], norms[0], 0)
            boundary, _ = layer_forward(start, first_weights, tables, facts)
            ended = ended + (boundary,)
        for index in active:
            if index not in started:
                started.add(index)
                gather = gathers[index]
                fresh = fresh + [(gather.block, part, 1, gather, part, [0]) for part in range(3)]
        extra = []
        if number in (1, 2):
            extra.append((packed[number - 1], sibling))
        if number == 4:
            extra.append((visiting, cross))
        moving = fresh if number >= 2 else []
        there, came, collected, swapped, results = gather_step(
            [gathers[index] for index in active], masks, moving, extra, ended
        )
        fresh = came if moving else fresh + came
        if number == 0:
            packed = list(pack_adapters(trained, swapped_units))
        if number in (1, 2):
            packed[number - 1] = jnp.where(home, packed[number - 1], results[0])
        if number == 4:
            visiting = results[0]
        marks = [assemble(*waiting.pop(0), count, dense)] if waiting and number < len(plan) - 1 else []
        ended = tuple(there) + tuple(results) + tuple(marks)
        if number == 3:
            ended = ended + tuple(packed)
        if moving:
            ended = ended + (swapped,)
            layout = [(gather.layer, part) for _, _, size, gather, part, _ in moving for _ in range(size)]
            places_of = [
                (known ^ low) + bases[gather.which] for _, _, _, gather, _, found in moving for known in found
            ]
            info = jnp.stack([core] + places_of)
            waiting.append((info, layout, collected, swapped))
    for item in waiting:
        assemble(*item, count, dense)
    weights = [tuple(dense[layer]) + (packed[0], packed[1], norms[layer], layer) for layer in range(local_layers)]
    valid = jnp.arange(seq_len)[None, :] < facts[0][:, None]
    end_grad = jnp.where(home, cotangent, visiting).astype(jnp.float32)
    end_grad = jnp.where(stage == 1, end_grad * valid[..., None].astype(jnp.float32), 0.0)
    end_grad = end_grad.reshape(tokens, model_width)
    def stage_forward(residual, after):
        kept = []
        for layer in range(local_layers):
            residual, kept_state = layer_forward(residual, weights[layer], tables, facts, after if layer == 0 else ())
            kept.append(kept_state)
        return residual, kept

    for layer in range(1, local_layers):
        boundary, _ = layer_forward(boundary, weights[layer], tables, facts)
    boundary = boundary.astype(jnp.bfloat16)
    forward_pairs = [(index, index + middle) for index in range(middle)]
    received = lax.ppermute(boundary, "dp", forward_pairs)
    lane = jnp.arange(128)
    counted = (domain[:, None] == lane[None, :]) | (lane == DOMAINS)[None, :]
    counts = jnp.sum(jnp.where(counted, lengths.astype(jnp.float32)[:, None], 0.0), axis=0, keepdims=True)
    for mask in masks + [middle]:
        counts = counts + flip_place(counts, mask)
    counts = jnp.maximum(counts, 1.0) * model_width
    entry = jnp.where(stage == 0, start, received.astype(jnp.float32))
    final, kept = stage_forward(entry, (counts,))
    final = final.astype(jnp.bfloat16)

    gradient = end_grad
    late = [None] * local_layers
    for layer in reversed(range(local_layers)):
        gradient, late[layer] = layer_backward(gradient, kept[layer], weights[layer], tables, facts)
    sent = gradient.astype(jnp.bfloat16)
    came_back = lax.ppermute(sent, "dp", [(after, before) for before, after in forward_pairs])
    late_halves = tie([swap_halves(block, 1, core, count) for block in late], came_back)
    late_piece = sum_halves(late_halves, count)

    gradient = jnp.where(stage == 0, came_back.astype(jnp.float32), 0.0)
    out_pairs = [(count + index + middle, index + middle) for index in range(middle)]
    out_pairs = out_pairs + [(index + middle, count + index) for index in range(middle)]
    visiting = both_axes(jnp.where(core == 0, final, received), out_pairs)
    section_out = jnp.where(home, jnp.where(stage == 0, boundary, final), visiting)
    section_out = section_out.reshape(1, rows_dev, seq_len, model_width)
    pieces = [None] * local_layers
    after = ()
    for layer in reversed(range(local_layers)):
        gradient, block = layer_backward(gradient, kept[layer], weights[layer], tables, facts, after)
        halves = swap_halves(block, 0, core, count)
        if layer == local_layers - 1:
            pieces[layer] = sum_halves([tie(halves, late_piece)], count)
            late_piece = cross_section(late_piece, 1, stage, count)
            after = (late_piece,)
        else:
            if layer == 0:
                late_whole = spread_section(tie(late_piece, pieces[local_layers - 1]), 1, count)
                halves = tie(halves, late_whole[1])
            pieces[layer] = sum_halves([halves], count)
            after = ()
    early_piece = cross_section(jnp.concatenate(pieces, 0), 0, stage, count)
    early_whole = spread_section(early_piece, 0, count)

    grad_pairs = [(index, count + index) for index in range(middle)]
    grad_pairs = grad_pairs + [(count + index, index + middle) for index in range(middle)]
    visiting = both_axes(jnp.where(core == 0, came_back, gradient.astype(jnp.bfloat16)), grad_pairs)
    section_grad = jnp.where(
        home, jnp.where(stage == 0, gradient, sent.astype(jnp.float32)), visiting.astype(jnp.float32)
    )
    section_grad = section_grad.reshape(1, rows_dev, seq_len, model_width)

    rate = peak_rate * (steps_since_reset[0].astype(jnp.float32) + 1.0) / WARM
    outputs = finish(place, core, rate, early_whole, late_whole, counts, trained, frozen)
    *outputs, rms = outputs
    return (section_out, section_grad, *outputs, rms[:, :, : DOMAINS + 1])


def solution(mesh):
    across = P("dp", None, None)
    copied = P("section", None, None)
    split = P("section", "dp", None)
    wide = P("section", "dp", None, None)
    return jax.shard_map(
        shards,
        mesh=mesh,
        in_specs=(across, across, P("dp"), P("dp"), P()) + (split,) * 4 + (copied,) * 10,
        out_specs=(wide, wide) + (copied,) * 10 + (split,) * 4 + (copied,),
        check_vma=False,
    )
```

```python
from functools import partial

import jax
import jax.numpy as jnp
from jax import lax
from jax.experimental import pallas as pl
from jax.experimental.pallas import tpu as pltpu
from jax.sharding import PartitionSpec as P

HEADS = 16
HEAD_DIM = 64
ROT = 16
DOMAINS = 16
WARM = 50
RANK = 128
WIDE = 1024
UNITS = 12
HALF_UNITS = 6

adapter_scale = 0.5
norm_eps = 1e-05
peak_rate = 0.0002
masked_score = -1e30


def both_axes(value, pairs):
    return lax.ppermute(value, ("section", "dp"), pairs)


def tie(value, *others):
    return lax.optimization_barrier((value, others))[0]


def flip_place(value, mask):
    count = lax.axis_size("dp")
    return lax.ppermute(value, "dp", [(place, place ^ mask) for place in range(count)])


def flip_core(value):
    return lax.ppermute(value, "section", [(0, 1), (1, 0)])


def pack_kernel(info_ref, query_ref, output_ref, upper_ref, down_ref, keep_ref, send_ref):
    rows = output_ref.shape[1]

    def write(first, second):
        for layer in range(output_ref.shape[0]):
            first[layer, 0] = query_ref[layer, :, :WIDE]
            first[layer, 1] = query_ref[layer, :, WIDE : 2 * WIDE]
            first[layer, 2] = query_ref[layer, :, 2 * WIDE :]
            first[layer, 3] = output_ref[layer]
            first[layer, 4] = upper_ref[layer, :, :WIDE]
            first[layer, 5] = upper_ref[layer, :, WIDE : 2 * WIDE]
            second[layer, 0] = upper_ref[layer, :, 2 * WIDE : 3 * WIDE]
            second[layer, 1] = upper_ref[layer, :, 3 * WIDE :]
            for index in range(4):
                second[layer, 2 + index] = down_ref[layer, index * rows : (index + 1) * rows]

    @pl.when(info_ref[0] == 0)
    def _():
        write(keep_ref, send_ref)

    @pl.when(info_ref[0] != 0)
    def _():
        write(send_ref, keep_ref)


def pack_halves(core, frozen):
    layers, rows = frozen[1].shape[:2]
    shape = jax.ShapeDtypeStruct((layers, HALF_UNITS, rows, WIDE), jnp.bfloat16)
    vmem = pl.BlockSpec(memory_space=pltpu.VMEM)
    return pl.pallas_call(
        pack_kernel,
        out_shape=[shape, shape],
        in_specs=[pl.BlockSpec(memory_space=pltpu.SMEM)] + [vmem] * 4,
        out_specs=[vmem, vmem],
        compiler_params=pltpu.CompilerParams(vmem_limit_bytes=32 << 20),
        cost_estimate=pl.CostEstimate(
            flops=0, bytes_accessed=8 * HALF_UNITS * layers * rows * WIDE, transcendentals=0
        ),
        name="pack",
    )(core.reshape(1), *frozen)


def pack_adapters_kernel(*refs):
    sources, (first_out, second_out) = refs[:8], refs[-2:]
    at = 0
    for source in sources[0::2]:
        first_out[:, at : at + source.shape[1]] = source[...]
        at = at + source.shape[1]
    at = 0
    for source in sources[1::2]:
        second_out[:, :, at : at + source.shape[2]] = source[...]
        at = at + source.shape[2]


def pack_adapters(trained, *after):
    layers = trained[0].shape[0]
    height = sum(factor.shape[1] for factor in trained[0::2])
    width = sum(factor.shape[2] for factor in trained[1::2])
    shapes = [
        jax.ShapeDtypeStruct((layers, height, RANK), jnp.bfloat16),
        jax.ShapeDtypeStruct((layers, RANK, width), jnp.bfloat16),
    ]

    def layer_block(value):
        return pl.BlockSpec((1,) + value.shape[1:], lambda step: (step, 0, 0))

    return pl.pallas_call(
        pack_adapters_kernel,
        out_shape=shapes,
        grid=(layers,),
        in_specs=[layer_block(factor) for factor in trained] + [pl.BlockSpec(memory_space=pl.ANY)] * len(after),
        out_specs=[layer_block(shape) for shape in shapes],
        compiler_params=pltpu.CompilerParams(vmem_limit_bytes=30 << 20),
        cost_estimate=pl.CostEstimate(flops=0, bytes_accessed=4 * RANK * layers * (height + width), transcendentals=0),
        name="pack_adapters",
    )(*trained, *after)


def rotations(masks):
    return [[masks[(start + index) % len(masks)] for index in range(len(masks))] for start in range(3)]


def assemble_kernel(layout, info_ref, mine, theirs, *refs):
    count = len({layer for layer, _ in layout})
    outs, token_out, sem = refs[-4 * count - 2 : -2], refs[-2], refs[-1]
    token_out[...] = jnp.zeros_like(token_out)
    first_layer = min(layer for layer, _ in layout)
    rows = mine.shape[2]

    def targets(half_index, layer, part, place):
        query_out, output_out, upper_out, down_out = outs[4 * (layer - first_layer) : 4 * (layer - first_layer) + 4]
        at = pl.multiple_of(place * rows, rows)
        down_at = pl.multiple_of(place * 4 * rows, rows)

        def columns(out, index):
            return out.at[pl.ds(at, rows), pl.ds(index * WIDE, WIDE)]

        def down(index):
            return down_out.at[pl.ds(down_at + index * rows, rows)]

        return [
            [(columns(query_out, 0), columns(query_out, 1)), (columns(query_out, 2), columns(output_out, 0)),
             (columns(upper_out, 0), columns(upper_out, 1))],
            [(columns(upper_out, 2), columns(upper_out, 3)), (down(0), down(1)), (down(2), down(3))],
        ][half_index][part]

    def run(first, second):
        copies = []
        for block, (layer, part) in enumerate(layout):
            for half_index, source in enumerate((first, second)):
                for unit, target in enumerate(targets(half_index, layer, part, info_ref[1 + block])):
                    where = sem.at[block, half_index * 2 + unit]
                    copies.append(pltpu.make_async_copy(source.at[block, unit], target, where))
                    copies[-1].start()
        for copy in copies:
            copy.wait()

    @pl.when(info_ref[0] == 0)
    def _():
        run(mine, theirs)

    @pl.when(info_ref[0] != 0)
    def _():
        run(theirs, mine)


def assemble(info, layout, mine, theirs, count, into):
    rows = mine.shape[2]
    total = rows * count
    layers = sorted({layer for layer, _ in layout})
    shapes = [(total, 3 * WIDE), (total, WIDE), (total, 4 * WIDE), (4 * total, WIDE)] * len(layers)
    extra = [matrix for layer in layers for matrix in (into[layer] or ())]
    anywhere = pl.BlockSpec(memory_space=pltpu.HBM)
    aliases, index = {}, 3
    for position, layer in enumerate(layers):
        if into[layer]:
            for matrix in range(4):
                aliases[index] = 4 * position + matrix
                index = index + 1
    made = pl.pallas_call(
        partial(assemble_kernel, tuple(layout)),
        out_shape=[jax.ShapeDtypeStruct(shape, jnp.bfloat16) for shape in shapes]
        + [jax.ShapeDtypeStruct((8, 128), jnp.float32)],
        in_specs=[pl.BlockSpec(memory_space=pltpu.SMEM)]
        + [pl.BlockSpec(memory_space=pltpu.VMEM)] * 2
        + [anywhere] * len(extra),
        out_specs=[anywhere] * len(shapes) + [pl.BlockSpec(memory_space=pltpu.VMEM)],
        scratch_shapes=[pltpu.SemaphoreType.DMA((len(layout), 4))],
        input_output_aliases=aliases,
        compiler_params=pltpu.CompilerParams(vmem_limit_bytes=60 << 20),
        cost_estimate=pl.CostEstimate(flops=0, bytes_accessed=12 * mine.size, transcendentals=0),
        name="assemble",
    )(info, mine, theirs, *extra)
    for position, layer in enumerate(layers):
        into[layer] = made[4 * position : 4 * position + 4]
    return made[-1]


def copy_kernel(plans, *refs):
    inputs, outs = refs[: -len(plans)], refs[-len(plans) :]
    for plan, out in zip(plans, outs):
        at = 0
        for source, begin, size in plan:
            out[at : at + size] = inputs[source][begin : begin + size]
            at = at + size


def copy_blocks(arrays, plans, after):
    tail = arrays[0].shape[1:]
    vmem = pl.BlockSpec(memory_space=pltpu.VMEM)
    shapes = [jax.ShapeDtypeStruct((sum(size for _, _, size in plan),) + tail, jnp.bfloat16) for plan in plans]
    moved = 4 * sum(shape.size for shape in shapes)
    return pl.pallas_call(
        partial(copy_kernel, tuple(tuple(plan) for plan in plans)),
        out_shape=shapes,
        in_specs=[vmem] * len(arrays) + [pl.BlockSpec(memory_space=pl.ANY)] * len(after),
        out_specs=[vmem] * len(shapes),
        compiler_params=pltpu.CompilerParams(vmem_limit_bytes=40 << 20),
        cost_estimate=pl.CostEstimate(flops=0, bytes_accessed=moved, transcendentals=0),
        name="collect",
    )(*arrays, *after)


class Gather:
    def __init__(self, layer, which, block, masks):
        self.layer, self.which = layer, which
        block = block.reshape((3, 2) + block.shape[1:])
        self.block = block
        self.held = [[(block, part, 1)] for part in range(3)]
        self.found = [[0], [0], [0]]
        self.turns = rotations(masks)
        self.step = 0


class Store:
    def __init__(self):
        self.arrays = []

    def index(self, array):
        for position, known in enumerate(self.arrays):
            if known is array:
                return position
        self.arrays.append(array)
        return len(self.arrays) - 1


def gather_step(active, masks, fresh, extra, after):
    store = Store()
    plans, lists = [], []
    for mask in masks:
        entries = [
            (gather, part) for gather in active for part in range(3) if gather.turns[part][gather.step] == mask
        ]
        if entries:
            plans.append(
                [
                    (store.index(array), begin, size)
                    for gather, part in entries
                    for array, begin, size in gather.held[part]
                ]
            )
            lists.append((mask, entries))
    if fresh:
        plans.append([(store.index(array), begin, size) for array, begin, size, _, _, _ in fresh])
    after = [value for value in after if all(value is not known for known in store.arrays)]
    values = list(copy_blocks(store.arrays, plans, after)) + [value for value, _ in extra]
    there = []
    for value, (mask, _) in zip(values, lists):
        there.append(flip_place(value, mask))
    collected = values[len(lists)] if fresh else None
    swapped = flip_core(collected) if fresh else None
    results = [send(value) for value, (_, send) in zip(values[len(plans) :], extra)]
    came = []
    for (mask, entries), value in zip(lists, there):
        begin = 0
        for gather, part in entries:
            size = sum(amount for _, _, amount in gather.held[part])
            known = [place ^ gather.turns[part][gather.step] for place in gather.found[part]]
            gather.held[part] = gather.held[part] + [(value, begin, size)]
            gather.found[part] = gather.found[part] + known
            came.append((value, begin, size, gather, part, known))
            begin = begin + size
    for gather in active:
        gather.step = gather.step + 1
    return there, came, collected, swapped, results


def pieces_by_place(block, pieces):
    if pieces == block.shape[0]:
        return block
    split = pieces // block.shape[0]
    columns = block.shape[2] // split
    block = block.reshape(block.shape[0], block.shape[1], split, columns).transpose(0, 2, 1, 3)
    return block.reshape(pieces, block.shape[2], columns)


def places_to_blocks(pieces, blocks):
    if pieces.shape[0] == blocks:
        return pieces
    split = pieces.shape[0] // blocks
    rows, columns = pieces.shape[1:]
    return pieces.reshape(blocks, split, rows, columns).transpose(0, 2, 1, 3).reshape(blocks, rows, split * columns)


def exchange(value, count):
    middle = count // 2
    groups = [[half_index * middle + index for index in range(middle)] for half_index in range(2)]
    return lax.all_to_all(value, "dp", 0, 0, axis_index_groups=groups)


def swap_halves(block, section, core, count):
    middle = count // 2
    inside = [place for place in range(count) if place // middle == section]
    swap = [(here * count + place, (1 - here) * count + place) for here in range(2) for place in inside]
    size = block.shape[0] // 2
    there = both_axes(lax.dynamic_slice_in_dim(block, (1 - core) * size, size, 0), swap)
    here = lax.dynamic_slice_in_dim(block, core * size, size, 0)
    return (here.astype(jnp.float32) + there.astype(jnp.float32)).astype(jnp.bfloat16)


def sum_halves(halves, count):
    pieces = [pieces_by_place(part, count // 2) for part in halves]
    pieces = pieces[0] if len(pieces) == 1 else jnp.concatenate(pieces, 1)
    return jnp.sum(exchange(pieces, count).astype(jnp.float32), axis=0).astype(jnp.bfloat16)


def scatter_section(blocks, section, core, count):
    return sum_halves([swap_halves(block, section, core, count) for block in blocks], count)


def cross_section(piece, section, stage, count):
    middle = count // 2
    across = [(place, place ^ middle) for place in range(count) if place // middle == section]
    return jnp.where(stage == section, piece, lax.ppermute(piece, "dp", across))


def spread_section(piece, section, count):
    middle = count // 2
    spread = exchange(jnp.broadcast_to(piece[None], (middle,) + piece.shape), count)
    here = places_to_blocks(spread, 8)
    there = lax.ppermute(here, "section", [(1 - section, section)])
    return (here, there) if section == 0 else (there, here)


def finish_kernel(
    info_ref, rate_ref, early0_ref, early1_ref, late0_ref, late1_ref, counts_ref,
    aq_ref, ao_ref, au_ref, ad_ref, bq_ref, bo_ref, bu_ref, bd_ref, wq_ref, wo_ref, wu_ref, wd_ref, *refs,
):
    gaq, gbq, gao, gbo, gau, gbu, gad, gbd, gain_out, bias_out, fq, fo, fu, fd, rms_out, g_ref, sem = refs[-17:]
    rate = rate_ref[0]
    size, height = early0_ref.shape[0], g_ref.shape[1]

    def fetch(sources, begin):
        copies = [
            pltpu.make_async_copy(
                source.at[:, pl.ds(begin, height)], g_ref.at[pl.ds(index * size, size)], sem.at[index]
            )
            for index, source in enumerate(sources)
        ]
        for copy in copies:
            copy.start()
        for copy in copies:
            copy.wait()

    @pl.when(info_ref[1] == 0)
    def _():
        fetch((early0_ref, early1_ref), pl.program_id(0) * height)

    @pl.when(info_ref[1] != 0)
    def _():
        fetch((late0_ref, late1_ref), pl.program_id(0) * height)

    def run():
        def columns(index, begin=0, end=RANK):
            return g_ref[index, begin:end].astype(jnp.float32)

        def project(first_at, second_at, a_ref, b_ref, w_ref, ga, gb, folded):
            for index in range(ga.shape[1] // WIDE):
                ga[0, index * WIDE : (index + 1) * WIDE] = columns(first_at + index).T
            span = w_ref.shape[1]
            rows = pl.ds(pl.multiple_of(info_ref[0] * span, span), span)
            new_first = a_ref[0, rows].astype(jnp.float32) - rate * ga[0, rows]
            for index in range(gb.shape[2] // WIDE):
                lanes = slice(index * WIDE, (index + 1) * WIDE)
                grad = columns(second_at + index)
                gb[0, :, lanes] = grad
                new_second = b_ref[0, :, lanes].astype(jnp.float32) - rate * grad
                product = jnp.dot(new_first, new_second, precision=lax.Precision.HIGHEST)
                folded[0, :, lanes] = (
                    w_ref[0, :, lanes].astype(jnp.float32) + adapter_scale * product
                ).astype(jnp.bfloat16)

        project(0, 2, aq_ref, bq_ref, wq_ref, gaq, gbq, fq)
        project(1, 5, ao_ref, bo_ref, wo_ref, gao, gbo, fo)
        project(6, 11, au_ref, bu_ref, wu_ref, gau, gbu, fu)
        project(7, 15, ad_ref, bd_ref, wd_ref, gad, gbd, fd)
        extra = [columns(index, RANK, RANK + 8)[:1] for index in (0, 6, 1, 7)]
        gain_out[0] = jnp.concatenate(extra[:2], 0)
        bias_out[0] = jnp.concatenate(extra[2:], 0)
        sums = columns(8, RANK, RANK + 8)[:1]
        sums = jnp.concatenate([sums[:, 128 * index : 128 * (index + 1)] for index in range(3)], 0)
        rms_out[0] = jnp.sqrt(sums / counts_ref[...])

    run()


def finish(place, core, rate, early, late, counts, trained, frozen):
    firsts, seconds = trained[0:8:2], trained[1:8:2]
    layers = firsts[0].shape[0]

    def layer_block(value):
        return pl.BlockSpec((1,) + value.shape[1:], lambda step, *_: (step, 0, 0))

    shapes = []
    for first, second in zip(firsts, seconds):
        shapes.append(jax.ShapeDtypeStruct(first.shape, jnp.float32))
        shapes.append(jax.ShapeDtypeStruct(second.shape, jnp.float32))
    shapes += [jax.ShapeDtypeStruct((layers, 2, WIDE), jnp.float32)] * 2
    shapes += [jax.ShapeDtypeStruct(matrix.shape, jnp.bfloat16) for matrix in frozen]
    shapes += [jax.ShapeDtypeStruct((layers, 3, 128), jnp.float32)]
    keep = pl.BlockSpec(memory_space=pl.ANY)
    return pl.pallas_call(
        finish_kernel,
        out_shape=shapes,
        grid_spec=pltpu.PrefetchScalarGridSpec(
            num_scalar_prefetch=1,
            grid=(layers,),
            in_specs=[pl.BlockSpec(memory_space=pltpu.SMEM)]
            + [keep] * 4
            + [pl.BlockSpec((1, 128), lambda step, *_: (0, 0))]
            + [layer_block(value) for value in firsts + seconds + frozen],
            out_specs=[layer_block(shape) for shape in shapes],
            scratch_shapes=[pltpu.VMEM((16, RANK + 8, WIDE), jnp.bfloat16), pltpu.SemaphoreType.DMA((2,))],
        ),
        compiler_params=pltpu.CompilerParams(vmem_limit_bytes=60 << 20),
        cost_estimate=pl.CostEstimate(flops=1 << 29, bytes_accessed=24 << 20, transcendentals=0),
        name="finish",
    )(jnp.stack([place, core]), rate.reshape(1), *early, *late, counts, *firsts, *seconds, *frozen)


def mm(left, right):
    return jnp.dot(left, right, preferred_element_type=jnp.float32)


def mm_nt(left, right):
    return lax.dot_general(left, right, (((1,), (1,)), ((), ())), preferred_element_type=jnp.float32)


def mm_tn(left, right):
    return lax.dot_general(left, right, (((0,), (0,)), ((), ())), preferred_element_type=jnp.float32)


def half(value):
    return value.astype(jnp.bfloat16)


def normalize(value):
    centred = value - jnp.mean(value, axis=-1, keepdims=True)
    scale = lax.rsqrt(jnp.mean(centred * centred, axis=-1, keepdims=True) + norm_eps)
    return centred * scale, scale


def norm_gradient(grad, normal, scale, gain):
    pulled = grad * gain
    inner = pulled - jnp.mean(pulled, axis=-1, keepdims=True)
    return scale * (inner - normal * jnp.mean(pulled * normal, axis=-1, keepdims=True))


def rotary_tables(seq_len):
    half_rot = ROT // 2
    lane = jnp.arange(2 * HEAD_DIM) % HEAD_DIM
    freqs = 10000.0 ** (-((lane % half_rot).astype(jnp.float32) * 2.0 / ROT))
    angles = jnp.arange(seq_len, dtype=jnp.float32)[:, None] * freqs[None, :]
    turning = (lane < ROT)[None, :]
    cosine = jnp.where(turning, jnp.cos(angles), 1.0)
    ahead = jnp.where((lane < half_rot)[None, :], -jnp.sin(angles), 0.0)
    behind = jnp.where(turning & (lane >= half_rot)[None, :], jnp.sin(angles), 0.0)
    return jnp.stack([cosine, ahead, behind])


def tile_table(table, rows, columns):
    return jnp.concatenate([jnp.concatenate([table] * (columns // table.shape[1]), 1)] * rows, 0)


def turn(value, cosine, ahead, behind):
    width = value.shape[1]
    step = ROT // 2
    return value * cosine + pltpu.roll(value, width - step, 1) * ahead + pltpu.roll(value, step, 1) * behind


def turn_back(value, cosine, ahead, behind):
    width = value.shape[1]
    step = ROT // 2
    return value * cosine + pltpu.roll(value * ahead, step, 1) + pltpu.roll(value * behind, width - step, 1)


def stack_heads(pair):
    low = lax.broadcasted_iota(jnp.int32, pair.shape, 1) < HEAD_DIM
    zero = jnp.zeros_like(pair)
    return jnp.concatenate([jnp.where(low, pair, zero), jnp.where(low, zero, pair)], 0)


def merge_heads(stacked):
    rows = stacked.shape[0] // 2
    low = lax.broadcasted_iota(jnp.int32, (rows, stacked.shape[1]), 1) < HEAD_DIM
    return jnp.where(low, stacked[:rows], stacked[rows:])


def pair_mask(seq_len, limit):
    row = lax.broadcasted_iota(jnp.int32, (2 * seq_len, seq_len), 0) % seq_len
    column = lax.broadcasted_iota(jnp.int32, (2 * seq_len, seq_len), 1)
    return (column <= row) & (column < limit)


def pair_softmax(query_stack, key_pair, mask):
    scores = mm_nt(query_stack, key_pair) * HEAD_DIM ** (-0.5)
    scores = jnp.where(mask, scores, masked_score)
    grown = jnp.exp(scores - jnp.max(scores, axis=-1, keepdims=True))
    return grown * (1.0 / jnp.sum(grown, axis=-1, keepdims=True))


GROUP = 8 * HEAD_DIM
BLOCK = 1024
PIECE = 256


def attention_forward_kernel(
    facts_ref, x_ref, norm_ref, table_ref, first_ref, wq_ref, wk_ref, wv_ref, bq_ref, bk_ref, bv_ref,
    wo_ref, ao_ref, bo_ref, *refs,
):
    q_out, k_out, v_out, mixed_out, midq_out, mido_out, att_out, a_scr, mid_scr = refs[-9:]
    step = pl.program_id(0)
    seqs = x_ref.shape[0] // table_ref.shape[1]
    seq_len = table_ref.shape[1]

    @pl.when(step == 0)
    def _():
        normal, _ = normalize(x_ref[...])
        a_scr[...] = half(normal * norm_ref[0:1] + norm_ref[2:3])
        midq_out[...] = half(mm(a_scr[...], first_ref[...]))
        att_out[...] = jnp.zeros_like(att_out)
        mid_scr[...] = jnp.zeros_like(mid_scr)

    normed = a_scr[...]
    mid = midq_out[...]
    tables = [tile_table(table_ref[index], seqs, GROUP) for index in range(3)]
    query = mm(normed, wq_ref[...]) + adapter_scale * mm(mid, bq_ref[...])
    q_out[...] = half(turn(query, *tables))
    key = mm(normed, wk_ref[...]) + adapter_scale * mm(mid, bk_ref[...])
    k_out[...] = half(turn(key, *tables))
    v_out[...] = half(mm(normed, wv_ref[...]) + adapter_scale * mm(mid, bv_ref[...]))
    work = []
    for seq in range(seqs):
        rows = slice(seq * seq_len, (seq + 1) * seq_len)
        mask = pair_mask(seq_len, facts_ref[0, seq])
        for pair in range(GROUP // (2 * HEAD_DIM)):
            lanes = slice(pair * 2 * HEAD_DIM, (pair + 1) * 2 * HEAD_DIM)
            work.append((rows, lanes, pair_softmax(stack_heads(q_out[rows, lanes]), k_out[rows, lanes], mask)))
    for rows, lanes, probability in work:
        mixed_out[rows, lanes] = half(merge_heads(mm(half(probability), v_out[rows, lanes])))
    mixed = mixed_out[...]
    att_out[...] += mm(mixed, wo_ref[...])
    mid_scr[...] += mm(mixed, ao_ref[...])

    @pl.when(step == pl.num_programs(0) - 1)
    def _():
        mido_out[...] = half(mid_scr[...])
        att_out[...] += adapter_scale * mm(mido_out[...], bo_ref[...])


def whole(*shape):
    return pl.BlockSpec(shape, lambda step, facts_ref: (0,) * len(shape))


def fixed(height, width, down=0, right=0):
    return pl.BlockSpec((height, width), lambda step, facts_ref: (down, right))


def layer_fixed(layer, height, width, down=0, right=0):
    return pl.BlockSpec((None, height, width), lambda step, facts_ref: (layer, down, right))


def layer_columns(layer, height, width, offset=0):
    return pl.BlockSpec((None, height, width), lambda step, facts_ref: (layer, 0, step + offset))


def layer_rows(layer, height, width, offset=0):
    return pl.BlockSpec((None, height, width), lambda step, facts_ref: (layer, step + offset, 0))


def column_block(height, width, offset=0):
    return pl.BlockSpec((height, width), lambda step, facts_ref: (0, step + offset))


def row_block(height, width, offset=0):
    return pl.BlockSpec((height, width), lambda step, facts_ref: (step + offset, 0))


def kernel_call(kernel, name, steps, in_specs, out_specs, out_shape, scratch, flops, size, exps=0, aliases={}):
    return pl.pallas_call(
        kernel,
        out_shape=out_shape,
        grid_spec=pltpu.PrefetchScalarGridSpec(
            num_scalar_prefetch=1, grid=(steps,), in_specs=in_specs, out_specs=out_specs, scratch_shapes=scratch
        ),
        compiler_params=pltpu.CompilerParams(
            dimension_semantics=("arbitrary",), vmem_limit_bytes=48 << 20
        ),
        input_output_aliases=aliases,
        cost_estimate=pl.CostEstimate(flops=flops, bytes_accessed=size, transcendentals=exps),
        name=name,
    )


def shaped(shape, dtype=jnp.bfloat16):
    return jax.ShapeDtypeStruct(shape, dtype)


def attention_forward(residual, weights, norms, tables, facts, after):
    tokens, width = residual.shape
    groups = width // GROUP
    joint, output = weights[0], weights[1]
    firsts, seconds, _, layer = weights[4:8]
    seq_len = tables.shape[1]
    return kernel_call(
        attention_forward_kernel,
        "attention_forward",
        groups,
        [
            whole(tokens, width),
            whole(4, width),
            whole(3, seq_len, 2 * HEAD_DIM),
            layer_fixed(layer, width, RANK),
            column_block(width, GROUP),
            column_block(width, GROUP, groups),
            column_block(width, GROUP, 2 * groups),
            layer_columns(layer, RANK, GROUP),
            layer_columns(layer, RANK, GROUP, groups),
            layer_columns(layer, RANK, GROUP, 2 * groups),
            row_block(GROUP, width),
            layer_rows(layer, GROUP, RANK, groups),
            layer_fixed(layer, RANK, width, 0, 3),
        ]
        + [pl.BlockSpec(memory_space=pl.ANY)] * len(after),
        [column_block(tokens, GROUP)] * 4 + [whole(tokens, RANK), whole(tokens, RANK), whole(tokens, width)],
        [shaped((tokens, width))] * 4
        + [shaped((tokens, RANK)), shaped((tokens, RANK)), shaped((tokens, width), jnp.float32)],
        [pltpu.VMEM((tokens, width), jnp.bfloat16), pltpu.VMEM((tokens, RANK), jnp.float32)],
        2 * tokens * width * width * 4,
        2 * 5 * width * width + 12 * tokens * width,
    )(
        facts, residual, norms, tables, firsts, joint, joint, joint, seconds, seconds, seconds, output,
        firsts, seconds, *after,
    )


def feed_forward_kernel(
    facts_ref, x_ref, norm_ref, att_ref, first_ref, wu_ref, bu_ref, wd_ref, ad_ref, bd_ref,
    act_out, slope_out, midu_out, midd_out, x_out, sums_out,
    a_scr, mid_scr,
):
    step = pl.program_id(0)

    @pl.when(step == 0)
    def _():
        normal, _ = normalize(x_ref[...])
        a_scr[...] = half(normal * norm_ref[1:2] + norm_ref[3:4])
        midu_out[...] = half(mm(a_scr[...], first_ref[...]))
        x_out[...] = jnp.zeros_like(x_out)
        mid_scr[...] = jnp.zeros_like(mid_scr)

    normed, mid = a_scr[...], midu_out[...]
    parts = [slice(begin, begin + PIECE) for begin in range(0, act_out.shape[1], PIECE)]
    uppers = [mm(normed, wu_ref[:, part]) + adapter_scale * mm(mid, bu_ref[:, part]) for part in parts]
    for upper, part in zip(uppers, parts):
        spread = 0.5 + 0.5 * lax.erf(upper * 0.5**0.5)
        density = jnp.exp(-0.5 * upper * upper) * (0.5 / jnp.pi) ** 0.5
        active = half(upper * spread)
        act_out[:, part] = active
        slope_out[:, part] = half(spread + upper * density)
        x_out[...] += mm(active, wd_ref[part])
        mid_scr[...] += mm(active, ad_ref[part])

    @pl.when(step == pl.num_programs(0) - 1)
    def _():
        midd_out[...] = half(mid_scr[...])
        feed = x_out[...] + adapter_scale * mm(midd_out[...], bd_ref[...])
        attended = att_ref[...]
        residual = x_ref[...]
        x_out[...] = residual + (attended + feed)
        lane = lax.broadcasted_iota(jnp.int32, (1, 128), 1)
        seqs = facts_ref.shape[1]
        seq_len = residual.shape[0] // seqs
        row = lax.broadcasted_iota(jnp.int32, (seq_len, 1), 0)
        parts = []
        for part in (residual, attended, feed):
            squares = jnp.sum(part * part, axis=-1, keepdims=True)
            sums = jnp.zeros((1, 128), jnp.float32)
            for seq in range(seqs):
                valid = jnp.where(row < facts_ref[0, seq], squares[seq * seq_len : (seq + 1) * seq_len], 0.0)
                counted = (lane == facts_ref[1, seq]) | (lane == DOMAINS)
                sums = sums + jnp.where(counted, jnp.sum(valid), 0.0)
            parts.append(sums)
        sums_out[...] = jnp.concatenate(parts + [jnp.zeros((5, 128), jnp.float32)], 0)


def feed_forward(residual, attended, weights, norms, facts):
    tokens, width = residual.shape
    upper, down = weights[2], weights[3]
    firsts, seconds, _, layer = weights[4:8]
    hidden = upper.shape[1]
    return kernel_call(
        feed_forward_kernel,
        "feed_forward",
        hidden // BLOCK,
        [
            whole(tokens, width),
            whole(4, width),
            whole(tokens, width),
            layer_fixed(layer, width, RANK, 2, 0),
            column_block(width, BLOCK),
            layer_columns(layer, RANK, BLOCK, 4 * width // BLOCK),
            row_block(BLOCK, width),
            layer_rows(layer, BLOCK, RANK, 3 * width // BLOCK),
            layer_fixed(layer, RANK, width, 0, 8),
        ],
        [column_block(tokens, BLOCK)] * 2
        + [whole(tokens, RANK), whole(tokens, RANK), whole(tokens, width), whole(8, 128)],
        [shaped((tokens, hidden))] * 2
        + [shaped((tokens, RANK))] * 2
        + [shaped((tokens, width), jnp.float32), shaped((8, 128), jnp.float32)],
        [pltpu.VMEM((tokens, width), jnp.bfloat16), pltpu.VMEM((tokens, RANK), jnp.float32)],
        2 * tokens * width * hidden * 2,
        4 * width * hidden + 4 * tokens * hidden + 12 * tokens * width,
        2 * tokens * hidden,
    )(facts, residual, norms, attended, firsts, upper, seconds, down, firsts, seconds)


def write_extra(block_out, grad, normal, sums):
    width = grad.shape[1]
    row = [jnp.sum(grad * normal, axis=0, keepdims=True), jnp.sum(grad, axis=0, keepdims=True)] + sums
    rest = block_out.shape[1] - sum(part.shape[1] for part in row)
    row = jnp.concatenate(row + [jnp.zeros((1, rest), jnp.float32)], 1)
    block_out[RANK:, :] = half(jnp.concatenate([row, jnp.zeros((7, row.shape[1]), jnp.float32)], 0))


def block_copies(block_out, whole_out, first, sem):
    width = whole_out.shape[2]
    copies = []
    for index in range(block_out.shape[1] // width):
        source = block_out.at[:, pl.ds(index * width, width)]
        copies.append(pltpu.make_async_copy(source, whole_out.at[first + index], sem.at[index]))
        copies[-1].start()
    return copies


def feed_backward_kernel(
    facts_ref, g_ref, x_ref, norm_ref, act_ref, slope_ref, midu_ref, midd_ref, sums_ref, wu_ref, wd_ref, au_ref,
    bu_ref, ad_ref, bd_ref,
    whole_out, gx_out,
    block_out, g_scr, gmd_scr, gmdt_scr, midut_scr, gmu_scr, sem,
):
    step = pl.program_id(0)
    width = x_ref.shape[1]
    hidden = pl.num_programs(0) * BLOCK

    @pl.when(step == 0)
    def _():
        g_scr[...] = half(g_ref[...])
        grad_mid = adapter_scale * mm_nt(g_scr[...], bd_ref[...])
        gmd_scr[...] = half(grad_mid)
        gmdt_scr[...] = half(half(grad_mid).astype(jnp.float32).T)
        midut_scr[...] = half(midu_ref[...].astype(jnp.float32).T)
        gx_out[...] = jnp.zeros_like(gx_out)
        gmu_scr[...] = jnp.zeros_like(gmu_scr)
        middt = half(midd_ref[...].astype(jnp.float32).T)
        block_out[:RANK, pl.ds(width + 2 * hidden, width)] = half(adapter_scale * mm(middt, g_scr[...]))

    grad_act = mm_nt(g_scr[...], wd_ref[...]) + mm_nt(gmd_scr[...], ad_ref[...])
    grad_up = half(half(grad_act).astype(jnp.float32) * slope_ref[...].astype(jnp.float32))
    first_at = pl.multiple_of(width + step * BLOCK, BLOCK)
    second_at = pl.multiple_of(width + hidden + step * BLOCK, BLOCK)
    block_out[:RANK, pl.ds(first_at, BLOCK)] = half(mm(gmdt_scr[...], act_ref[...]))
    block_out[:RANK, pl.ds(second_at, BLOCK)] = half(adapter_scale * mm(midut_scr[...], grad_up))
    gmu_scr[...] += mm_nt(grad_up, bu_ref[...])
    gx_out[...] += mm_nt(grad_up, wu_ref[...])

    @pl.when(step == pl.num_programs(0) - 1)
    def _():
        grad_mid = half(adapter_scale * gmu_scr[...])
        normal, scale = normalize(x_ref[...])
        normed = half(normal * norm_ref[1:2] + norm_ref[3:4])
        block_out[:RANK, :width] = half(mm(half(grad_mid.astype(jnp.float32).T), normed))
        grad = gx_out[...] + mm_nt(grad_mid, au_ref[...])
        write_extra(block_out, grad, normal, [sums_ref[index : index + 1] for index in range(3)])
        gather = block_copies(block_out, whole_out, 6, sem)
        gx_out[...] = g_ref[...] + norm_gradient(grad, normal, scale, norm_ref[1:2])
        for copy in gather:
            copy.wait()


def feed_backward(gradient, residual, weights, norms, kept, facts):
    tokens, width = residual.shape
    upper, down = weights[2], weights[3]
    firsts, seconds, _, layer = weights[4:8]
    active, slope, mid_u, mid_d, sums = kept
    hidden = upper.shape[1]
    return kernel_call(
        feed_backward_kernel,
        "feed_backward",
        hidden // BLOCK,
        [
            whole(tokens, width),
            whole(tokens, width),
            whole(4, width),
            column_block(tokens, BLOCK),
            column_block(tokens, BLOCK),
            whole(tokens, RANK),
            whole(tokens, RANK),
            whole(8, 128),
            column_block(width, BLOCK),
            row_block(BLOCK, width),
            layer_fixed(layer, width, RANK, 2, 0),
            layer_columns(layer, RANK, BLOCK, 4 * width // BLOCK),
            layer_rows(layer, BLOCK, RANK, 3 * width // BLOCK),
            layer_fixed(layer, RANK, width, 0, 8),
        ],
        [pl.BlockSpec(memory_space=pl.ANY), whole(tokens, width)],
        [shaped((16, RANK + 8, width)), shaped((tokens, width), jnp.float32)],
        [
            pltpu.VMEM((RANK + 8, 2 * width + 2 * hidden), jnp.bfloat16),
            pltpu.VMEM((tokens, width), jnp.bfloat16),
            pltpu.VMEM((tokens, RANK), jnp.bfloat16),
            pltpu.VMEM((RANK, tokens), jnp.bfloat16),
            pltpu.VMEM((RANK, tokens), jnp.bfloat16),
            pltpu.VMEM((tokens, RANK), jnp.float32),
            pltpu.SemaphoreType.DMA((10,)),
        ],
        2 * tokens * width * hidden * 2,
        4 * width * hidden + 4 * tokens * hidden + 16 * tokens * width,
    )(
        facts, gradient, residual, norms, active, slope, mid_u, mid_d, sums, upper, down, firsts, seconds,
        firsts, seconds,
    )


def attention_backward_kernel(
    facts_ref, g_ref, gx_ref, x_ref, norm_ref, table_ref, q_ref, k_ref, v_ref, mixed_ref, midq_ref, mido_ref,
    wq_ref, wk_ref, wv_ref, aq_ref, bq_ref, bk_ref, bv_ref, wo_ref, ao_ref, bo_ref, feed_block_ref, *refs,
):
    whole_out, gx_out = refs[-13:-11]
    block_out, g_scr, gmo_scr, gmot_scr, midqt_scr, gmq_scr, acc_scr, gq_scr, gk_scr, gv_scr, sem = refs[-11:]
    step = pl.program_id(0)
    width = x_ref.shape[1]
    seq_len = table_ref.shape[1]
    seqs = x_ref.shape[0] // seq_len
    scale_factor = HEAD_DIM ** (-0.5)

    @pl.when(step == 0)
    def _():
        g_scr[...] = half(g_ref[...])
        grad_mid = half(adapter_scale * mm_nt(g_scr[...], bo_ref[...]))
        gmo_scr[...] = grad_mid
        gmot_scr[...] = half(grad_mid.astype(jnp.float32).T)
        midqt_scr[...] = half(midq_ref[...].astype(jnp.float32).T)
        acc_scr[...] = jnp.zeros_like(acc_scr)
        gmq_scr[...] = jnp.zeros_like(gmq_scr)
        midot = half(mido_ref[...].astype(jnp.float32).T)
        block_out[:RANK, pl.ds(5 * width, width)] = half(adapter_scale * mm(midot, g_scr[...]))

    grad_mixed = half(mm_nt(g_scr[...], wo_ref[...]) + mm_nt(gmo_scr[...], ao_ref[...]))
    first_at = pl.multiple_of(width + step * GROUP, GROUP)
    block_out[:RANK, pl.ds(first_at, GROUP)] = half(mm(gmot_scr[...], mixed_ref[...]))
    work = []
    for seq in range(seqs):
        rows = slice(seq * seq_len, (seq + 1) * seq_len)
        mask = pair_mask(seq_len, facts_ref[0, seq])
        for pair in range(GROUP // (2 * HEAD_DIM)):
            lanes = slice(pair * 2 * HEAD_DIM, (pair + 1) * 2 * HEAD_DIM)
            query_stack = stack_heads(q_ref[rows, lanes])
            grad_stack = stack_heads(grad_mixed[rows, lanes])
            probability = pair_softmax(query_stack, k_ref[rows, lanes], mask)
            grad_prob = mm_nt(grad_stack, v_ref[rows, lanes])
            inner = jnp.sum(probability * grad_prob, axis=-1, keepdims=True)
            grad_scores = half(probability * (grad_prob - inner))
            work.append((rows, lanes, query_stack, grad_stack, half(probability), grad_scores))
    for rows, lanes, query_stack, grad_stack, probability, grad_scores in work:
        gv_scr[rows, lanes] = half(mm_tn(probability, grad_stack))
        gq_scr[rows, lanes] = merge_heads(mm(grad_scores, k_ref[rows, lanes])) * scale_factor
        gk_scr[rows, lanes] = mm_tn(grad_scores, query_stack) * scale_factor
    tables = [tile_table(table_ref[index], seqs, GROUP) for index in range(3)]
    joint = (half(turn_back(gq_scr[...], *tables)), half(turn_back(gk_scr[...], *tables)), gv_scr[...])
    mid = midqt_scr[...]
    for index, (grad, w_ref, b_ref) in enumerate(zip(joint, (wq_ref, wk_ref, wv_ref), (bq_ref, bk_ref, bv_ref))):
        second_at = pl.multiple_of((2 + index) * width + step * GROUP, GROUP)
        block_out[:RANK, pl.ds(second_at, GROUP)] = half(adapter_scale * mm(mid, grad))
        gmq_scr[...] += mm_nt(grad, b_ref[...])
        acc_scr[...] += mm_nt(grad, w_ref[...])

    @pl.when(step == pl.num_programs(0) - 1)
    def _():
        grad_mid = half(adapter_scale * gmq_scr[...])
        normal, scale = normalize(x_ref[...])
        normed = half(normal * norm_ref[0:1] + norm_ref[2:3])
        block_out[:RANK, :width] = half(mm(half(grad_mid.astype(jnp.float32).T), normed))
        grad = acc_scr[...] + mm_nt(grad_mid, aq_ref[...])
        write_extra(block_out, grad, normal, [])
        gather = block_copies(block_out, whole_out, 0, sem)
        gx_out[...] = gx_ref[...] + norm_gradient(grad, normal, scale, norm_ref[0:1])
        for copy in gather:
            copy.wait()


def attention_backward(gradient, grad_feed, feed_block, residual, weights, norms, tables, kept, facts, after):
    tokens, width = residual.shape
    groups = width // GROUP
    joint, output = weights[0], weights[1]
    firsts, seconds, _, layer = weights[4:8]
    queries, keys, values, mixed, mid_q, mid_o = kept
    seq_len = tables.shape[1]
    block = column_block(tokens, GROUP)
    return kernel_call(
        attention_backward_kernel,
        "attention_backward",
        groups,
        [
            whole(tokens, width),
            whole(tokens, width),
            whole(tokens, width),
            whole(4, width),
            whole(3, seq_len, 2 * HEAD_DIM),
            block,
            block,
            block,
            block,
            whole(tokens, RANK),
            whole(tokens, RANK),
            column_block(width, GROUP),
            column_block(width, GROUP, groups),
            column_block(width, GROUP, 2 * groups),
            layer_fixed(layer, width, RANK),
            layer_columns(layer, RANK, GROUP),
            layer_columns(layer, RANK, GROUP, groups),
            layer_columns(layer, RANK, GROUP, 2 * groups),
            row_block(GROUP, width),
            layer_rows(layer, GROUP, RANK, groups),
            layer_fixed(layer, RANK, width, 0, 3),
            pl.BlockSpec(memory_space=pl.ANY),
        ]
        + [pl.BlockSpec(memory_space=pl.ANY)] * len(after),
        [pl.BlockSpec(memory_space=pl.ANY), whole(tokens, width)],
        [shaped((16, RANK + 8, width)), shaped((tokens, width), jnp.float32)],
        [
            pltpu.VMEM((RANK + 8, 6 * width), jnp.bfloat16),
            pltpu.VMEM((tokens, width), jnp.bfloat16),
            pltpu.VMEM((tokens, RANK), jnp.bfloat16),
            pltpu.VMEM((RANK, tokens), jnp.bfloat16),
            pltpu.VMEM((RANK, tokens), jnp.bfloat16),
            pltpu.VMEM((tokens, RANK), jnp.float32),
            pltpu.VMEM((tokens, width), jnp.float32),
            pltpu.VMEM((tokens, GROUP), jnp.float32),
            pltpu.VMEM((tokens, GROUP), jnp.float32),
            pltpu.VMEM((tokens, GROUP), jnp.bfloat16),
            pltpu.SemaphoreType.DMA((6,)),
        ],
        2 * tokens * width * width * 4,
        2 * 5 * width * width + 24 * tokens * width,
        aliases={22: 0},
    )(
        facts, gradient, grad_feed, residual, norms, tables, queries, keys, values, mixed, mid_q, mid_o, joint,
        joint, joint, firsts, seconds, seconds, seconds, output, firsts, seconds, feed_block, *after,
    )


def layer_forward(residual, weights, tables, facts, after=()):
    norms = weights[6]
    *kept_attention, attended = attention_forward(residual, weights, norms, tables, facts, after)
    *kept_feed, output, sums = feed_forward(residual, attended, weights, norms, facts)
    return output, (residual, kept_attention, kept_feed + [sums])


def layer_backward(gradient, kept, weights, tables, facts, after=()):
    residual, kept_attention, kept_feed = kept
    norms = weights[6]
    feed_block, grad_feed = feed_backward(gradient, residual, weights, norms, kept_feed, facts)
    block, grad_input = attention_backward(
        gradient, grad_feed, feed_block, residual, weights, norms, tables, kept_attention, facts, after
    )
    return grad_input, block


def gather_plan(gathers, turns):
    if (gathers, turns) == (4, 3):
        return [[0, 2], [0, 2], [0, 1], [2, 1], [1, 3], [3], [3]]
    order = [0, 2, 1, 3]
    return [[order[step // turns]] for step in range(gathers * turns)]


def shards(
    inputs,
    cotangent,
    domain,
    lengths,
    steps_since_reset,
    frozen_query_weight,
    frozen_output_weight,
    frozen_up_weight,
    frozen_down_weight,
    query_adapter_first,
    query_adapter_second,
    output_adapter_first,
    output_adapter_second,
    up_adapter_first,
    up_adapter_second,
    down_adapter_first,
    down_adapter_second,
    layer_norm_gain,
    layer_norm_bias,
):
    core = lax.axis_index("section")
    place = lax.axis_index("dp")
    count = lax.axis_size("dp")
    middle = count // 2
    stage = place // middle
    low = place % middle
    home = core == stage
    masks = [1 << bit for bit in range(middle.bit_length() - 1)]
    frozen = (frozen_query_weight, frozen_output_weight, frozen_up_weight, frozen_down_weight)
    trained = (
        query_adapter_first,
        query_adapter_second,
        output_adapter_first,
        output_adapter_second,
        up_adapter_first,
        up_adapter_second,
        down_adapter_first,
        down_adapter_second,
    )
    local_layers = frozen_query_weight.shape[0]
    rows_dev, seq_len, model_width = inputs.shape
    tokens = rows_dev * seq_len

    places = [(index // middle, index) for index in range(count)]
    to_sibling = [(here * count + index, (1 - here) * count + index) for here, index in places]
    to_cross = [((1 - here) * count + index, here * count + (index ^ middle)) for here, index in places]
    sibling, cross = [partial(both_axes, pairs=pairs) for pairs in (to_sibling, to_cross)]

    same, other = pack_halves(core, frozen)
    swapped_units = flip_core(other)
    own = jnp.where(home, same, swapped_units)
    leaving = jnp.where(home, swapped_units, same)
    partner = [flip_place(leaving[0], middle)]
    for layer in range(1, local_layers):
        partner.append(flip_place(tie(leaving[layer], partner[-1]), middle))
    gathers = []
    for layer in range(local_layers):
        gathers.append(Gather(layer, 0, own[layer], masks))
        gathers.append(Gather(layer, 1, partner[layer], masks))
    plan = gather_plan(len(gathers), len(masks)) + [[]]
    dense = [None] * local_layers
    facts = jnp.stack([lengths, domain])
    norms = jnp.concatenate([layer_norm_gain, layer_norm_bias], 1)
    facts = jnp.where(home, facts, cross(facts))
    norms = jnp.where(home, norms, sibling(norms))
    visiting = jnp.where(stage == 0, cotangent, inputs)
    tables = rotary_tables(seq_len)
    ended, fresh, started, waiting = (), [], set(), []
    bases = [jnp.where(stage == which, 0, middle) for which in range(2)]
    for number, active in enumerate(plan):
        if number == len(plan) - 1:
            start = jnp.where(home, inputs, visiting).astype(jnp.float32).reshape(tokens, model_width)
            while waiting and min(layer for layer, _ in waiting[0][1]) == 0:
                assemble(*waiting.pop(0), count, dense)
            first_weights = tuple(dense[0]) + (packed[0], packed[1], norms[0], 0)
            boundary, _ = layer_forward(start, first_weights, tables, facts)
            ended = ended + (boundary,)
        for index in active:
            if index not in started:
                started.add(index)
                gather = gathers[index]
                fresh = fresh + [(gather.block, part, 1, gather, part, [0]) for part in range(3)]
        extra = []
        if number in (1, 2):
            extra.append((packed[number - 1], sibling))
        if number == 4:
            extra.append((visiting, cross))
        moving = fresh if number >= 2 else []
        there, came, collected, swapped, results = gather_step(
            [gathers[index] for index in active], masks, moving, extra, ended
        )
        fresh = came if moving else fresh + came
        if number == 0:
            packed = list(pack_adapters(trained, swapped_units))
        if number in (1, 2):
            packed[number - 1] = jnp.where(home, packed[number - 1], results[0])
        if number == 4:
            visiting = results[0]
        marks = [assemble(*waiting.pop(0), count, dense)] if waiting and number < len(plan) - 1 else []
        ended = tuple(there) + tuple(results) + tuple(marks)
        if number == 3:
            ended = ended + tuple(packed)
        if moving:
            ended = ended + (swapped,)
            layout = [(gather.layer, part) for _, _, size, gather, part, _ in moving for _ in range(size)]
            places_of = [
                (known ^ low) + bases[gather.which] for _, _, _, gather, _, found in moving for known in found
            ]
            info = jnp.stack([core] + places_of)
            waiting.append((info, layout, collected, swapped))
    for item in waiting:
        assemble(*item, count, dense)
    weights = [tuple(dense[layer]) + (packed[0], packed[1], norms[layer], layer) for layer in range(local_layers)]
    valid = jnp.arange(seq_len)[None, :] < facts[0][:, None]
    end_grad = jnp.where(home, cotangent, visiting).astype(jnp.float32)
    end_grad = jnp.where(stage == 1, end_grad * valid[..., None].astype(jnp.float32), 0.0)
    end_grad = end_grad.reshape(tokens, model_width)
    def stage_forward(residual, after):
        kept = []
        for layer in range(local_layers):
            residual, kept_state = layer_forward(residual, weights[layer], tables, facts, after if layer == 0 else ())
            kept.append(kept_state)
        return residual, kept

    for layer in range(1, local_layers):
        boundary, _ = layer_forward(boundary, weights[layer], tables, facts)
    boundary = boundary.astype(jnp.bfloat16)
    forward_pairs = [(index, index + middle) for index in range(middle)]
    received = lax.ppermute(boundary, "dp", forward_pairs)
    lane = jnp.arange(128)
    counted = (domain[:, None] == lane[None, :]) | (lane == DOMAINS)[None, :]
    counts = jnp.sum(jnp.where(counted, lengths.astype(jnp.float32)[:, None], 0.0), axis=0, keepdims=True)
    for mask in masks + [middle]:
        counts = counts + flip_place(counts, mask)
    counts = jnp.maximum(counts, 1.0) * model_width
    entry = jnp.where(stage == 0, start, received.astype(jnp.float32))
    final, kept = stage_forward(entry, (counts,))
    final = final.astype(jnp.bfloat16)

    gradient = end_grad
    late = [None] * local_layers
    for layer in reversed(range(local_layers)):
        gradient, late[layer] = layer_backward(gradient, kept[layer], weights[layer], tables, facts)
    sent = gradient.astype(jnp.bfloat16)
    came_back = lax.ppermute(sent, "dp", [(after, before) for before, after in forward_pairs])
    late_halves = tie([swap_halves(block, 1, core, count) for block in late], came_back)
    late_piece = sum_halves(late_halves, count)

    gradient = jnp.where(stage == 0, came_back.astype(jnp.float32), 0.0)
    out_pairs = [(count + index + middle, index + middle) for index in range(middle)]
    out_pairs = out_pairs + [(index + middle, count + index) for index in range(middle)]
    visiting = both_axes(jnp.where(core == 0, final, received), out_pairs)
    section_out = jnp.where(home, jnp.where(stage == 0, boundary, final), visiting)
    section_out = section_out.reshape(1, rows_dev, seq_len, model_width)
    pieces = [None] * local_layers
    after = ()
    for layer in reversed(range(local_layers)):
        gradient, block = layer_backward(gradient, kept[layer], weights[layer], tables, facts, after)
        halves = swap_halves(block, 0, core, count)
        if layer == local_layers - 1:
            pieces[layer] = sum_halves([tie(halves, late_piece)], count)
            late_piece = cross_section(late_piece, 1, stage, count)
            after = (late_piece,)
        else:
            if layer == 0:
                late_whole = spread_section(tie(late_piece, pieces[local_layers - 1]), 1, count)
                halves = tie(halves, late_whole[1])
            pieces[layer] = sum_halves([halves], count)
            after = ()
    early_piece = cross_section(jnp.concatenate(pieces, 0), 0, stage, count)
    early_whole = spread_section(early_piece, 0, count)

    grad_pairs = [(index, count + index) for index in range(middle)]
    grad_pairs = grad_pairs + [(count + index, index + middle) for index in range(middle)]
    visiting = both_axes(jnp.where(core == 0, came_back, gradient.astype(jnp.bfloat16)), grad_pairs)
    section_grad = jnp.where(
        home, jnp.where(stage == 0, gradient, sent.astype(jnp.float32)), visiting.astype(jnp.float32)
    )
    section_grad = section_grad.reshape(1, rows_dev, seq_len, model_width)

    rate = peak_rate * (steps_since_reset[0].astype(jnp.float32) + 1.0) / WARM
    outputs = finish(place, core, rate, early_whole, late_whole, counts, trained, frozen)
    *outputs, rms = outputs
    return (section_out, section_grad, *outputs, rms[:, :, : DOMAINS + 1])


def solution(mesh):
    across = P("dp", None, None)
    copied = P("section", None, None)
    split = P("section", "dp", None)
    wide = P("section", "dp", None, None)
    return jax.shard_map(
        shards,
        mesh=mesh,
        in_specs=(across, across, P("dp"), P("dp"), P()) + (split,) * 4 + (copied,) * 10,
        out_specs=(wide, wide) + (copied,) * 10 + (split,) * 4 + (copied,),
        check_vma=False,
    )
```

```python
from functools import partial

import jax
import jax.numpy as jnp
from jax import lax
from jax.experimental import pallas as pl
from jax.experimental.pallas import tpu as pltpu
from jax.sharding import PartitionSpec as P

HEADS = 16
HEAD_DIM = 64
ROT = 16
DOMAINS = 16
WARM = 50
RANK = 128
WIDE = 1024
UNITS = 12
HALF_UNITS = 6

adapter_scale = 0.5
norm_eps = 1e-05
peak_rate = 0.0002
masked_score = -1e30


def both_axes(value, pairs):
    return lax.ppermute(value, ("section", "dp"), pairs)


def tie(value, *others):
    return lax.optimization_barrier((value, others))[0]


def flip_place(value, mask):
    count = lax.axis_size("dp")
    return lax.ppermute(value, "dp", [(place, place ^ mask) for place in range(count)])


def flip_core(value):
    return lax.ppermute(value, "section", [(0, 1), (1, 0)])


def pack_kernel(info_ref, query_ref, output_ref, upper_ref, down_ref, keep_ref, send_ref):
    rows = output_ref.shape[1]

    def write(first, second):
        for layer in range(output_ref.shape[0]):
            first[layer, 0] = query_ref[layer, :, :WIDE]
            first[layer, 1] = query_ref[layer, :, WIDE : 2 * WIDE]
            first[layer, 2] = query_ref[layer, :, 2 * WIDE :]
            first[layer, 3] = output_ref[layer]
            first[layer, 4] = upper_ref[layer, :, :WIDE]
            first[layer, 5] = upper_ref[layer, :, WIDE : 2 * WIDE]
            second[layer, 0] = upper_ref[layer, :, 2 * WIDE : 3 * WIDE]
            second[layer, 1] = upper_ref[layer, :, 3 * WIDE :]
            for index in range(4):
                second[layer, 2 + index] = down_ref[layer, index * rows : (index + 1) * rows]

    @pl.when(info_ref[0] == 0)
    def _():
        write(keep_ref, send_ref)

    @pl.when(info_ref[0] != 0)
    def _():
        write(send_ref, keep_ref)


def pack_halves(core, frozen):
    layers, rows = frozen[1].shape[:2]
    shape = jax.ShapeDtypeStruct((layers, HALF_UNITS, rows, WIDE), jnp.bfloat16)
    vmem = pl.BlockSpec(memory_space=pltpu.VMEM)
    return pl.pallas_call(
        pack_kernel,
        out_shape=[shape, shape],
        in_specs=[pl.BlockSpec(memory_space=pltpu.SMEM)] + [vmem] * 4,
        out_specs=[vmem, vmem],
        compiler_params=pltpu.CompilerParams(vmem_limit_bytes=32 << 20),
        cost_estimate=pl.CostEstimate(
            flops=0, bytes_accessed=8 * HALF_UNITS * layers * rows * WIDE, transcendentals=0
        ),
        name="pack",
    )(core.reshape(1), *frozen)


def pack_adapters_kernel(*refs):
    sources, (first_out, second_out) = refs[:8], refs[-2:]
    at = 0
    for source in sources[0::2]:
        first_out[:, at : at + source.shape[1]] = source[...]
        at = at + source.shape[1]
    at = 0
    for source in sources[1::2]:
        second_out[:, :, at : at + source.shape[2]] = source[...]
        at = at + source.shape[2]


def pack_adapters(trained, *after):
    layers = trained[0].shape[0]
    height = sum(factor.shape[1] for factor in trained[0::2])
    width = sum(factor.shape[2] for factor in trained[1::2])
    shapes = [
        jax.ShapeDtypeStruct((layers, height, RANK), jnp.bfloat16),
        jax.ShapeDtypeStruct((layers, RANK, width), jnp.bfloat16),
    ]

    def layer_block(value):
        return pl.BlockSpec((1,) + value.shape[1:], lambda step: (step, 0, 0))

    return pl.pallas_call(
        pack_adapters_kernel,
        out_shape=shapes,
        grid=(layers,),
        in_specs=[layer_block(factor) for factor in trained] + [pl.BlockSpec(memory_space=pl.ANY)] * len(after),
        out_specs=[layer_block(shape) for shape in shapes],
        compiler_params=pltpu.CompilerParams(vmem_limit_bytes=30 << 20),
        cost_estimate=pl.CostEstimate(flops=0, bytes_accessed=4 * RANK * layers * (height + width), transcendentals=0),
        name="pack_adapters",
    )(*trained, *after)


def rotations(masks):
    return [[masks[(start + index) % len(masks)] for index in range(len(masks))] for start in range(3)]


def assemble_kernel(layout, info_ref, mine, theirs, *refs):
    count = len({layer for layer, _ in layout})
    outs, token_out, sem = refs[-4 * count - 2 : -2], refs[-2], refs[-1]
    token_out[...] = jnp.zeros_like(token_out)
    first_layer = min(layer for layer, _ in layout)
    rows = mine.shape[2]

    def targets(half_index, layer, part, place):
        query_out, output_out, upper_out, down_out = outs[4 * (layer - first_layer) : 4 * (layer - first_layer) + 4]
        at = pl.multiple_of(place * rows, rows)
        down_at = pl.multiple_of(place * 4 * rows, rows)

        def columns(out, index):
            return out.at[pl.ds(at, rows), pl.ds(index * WIDE, WIDE)]

        def down(index):
            return down_out.at[pl.ds(down_at + index * rows, rows)]

        return [
            [(columns(query_out, 0), columns(query_out, 1)), (columns(query_out, 2), columns(output_out, 0)),
             (columns(upper_out, 0), columns(upper_out, 1))],
            [(columns(upper_out, 2), columns(upper_out, 3)), (down(0), down(1)), (down(2), down(3))],
        ][half_index][part]

    def run(first, second):
        copies = []
        for block, (layer, part) in enumerate(layout):
            for half_index, source in enumerate((first, second)):
                for unit, target in enumerate(targets(half_index, layer, part, info_ref[1 + block])):
                    where = sem.at[block, half_index * 2 + unit]
                    copies.append(pltpu.make_async_copy(source.at[block, unit], target, where))
                    copies[-1].start()
        for copy in copies:
            copy.wait()

    @pl.when(info_ref[0] == 0)
    def _():
        run(mine, theirs)

    @pl.when(info_ref[0] != 0)
    def _():
        run(theirs, mine)


def assemble(info, layout, mine, theirs, count, into):
    rows = mine.shape[2]
    total = rows * count
    layers = sorted({layer for layer, _ in layout})
    shapes = [(total, 3 * WIDE), (total, WIDE), (total, 4 * WIDE), (4 * total, WIDE)] * len(layers)
    extra = [matrix for layer in layers for matrix in (into[layer] or ())]
    anywhere = pl.BlockSpec(memory_space=pltpu.HBM)
    aliases, index = {}, 3
    for position, layer in enumerate(layers):
        if into[layer]:
            for matrix in range(4):
                aliases[index] = 4 * position + matrix
                index = index + 1
    made = pl.pallas_call(
        partial(assemble_kernel, tuple(layout)),
        out_shape=[jax.ShapeDtypeStruct(shape, jnp.bfloat16) for shape in shapes]
        + [jax.ShapeDtypeStruct((8, 128), jnp.float32)],
        in_specs=[pl.BlockSpec(memory_space=pltpu.SMEM)]
        + [pl.BlockSpec(memory_space=pltpu.VMEM)] * 2
        + [anywhere] * len(extra),
        out_specs=[anywhere] * len(shapes) + [pl.BlockSpec(memory_space=pltpu.VMEM)],
        scratch_shapes=[pltpu.SemaphoreType.DMA((len(layout), 4))],
        input_output_aliases=aliases,
        compiler_params=pltpu.CompilerParams(vmem_limit_bytes=60 << 20),
        cost_estimate=pl.CostEstimate(flops=0, bytes_accessed=12 * mine.size, transcendentals=0),
        name="assemble",
    )(info, mine, theirs, *extra)
    for position, layer in enumerate(layers):
        into[layer] = made[4 * position : 4 * position + 4]
    return made[-1]


def copy_kernel(plans, *refs):
    inputs, outs = refs[: -len(plans)], refs[-len(plans) :]
    for plan, out in zip(plans, outs):
        at = 0
        for source, begin, size in plan:
            out[at : at + size] = inputs[source][begin : begin + size]
            at = at + size


def copy_blocks(arrays, plans, after):
    tail = arrays[0].shape[1:]
    vmem = pl.BlockSpec(memory_space=pltpu.VMEM)
    shapes = [jax.ShapeDtypeStruct((sum(size for _, _, size in plan),) + tail, jnp.bfloat16) for plan in plans]
    moved = 4 * sum(shape.size for shape in shapes)
    return pl.pallas_call(
        partial(copy_kernel, tuple(tuple(plan) for plan in plans)),
        out_shape=shapes,
        in_specs=[vmem] * len(arrays) + [pl.BlockSpec(memory_space=pl.ANY)] * len(after),
        out_specs=[vmem] * len(shapes),
        compiler_params=pltpu.CompilerParams(vmem_limit_bytes=40 << 20),
        cost_estimate=pl.CostEstimate(flops=0, bytes_accessed=moved, transcendentals=0),
        name="collect",
    )(*arrays, *after)


class Gather:
    def __init__(self, layer, which, block, masks):
        self.layer, self.which = layer, which
        block = block.reshape((3, 2) + block.shape[1:])
        self.block = block
        self.held = [[(block, part, 1)] for part in range(3)]
        self.found = [[0], [0], [0]]
        self.turns = rotations(masks)
        self.step = 0


class Store:
    def __init__(self):
        self.arrays = []

    def index(self, array):
        for position, known in enumerate(self.arrays):
            if known is array:
                return position
        self.arrays.append(array)
        return len(self.arrays) - 1


def gather_step(active, masks, fresh, extra, after):
    store = Store()
    plans, lists = [], []
    for mask in masks:
        entries = [
            (gather, part) for gather in active for part in range(3) if gather.turns[part][gather.step] == mask
        ]
        if entries:
            plans.append(
                [
                    (store.index(array), begin, size)
                    for gather, part in entries
                    for array, begin, size in gather.held[part]
                ]
            )
            lists.append((mask, entries))
    if fresh:
        plans.append([(store.index(array), begin, size) for array, begin, size, _, _, _ in fresh])
    after = [value for value in after if all(value is not known for known in store.arrays)]
    values = list(copy_blocks(store.arrays, plans, after)) + [value for value, _ in extra]
    there = []
    for value, (mask, _) in zip(values, lists):
        there.append(flip_place(value, mask))
    collected = values[len(lists)] if fresh else None
    swapped = flip_core(collected) if fresh else None
    results = [send(value) for value, (_, send) in zip(values[len(plans) :], extra)]
    came = []
    for (mask, entries), value in zip(lists, there):
        begin = 0
        for gather, part in entries:
            size = sum(amount for _, _, amount in gather.held[part])
            known = [place ^ gather.turns[part][gather.step] for place in gather.found[part]]
            gather.held[part] = gather.held[part] + [(value, begin, size)]
            gather.found[part] = gather.found[part] + known
            came.append((value, begin, size, gather, part, known))
            begin = begin + size
    for gather in active:
        gather.step = gather.step + 1
    return there, came, collected, swapped, results


def pieces_by_place(block, pieces):
    if pieces == block.shape[0]:
        return block
    split = pieces // block.shape[0]
    columns = block.shape[2] // split
    block = block.reshape(block.shape[0], block.shape[1], split, columns).transpose(0, 2, 1, 3)
    return block.reshape(pieces, block.shape[2], columns)


def places_to_blocks(pieces, blocks):
    if pieces.shape[0] == blocks:
        return pieces
    split = pieces.shape[0] // blocks
    rows, columns = pieces.shape[1:]
    return pieces.reshape(blocks, split, rows, columns).transpose(0, 2, 1, 3).reshape(blocks, rows, split * columns)


def exchange(value, count):
    middle = count // 2
    groups = [[half_index * middle + index for index in range(middle)] for half_index in range(2)]
    return lax.all_to_all(value, "dp", 0, 0, axis_index_groups=groups)


def swap_halves(block, section, core, count):
    middle = count // 2
    inside = [place for place in range(count) if place // middle == section]
    swap = [(here * count + place, (1 - here) * count + place) for here in range(2) for place in inside]
    size = block.shape[0] // 2
    there = both_axes(lax.dynamic_slice_in_dim(block, (1 - core) * size, size, 0), swap)
    here = lax.dynamic_slice_in_dim(block, core * size, size, 0)
    return (here.astype(jnp.float32) + there.astype(jnp.float32)).astype(jnp.bfloat16)


def sum_halves(halves, count):
    pieces = [pieces_by_place(part, count // 2) for part in halves]
    pieces = pieces[0] if len(pieces) == 1 else jnp.concatenate(pieces, 1)
    return jnp.sum(exchange(pieces, count).astype(jnp.float32), axis=0).astype(jnp.bfloat16)


def scatter_section(blocks, section, core, count):
    return sum_halves([swap_halves(block, section, core, count) for block in blocks], count)


def cross_section(piece, section, stage, count):
    middle = count // 2
    across = [(place, place ^ middle) for place in range(count) if place // middle == section]
    return jnp.where(stage == section, piece, lax.ppermute(piece, "dp", across))


def spread_section(piece, section, count):
    middle = count // 2
    spread = exchange(jnp.broadcast_to(piece[None], (middle,) + piece.shape), count)
    here = places_to_blocks(spread, 8)
    there = lax.ppermute(here, "section", [(1 - section, section)])
    return (here, there) if section == 0 else (there, here)


def finish_kernel(
    info_ref, rate_ref, early0_ref, early1_ref, late0_ref, late1_ref, counts_ref,
    aq_ref, ao_ref, au_ref, ad_ref, bq_ref, bo_ref, bu_ref, bd_ref, wq_ref, wo_ref, wu_ref, wd_ref, *refs,
):
    gaq, gbq, gao, gbo, gau, gbu, gad, gbd, gain_out, bias_out, fq, fo, fu, fd, rms_out, g_ref, sem = refs[-17:]
    rate = rate_ref[0]
    size, height = early0_ref.shape[0], g_ref.shape[1]

    def fetch(sources, begin):
        copies = [
            pltpu.make_async_copy(
                source.at[:, pl.ds(begin, height)], g_ref.at[pl.ds(index * size, size)], sem.at[index]
            )
            for index, source in enumerate(sources)
        ]
        for copy in copies:
            copy.start()
        for copy in copies:
            copy.wait()

    @pl.when(info_ref[1] == 0)
    def _():
        fetch((early0_ref, early1_ref), pl.program_id(0) * height)

    @pl.when(info_ref[1] != 0)
    def _():
        fetch((late0_ref, late1_ref), pl.program_id(0) * height)

    def run():
        def columns(index, begin=0, end=RANK):
            return g_ref[index, begin:end].astype(jnp.float32)

        def project(first_at, second_at, a_ref, b_ref, w_ref, ga, gb, folded):
            for index in range(ga.shape[1] // WIDE):
                ga[0, index * WIDE : (index + 1) * WIDE] = columns(first_at + index).T
            span = w_ref.shape[1]
            rows = pl.ds(pl.multiple_of(info_ref[0] * span, span), span)
            new_first = a_ref[0, rows].astype(jnp.float32) - rate * ga[0, rows]
            for index in range(gb.shape[2] // WIDE):
                lanes = slice(index * WIDE, (index + 1) * WIDE)
                grad = columns(second_at + index)
                gb[0, :, lanes] = grad
                new_second = b_ref[0, :, lanes].astype(jnp.float32) - rate * grad
                product = jnp.dot(new_first, new_second, precision=lax.Precision.HIGHEST)
                folded[0, :, lanes] = (
                    w_ref[0, :, lanes].astype(jnp.float32) + adapter_scale * product
                ).astype(jnp.bfloat16)

        project(0, 2, aq_ref, bq_ref, wq_ref, gaq, gbq, fq)
        project(1, 5, ao_ref, bo_ref, wo_ref, gao, gbo, fo)
        project(6, 11, au_ref, bu_ref, wu_ref, gau, gbu, fu)
        project(7, 15, ad_ref, bd_ref, wd_ref, gad, gbd, fd)
        extra = [columns(index, RANK, RANK + 8)[:1] for index in (0, 6, 1, 7)]
        gain_out[0] = jnp.concatenate(extra[:2], 0)
        bias_out[0] = jnp.concatenate(extra[2:], 0)
        sums = columns(8, RANK, RANK + 8)[:1]
        sums = jnp.concatenate([sums[:, 128 * index : 128 * (index + 1)] for index in range(3)], 0)
        rms_out[0] = jnp.sqrt(sums / counts_ref[...])

    run()


def finish(place, core, rate, early, late, counts, trained, frozen):
    firsts, seconds = trained[0:8:2], trained[1:8:2]
    layers = firsts[0].shape[0]

    def layer_block(value):
        return pl.BlockSpec((1,) + value.shape[1:], lambda step, *_: (step, 0, 0))

    shapes = []
    for first, second in zip(firsts, seconds):
        shapes.append(jax.ShapeDtypeStruct(first.shape, jnp.float32))
        shapes.append(jax.ShapeDtypeStruct(second.shape, jnp.float32))
    shapes += [jax.ShapeDtypeStruct((layers, 2, WIDE), jnp.float32)] * 2
    shapes += [jax.ShapeDtypeStruct(matrix.shape, jnp.bfloat16) for matrix in frozen]
    shapes += [jax.ShapeDtypeStruct((layers, 3, 128), jnp.float32)]
    keep = pl.BlockSpec(memory_space=pl.ANY)
    return pl.pallas_call(
        finish_kernel,
        out_shape=shapes,
        grid_spec=pltpu.PrefetchScalarGridSpec(
            num_scalar_prefetch=1,
            grid=(layers,),
            in_specs=[pl.BlockSpec(memory_space=pltpu.SMEM)]
            + [keep] * 4
            + [pl.BlockSpec((1, 128), lambda step, *_: (0, 0))]
            + [layer_block(value) for value in firsts + seconds + frozen],
            out_specs=[layer_block(shape) for shape in shapes],
            scratch_shapes=[pltpu.VMEM((16, RANK + 8, WIDE), jnp.bfloat16), pltpu.SemaphoreType.DMA((2,))],
        ),
        compiler_params=pltpu.CompilerParams(vmem_limit_bytes=60 << 20),
        cost_estimate=pl.CostEstimate(flops=1 << 29, bytes_accessed=24 << 20, transcendentals=0),
        name="finish",
    )(jnp.stack([place, core]), rate.reshape(1), *early, *late, counts, *firsts, *seconds, *frozen)


def mm(left, right):
    return jnp.dot(left, right, preferred_element_type=jnp.float32)


def mm_nt(left, right):
    return lax.dot_general(left, right, (((1,), (1,)), ((), ())), preferred_element_type=jnp.float32)


def mm_tn(left, right):
    return lax.dot_general(left, right, (((0,), (0,)), ((), ())), preferred_element_type=jnp.float32)


def half(value):
    return value.astype(jnp.bfloat16)


def normalize(value):
    centred = value - jnp.mean(value, axis=-1, keepdims=True)
    scale = lax.rsqrt(jnp.mean(centred * centred, axis=-1, keepdims=True) + norm_eps)
    return centred * scale, scale


def norm_gradient(grad, normal, scale, gain):
    pulled = grad * gain
    inner = pulled - jnp.mean(pulled, axis=-1, keepdims=True)
    return scale * (inner - normal * jnp.mean(pulled * normal, axis=-1, keepdims=True))


def rotary_tables(seq_len):
    half_rot = ROT // 2
    lane = jnp.arange(2 * HEAD_DIM) % HEAD_DIM
    freqs = 10000.0 ** (-((lane % half_rot).astype(jnp.float32) * 2.0 / ROT))
    angles = jnp.arange(seq_len, dtype=jnp.float32)[:, None] * freqs[None, :]
    turning = (lane < ROT)[None, :]
    cosine = jnp.where(turning, jnp.cos(angles), 1.0)
    ahead = jnp.where((lane < half_rot)[None, :], -jnp.sin(angles), 0.0)
    behind = jnp.where(turning & (lane >= half_rot)[None, :], jnp.sin(angles), 0.0)
    return jnp.stack([cosine, ahead, behind])


def tile_table(table, rows, columns):
    return jnp.concatenate([jnp.concatenate([table] * (columns // table.shape[1]), 1)] * rows, 0)


def turn(value, cosine, ahead, behind):
    width = value.shape[1]
    step = ROT // 2
    return value * cosine + pltpu.roll(value, width - step, 1) * ahead + pltpu.roll(value, step, 1) * behind


def turn_back(value, cosine, ahead, behind):
    width = value.shape[1]
    step = ROT // 2
    return value * cosine + pltpu.roll(value * ahead, step, 1) + pltpu.roll(value * behind, width - step, 1)


def stack_heads(pair):
    low = lax.broadcasted_iota(jnp.int32, pair.shape, 1) < HEAD_DIM
    zero = jnp.zeros_like(pair)
    return jnp.concatenate([jnp.where(low, pair, zero), jnp.where(low, zero, pair)], 0)


def merge_heads(stacked):
    rows = stacked.shape[0] // 2
    low = lax.broadcasted_iota(jnp.int32, (rows, stacked.shape[1]), 1) < HEAD_DIM
    return jnp.where(low, stacked[:rows], stacked[rows:])


def pair_mask(seq_len, limit):
    row = lax.broadcasted_iota(jnp.int32, (2 * seq_len, seq_len), 0) % seq_len
    column = lax.broadcasted_iota(jnp.int32, (2 * seq_len, seq_len), 1)
    return (column <= row) & (column < limit)


def pair_softmax(query_stack, key_pair, mask):
    scores = mm_nt(query_stack, key_pair) * HEAD_DIM ** (-0.5)
    scores = jnp.where(mask, scores, masked_score)
    grown = jnp.exp(scores - jnp.max(scores, axis=-1, keepdims=True))
    return grown * (1.0 / jnp.sum(grown, axis=-1, keepdims=True))


GROUP = 8 * HEAD_DIM
BLOCK = 1024
BACK_BLOCK = 2048
PIECE = 256


def attention_forward_kernel(
    facts_ref, x_ref, norm_ref, table_ref, first_ref, wq_ref, wk_ref, wv_ref, bq_ref, bk_ref, bv_ref,
    wo_ref, ao_ref, bo_ref, *refs,
):
    q_out, k_out, v_out, mixed_out, midq_out, mido_out, att_out, a_scr, mid_scr = refs[-9:]
    step = pl.program_id(0)
    seqs = x_ref.shape[0] // table_ref.shape[1]
    seq_len = table_ref.shape[1]

    @pl.when(step == 0)
    def _():
        normal, _ = normalize(x_ref[...])
        a_scr[...] = half(normal * norm_ref[0:1] + norm_ref[2:3])
        midq_out[...] = half(mm(a_scr[...], first_ref[...]))
        att_out[...] = jnp.zeros_like(att_out)
        mid_scr[...] = jnp.zeros_like(mid_scr)

    normed = a_scr[...]
    mid = midq_out[...]
    tables = [tile_table(table_ref[index], seqs, GROUP) for index in range(3)]
    query = mm(normed, wq_ref[...]) + adapter_scale * mm(mid, bq_ref[...])
    q_out[...] = half(turn(query, *tables))
    key = mm(normed, wk_ref[...]) + adapter_scale * mm(mid, bk_ref[...])
    k_out[...] = half(turn(key, *tables))
    v_out[...] = half(mm(normed, wv_ref[...]) + adapter_scale * mm(mid, bv_ref[...]))
    work = []
    for seq in range(seqs):
        rows = slice(seq * seq_len, (seq + 1) * seq_len)
        mask = pair_mask(seq_len, facts_ref[0, seq])
        for pair in range(GROUP // (2 * HEAD_DIM)):
            lanes = slice(pair * 2 * HEAD_DIM, (pair + 1) * 2 * HEAD_DIM)
            work.append((rows, lanes, pair_softmax(stack_heads(q_out[rows, lanes]), k_out[rows, lanes], mask)))
    for rows, lanes, probability in work:
        mixed_out[rows, lanes] = half(merge_heads(mm(half(probability), v_out[rows, lanes])))
    mixed = mixed_out[...]
    att_out[...] += mm(mixed, wo_ref[...])
    mid_scr[...] += mm(mixed, ao_ref[...])

    @pl.when(step == pl.num_programs(0) - 1)
    def _():
        mido_out[...] = half(mid_scr[...])
        att_out[...] += adapter_scale * mm(mido_out[...], bo_ref[...])


def whole(*shape):
    return pl.BlockSpec(shape, lambda step, facts_ref: (0,) * len(shape))


def fixed(height, width, down=0, right=0):
    return pl.BlockSpec((height, width), lambda step, facts_ref: (down, right))


def layer_fixed(layer, height, width, down=0, right=0):
    return pl.BlockSpec((None, height, width), lambda step, facts_ref: (layer, down, right))


def layer_columns(layer, height, width, offset=0):
    return pl.BlockSpec((None, height, width), lambda step, facts_ref: (layer, 0, step + offset))


def layer_rows(layer, height, width, offset=0):
    return pl.BlockSpec((None, height, width), lambda step, facts_ref: (layer, step + offset, 0))


def column_block(height, width, offset=0):
    return pl.BlockSpec((height, width), lambda step, facts_ref: (0, step + offset))


def row_block(height, width, offset=0):
    return pl.BlockSpec((height, width), lambda step, facts_ref: (step + offset, 0))


def kernel_call(kernel, name, steps, in_specs, out_specs, out_shape, scratch, flops, size, exps=0, aliases={}):
    return pl.pallas_call(
        kernel,
        out_shape=out_shape,
        grid_spec=pltpu.PrefetchScalarGridSpec(
            num_scalar_prefetch=1, grid=(steps,), in_specs=in_specs, out_specs=out_specs, scratch_shapes=scratch
        ),
        compiler_params=pltpu.CompilerParams(
            dimension_semantics=("arbitrary",), vmem_limit_bytes=48 << 20
        ),
        input_output_aliases=aliases,
        cost_estimate=pl.CostEstimate(flops=flops, bytes_accessed=size, transcendentals=exps),
        name=name,
    )


def shaped(shape, dtype=jnp.bfloat16):
    return jax.ShapeDtypeStruct(shape, dtype)


def attention_forward(residual, weights, norms, tables, facts, after):
    tokens, width = residual.shape
    groups = width // GROUP
    joint, output = weights[0], weights[1]
    firsts, seconds, _, layer = weights[4:8]
    seq_len = tables.shape[1]
    return kernel_call(
        attention_forward_kernel,
        "attention_forward",
        groups,
        [
            whole(tokens, width),
            whole(4, width),
            whole(3, seq_len, 2 * HEAD_DIM),
            layer_fixed(layer, width, RANK),
            column_block(width, GROUP),
            column_block(width, GROUP, groups),
            column_block(width, GROUP, 2 * groups),
            layer_columns(layer, RANK, GROUP),
            layer_columns(layer, RANK, GROUP, groups),
            layer_columns(layer, RANK, GROUP, 2 * groups),
            row_block(GROUP, width),
            layer_rows(layer, GROUP, RANK, groups),
            layer_fixed(layer, RANK, width, 0, 3),
        ]
        + [pl.BlockSpec(memory_space=pl.ANY)] * len(after),
        [column_block(tokens, GROUP)] * 4 + [whole(tokens, RANK), whole(tokens, RANK), whole(tokens, width)],
        [shaped((tokens, width))] * 4
        + [shaped((tokens, RANK)), shaped((tokens, RANK)), shaped((tokens, width), jnp.float32)],
        [pltpu.VMEM((tokens, width), jnp.bfloat16), pltpu.VMEM((tokens, RANK), jnp.float32)],
        2 * tokens * width * width * 4,
        2 * 5 * width * width + 12 * tokens * width,
    )(
        facts, residual, norms, tables, firsts, joint, joint, joint, seconds, seconds, seconds, output,
        firsts, seconds, *after,
    )


def feed_forward_kernel(
    facts_ref, x_ref, norm_ref, att_ref, first_ref, wu_ref, bu_ref, wd_ref, ad_ref, bd_ref,
    act_out, slope_out, midu_out, midd_out, x_out, sums_out,
    a_scr, mid_scr,
):
    step = pl.program_id(0)

    @pl.when(step == 0)
    def _():
        normal, _ = normalize(x_ref[...])
        a_scr[...] = half(normal * norm_ref[1:2] + norm_ref[3:4])
        midu_out[...] = half(mm(a_scr[...], first_ref[...]))
        x_out[...] = jnp.zeros_like(x_out)
        mid_scr[...] = jnp.zeros_like(mid_scr)

    normed, mid = a_scr[...], midu_out[...]
    parts = [slice(begin, begin + PIECE) for begin in range(0, act_out.shape[1], PIECE)]
    uppers = [mm(normed, wu_ref[:, part]) + adapter_scale * mm(mid, bu_ref[:, part]) for part in parts]
    for upper, part in zip(uppers, parts):
        spread = 0.5 + 0.5 * lax.erf(upper * 0.5**0.5)
        density = jnp.exp(-0.5 * upper * upper) * (0.5 / jnp.pi) ** 0.5
        active = half(upper * spread)
        act_out[:, part] = active
        slope_out[:, part] = half(spread + upper * density)
        x_out[...] += mm(active, wd_ref[part])
        mid_scr[...] += mm(active, ad_ref[part])

    @pl.when(step == pl.num_programs(0) - 1)
    def _():
        midd_out[...] = half(mid_scr[...])
        feed = x_out[...] + adapter_scale * mm(midd_out[...], bd_ref[...])
        attended = att_ref[...]
        residual = x_ref[...]
        x_out[...] = residual + (attended + feed)
        lane = lax.broadcasted_iota(jnp.int32, (1, 128), 1)
        seqs = facts_ref.shape[1]
        seq_len = residual.shape[0] // seqs
        row = lax.broadcasted_iota(jnp.int32, (seq_len, 1), 0)
        parts = []
        for part in (residual, attended, feed):
            squares = jnp.sum(part * part, axis=-1, keepdims=True)
            sums = jnp.zeros((1, 128), jnp.float32)
            for seq in range(seqs):
                valid = jnp.where(row < facts_ref[0, seq], squares[seq * seq_len : (seq + 1) * seq_len], 0.0)
                counted = (lane == facts_ref[1, seq]) | (lane == DOMAINS)
                sums = sums + jnp.where(counted, jnp.sum(valid), 0.0)
            parts.append(sums)
        sums_out[...] = jnp.concatenate(parts + [jnp.zeros((5, 128), jnp.float32)], 0)


def feed_forward(residual, attended, weights, norms, facts):
    tokens, width = residual.shape
    upper, down = weights[2], weights[3]
    firsts, seconds, _, layer = weights[4:8]
    hidden = upper.shape[1]
    return kernel_call(
        feed_forward_kernel,
        "feed_forward",
        hidden // BLOCK,
        [
            whole(tokens, width),
            whole(4, width),
            whole(tokens, width),
            layer_fixed(layer, width, RANK, 2, 0),
            column_block(width, BLOCK),
            layer_columns(layer, RANK, BLOCK, 4 * width // BLOCK),
            row_block(BLOCK, width),
            layer_rows(layer, BLOCK, RANK, 3 * width // BLOCK),
            layer_fixed(layer, RANK, width, 0, 8),
        ],
        [column_block(tokens, BLOCK)] * 2
        + [whole(tokens, RANK), whole(tokens, RANK), whole(tokens, width), whole(8, 128)],
        [shaped((tokens, hidden))] * 2
        + [shaped((tokens, RANK))] * 2
        + [shaped((tokens, width), jnp.float32), shaped((8, 128), jnp.float32)],
        [pltpu.VMEM((tokens, width), jnp.bfloat16), pltpu.VMEM((tokens, RANK), jnp.float32)],
        2 * tokens * width * hidden * 2,
        4 * width * hidden + 4 * tokens * hidden + 12 * tokens * width,
        2 * tokens * hidden,
    )(facts, residual, norms, attended, firsts, upper, seconds, down, firsts, seconds)


def write_extra(block_out, grad, normal, sums):
    width = grad.shape[1]
    row = [jnp.sum(grad * normal, axis=0, keepdims=True), jnp.sum(grad, axis=0, keepdims=True)] + sums
    rest = block_out.shape[1] - sum(part.shape[1] for part in row)
    row = jnp.concatenate(row + [jnp.zeros((1, rest), jnp.float32)], 1)
    block_out[RANK:, :] = half(jnp.concatenate([row, jnp.zeros((7, row.shape[1]), jnp.float32)], 0))


def block_copies(block_out, whole_out, first, sem):
    width = whole_out.shape[2]
    copies = []
    for index in range(block_out.shape[1] // width):
        source = block_out.at[:, pl.ds(index * width, width)]
        copies.append(pltpu.make_async_copy(source, whole_out.at[first + index], sem.at[index]))
        copies[-1].start()
    return copies


def feed_backward_kernel(
    facts_ref, g_ref, x_ref, norm_ref, act_ref, slope_ref, midu_ref, midd_ref, sums_ref, wu_ref, wd_ref, au_ref,
    bu_ref, ad_ref, ad_next_ref, bd_ref,
    whole_out, gx_out,
    block_out, g_scr, gmd_scr, gmdt_scr, midut_scr, gmu_scr, sem,
):
    step = pl.program_id(0)
    width = x_ref.shape[1]
    hidden = pl.num_programs(0) * BACK_BLOCK

    @pl.when(step == 0)
    def _():
        g_scr[...] = half(g_ref[...])
        grad_mid = adapter_scale * mm_nt(g_scr[...], bd_ref[...])
        gmd_scr[...] = half(grad_mid)
        gmdt_scr[...] = half(half(grad_mid).astype(jnp.float32).T)
        midut_scr[...] = half(midu_ref[...].astype(jnp.float32).T)
        gx_out[...] = jnp.zeros_like(gx_out)
        gmu_scr[...] = jnp.zeros_like(gmu_scr)
        middt = half(midd_ref[...].astype(jnp.float32).T)
        block_out[:RANK, pl.ds(width + 2 * hidden, width)] = half(adapter_scale * mm(middt, g_scr[...]))

    grad_act = mm_nt(g_scr[...], wd_ref[...]) + mm_nt(gmd_scr[...], jnp.concatenate([ad_ref[...], ad_next_ref[...]], 0))
    grad_up = half(half(grad_act).astype(jnp.float32) * slope_ref[...].astype(jnp.float32))
    first_at = pl.multiple_of(width + step * BACK_BLOCK, BACK_BLOCK)
    second_at = pl.multiple_of(width + hidden + step * BACK_BLOCK, BACK_BLOCK)
    block_out[:RANK, pl.ds(first_at, BACK_BLOCK)] = half(mm(gmdt_scr[...], act_ref[...]))
    block_out[:RANK, pl.ds(second_at, BACK_BLOCK)] = half(adapter_scale * mm(midut_scr[...], grad_up))
    gmu_scr[...] += mm_nt(grad_up, bu_ref[...])
    gx_out[...] += mm_nt(grad_up, wu_ref[...])

    @pl.when(step == pl.num_programs(0) - 1)
    def _():
        grad_mid = half(adapter_scale * gmu_scr[...])
        normal, scale = normalize(x_ref[...])
        normed = half(normal * norm_ref[1:2] + norm_ref[3:4])
        block_out[:RANK, :width] = half(mm(half(grad_mid.astype(jnp.float32).T), normed))
        grad = gx_out[...] + mm_nt(grad_mid, au_ref[...])
        write_extra(block_out, grad, normal, [sums_ref[index : index + 1] for index in range(3)])
        gather = block_copies(block_out, whole_out, 6, sem)
        gx_out[...] = g_ref[...] + norm_gradient(grad, normal, scale, norm_ref[1:2])
        for copy in gather:
            copy.wait()


def feed_backward(gradient, residual, weights, norms, kept, facts):
    tokens, width = residual.shape
    upper, down = weights[2], weights[3]
    firsts, seconds, _, layer = weights[4:8]
    active, slope, mid_u, mid_d, sums = kept
    hidden = upper.shape[1]
    return kernel_call(
        feed_backward_kernel,
        "feed_backward",
        hidden // BACK_BLOCK,
        [
            whole(tokens, width),
            whole(tokens, width),
            whole(4, width),
            column_block(tokens, BACK_BLOCK),
            column_block(tokens, BACK_BLOCK),
            whole(tokens, RANK),
            whole(tokens, RANK),
            whole(8, 128),
            column_block(width, BACK_BLOCK),
            row_block(BACK_BLOCK, width),
            layer_fixed(layer, width, RANK, 2, 0),
            layer_columns(layer, RANK, BACK_BLOCK, 4 * width // BACK_BLOCK),
            pl.BlockSpec((None, BACK_BLOCK // 2, RANK), lambda step, facts_ref: (layer, 2 * step + 3, 0)),
            pl.BlockSpec((None, BACK_BLOCK // 2, RANK), lambda step, facts_ref: (layer, 2 * step + 4, 0)),
            layer_fixed(layer, RANK, width, 0, 8),
        ],
        [pl.BlockSpec(memory_space=pl.ANY), whole(tokens, width)],
        [shaped((16, RANK + 8, width)), shaped((tokens, width), jnp.float32)],
        [
            pltpu.VMEM((RANK + 8, 2 * width + 2 * hidden), jnp.bfloat16),
            pltpu.VMEM((tokens, width), jnp.bfloat16),
            pltpu.VMEM((tokens, RANK), jnp.bfloat16),
            pltpu.VMEM((RANK, tokens), jnp.bfloat16),
            pltpu.VMEM((RANK, tokens), jnp.bfloat16),
            pltpu.VMEM((tokens, RANK), jnp.float32),
            pltpu.SemaphoreType.DMA((10,)),
        ],
        2 * tokens * width * hidden * 2,
        4 * width * hidden + 4 * tokens * hidden + 16 * tokens * width,
    )(
        facts, gradient, residual, norms, active, slope, mid_u, mid_d, sums, upper, down, firsts, seconds,
        firsts, firsts, seconds,
    )


def attention_backward_kernel(
    facts_ref, g_ref, gx_ref, x_ref, norm_ref, table_ref, q_ref, k_ref, v_ref, mixed_ref, midq_ref, mido_ref,
    wq_ref, wk_ref, wv_ref, aq_ref, bq_ref, bk_ref, bv_ref, wo_ref, ao_ref, bo_ref, feed_block_ref, *refs,
):
    whole_out, gx_out = refs[-13:-11]
    block_out, g_scr, gmo_scr, gmot_scr, midqt_scr, gmq_scr, acc_scr, gq_scr, gk_scr, gv_scr, sem = refs[-11:]
    step = pl.program_id(0)
    width = x_ref.shape[1]
    seq_len = table_ref.shape[1]
    seqs = x_ref.shape[0] // seq_len
    scale_factor = HEAD_DIM ** (-0.5)

    @pl.when(step == 0)
    def _():
        g_scr[...] = half(g_ref[...])
        grad_mid = half(adapter_scale * mm_nt(g_scr[...], bo_ref[...]))
        gmo_scr[...] = grad_mid
        gmot_scr[...] = half(grad_mid.astype(jnp.float32).T)
        midqt_scr[...] = half(midq_ref[...].astype(jnp.float32).T)
        acc_scr[...] = jnp.zeros_like(acc_scr)
        gmq_scr[...] = jnp.zeros_like(gmq_scr)
        midot = half(mido_ref[...].astype(jnp.float32).T)
        block_out[:RANK, pl.ds(5 * width, width)] = half(adapter_scale * mm(midot, g_scr[...]))

    grad_mixed = half(mm_nt(g_scr[...], wo_ref[...]) + mm_nt(gmo_scr[...], ao_ref[...]))
    first_at = pl.multiple_of(width + step * GROUP, GROUP)
    block_out[:RANK, pl.ds(first_at, GROUP)] = half(mm(gmot_scr[...], mixed_ref[...]))
    work = []
    for seq in range(seqs):
        rows = slice(seq * seq_len, (seq + 1) * seq_len)
        mask = pair_mask(seq_len, facts_ref[0, seq])
        for pair in range(GROUP // (2 * HEAD_DIM)):
            lanes = slice(pair * 2 * HEAD_DIM, (pair + 1) * 2 * HEAD_DIM)
            query_stack = stack_heads(q_ref[rows, lanes])
            grad_stack = stack_heads(grad_mixed[rows, lanes])
            probability = pair_softmax(query_stack, k_ref[rows, lanes], mask)
            grad_prob = mm_nt(grad_stack, v_ref[rows, lanes])
            inner = jnp.sum(probability * grad_prob, axis=-1, keepdims=True)
            grad_scores = half(probability * (grad_prob - inner))
            work.append((rows, lanes, query_stack, grad_stack, half(probability), grad_scores))
    for rows, lanes, query_stack, grad_stack, probability, grad_scores in work:
        gv_scr[rows, lanes] = half(mm_tn(probability, grad_stack))
        gq_scr[rows, lanes] = merge_heads(mm(grad_scores, k_ref[rows, lanes])) * scale_factor
        gk_scr[rows, lanes] = mm_tn(grad_scores, query_stack) * scale_factor
    tables = [tile_table(table_ref[index], seqs, GROUP) for index in range(3)]
    joint = (half(turn_back(gq_scr[...], *tables)), half(turn_back(gk_scr[...], *tables)), gv_scr[...])
    mid = midqt_scr[...]
    for index, (grad, w_ref, b_ref) in enumerate(zip(joint, (wq_ref, wk_ref, wv_ref), (bq_ref, bk_ref, bv_ref))):
        second_at = pl.multiple_of((2 + index) * width + step * GROUP, GROUP)
        block_out[:RANK, pl.ds(second_at, GROUP)] = half(adapter_scale * mm(mid, grad))
        gmq_scr[...] += mm_nt(grad, b_ref[...])
        acc_scr[...] += mm_nt(grad, w_ref[...])

    @pl.when(step == pl.num_programs(0) - 1)
    def _():
        grad_mid = half(adapter_scale * gmq_scr[...])
        normal, scale = normalize(x_ref[...])
        normed = half(normal * norm_ref[0:1] + norm_ref[2:3])
        block_out[:RANK, :width] = half(mm(half(grad_mid.astype(jnp.float32).T), normed))
        grad = acc_scr[...] + mm_nt(grad_mid, aq_ref[...])
        write_extra(block_out, grad, normal, [])
        gather = block_copies(block_out, whole_out, 0, sem)
        gx_out[...] = gx_ref[...] + norm_gradient(grad, normal, scale, norm_ref[0:1])
        for copy in gather:
            copy.wait()


def attention_backward(gradient, grad_feed, feed_block, residual, weights, norms, tables, kept, facts, after):
    tokens, width = residual.shape
    groups = width // GROUP
    joint, output = weights[0], weights[1]
    firsts, seconds, _, layer = weights[4:8]
    queries, keys, values, mixed, mid_q, mid_o = kept
    seq_len = tables.shape[1]
    block = column_block(tokens, GROUP)
    return kernel_call(
        attention_backward_kernel,
        "attention_backward",
        groups,
        [
            whole(tokens, width),
            whole(tokens, width),
            whole(tokens, width),
            whole(4, width),
            whole(3, seq_len, 2 * HEAD_DIM),
            block,
            block,
            block,
            block,
            whole(tokens, RANK),
            whole(tokens, RANK),
            column_block(width, GROUP),
            column_block(width, GROUP, groups),
            column_block(width, GROUP, 2 * groups),
            layer_fixed(layer, width, RANK),
            layer_columns(layer, RANK, GROUP),
            layer_columns(layer, RANK, GROUP, groups),
            layer_columns(layer, RANK, GROUP, 2 * groups),
            row_block(GROUP, width),
            layer_rows(layer, GROUP, RANK, groups),
            layer_fixed(layer, RANK, width, 0, 3),
            pl.BlockSpec(memory_space=pl.ANY),
        ]
        + [pl.BlockSpec(memory_space=pl.ANY)] * len(after),
        [pl.BlockSpec(memory_space=pl.ANY), whole(tokens, width)],
        [shaped((16, RANK + 8, width)), shaped((tokens, width), jnp.float32)],
        [
            pltpu.VMEM((RANK + 8, 6 * width), jnp.bfloat16),
            pltpu.VMEM((tokens, width), jnp.bfloat16),
            pltpu.VMEM((tokens, RANK), jnp.bfloat16),
            pltpu.VMEM((RANK, tokens), jnp.bfloat16),
            pltpu.VMEM((RANK, tokens), jnp.bfloat16),
            pltpu.VMEM((tokens, RANK), jnp.float32),
            pltpu.VMEM((tokens, width), jnp.float32),
            pltpu.VMEM((tokens, GROUP), jnp.float32),
            pltpu.VMEM((tokens, GROUP), jnp.float32),
            pltpu.VMEM((tokens, GROUP), jnp.bfloat16),
            pltpu.SemaphoreType.DMA((6,)),
        ],
        2 * tokens * width * width * 4,
        2 * 5 * width * width + 24 * tokens * width,
        aliases={22: 0},
    )(
        facts, gradient, grad_feed, residual, norms, tables, queries, keys, values, mixed, mid_q, mid_o, joint,
        joint, joint, firsts, seconds, seconds, seconds, output, firsts, seconds, feed_block, *after,
    )


def layer_forward(residual, weights, tables, facts, after=()):
    norms = weights[6]
    *kept_attention, attended = attention_forward(residual, weights, norms, tables, facts, after)
    *kept_feed, output, sums = feed_forward(residual, attended, weights, norms, facts)
    return output, (residual, kept_attention, kept_feed + [sums])


def layer_backward(gradient, kept, weights, tables, facts, after=()):
    residual, kept_attention, kept_feed = kept
    norms = weights[6]
    feed_block, grad_feed = feed_backward(gradient, residual, weights, norms, kept_feed, facts)
    block, grad_input = attention_backward(
        gradient, grad_feed, feed_block, residual, weights, norms, tables, kept_attention, facts, after
    )
    return grad_input, block


def gather_plan(gathers, turns):
    if (gathers, turns) == (4, 3):
        return [[0, 2], [0, 2], [0, 1], [2, 1], [1, 3], [3], [3]]
    order = [0, 2, 1, 3]
    return [[order[step // turns]] for step in range(gathers * turns)]


def shards(
    inputs,
    cotangent,
    domain,
    lengths,
    steps_since_reset,
    frozen_query_weight,
    frozen_output_weight,
    frozen_up_weight,
    frozen_down_weight,
    query_adapter_first,
    query_adapter_second,
    output_adapter_first,
    output_adapter_second,
    up_adapter_first,
    up_adapter_second,
    down_adapter_first,
    down_adapter_second,
    layer_norm_gain,
    layer_norm_bias,
):
    core = lax.axis_index("section")
    place = lax.axis_index("dp")
    count = lax.axis_size("dp")
    middle = count // 2
    stage = place // middle
    low = place % middle
    home = core == stage
    masks = [1 << bit for bit in range(middle.bit_length() - 1)]
    frozen = (frozen_query_weight, frozen_output_weight, frozen_up_weight, frozen_down_weight)
    trained = (
        query_adapter_first,
        query_adapter_second,
        output_adapter_first,
        output_adapter_second,
        up_adapter_first,
        up_adapter_second,
        down_adapter_first,
        down_adapter_second,
    )
    local_layers = frozen_query_weight.shape[0]
    rows_dev, seq_len, model_width = inputs.shape
    tokens = rows_dev * seq_len

    places = [(index // middle, index) for index in range(count)]
    to_sibling = [(here * count + index, (1 - here) * count + index) for here, index in places]
    to_cross = [((1 - here) * count + index, here * count + (index ^ middle)) for here, index in places]
    sibling, cross = [partial(both_axes, pairs=pairs) for pairs in (to_sibling, to_cross)]

    same, other = pack_halves(core, frozen)
    swapped_units = flip_core(other)
    own = jnp.where(home, same, swapped_units)
    leaving = jnp.where(home, swapped_units, same)
    partner = [flip_place(leaving[0], middle)]
    for layer in range(1, local_layers):
        partner.append(flip_place(tie(leaving[layer], partner[-1]), middle))
    gathers = []
    for layer in range(local_layers):
        gathers.append(Gather(layer, 0, own[layer], masks))
        gathers.append(Gather(layer, 1, partner[layer], masks))
    plan = gather_plan(len(gathers), len(masks)) + [[]]
    dense = [None] * local_layers
    facts = jnp.stack([lengths, domain])
    norms = jnp.concatenate([layer_norm_gain, layer_norm_bias], 1)
    facts = jnp.where(home, facts, cross(facts))
    norms = jnp.where(home, norms, sibling(norms))
    visiting = jnp.where(stage == 0, cotangent, inputs)
    tables = rotary_tables(seq_len)
    ended, fresh, started, waiting = (), [], set(), []
    bases = [jnp.where(stage == which, 0, middle) for which in range(2)]
    for number, active in enumerate(plan):
        if number == len(plan) - 1:
            start = jnp.where(home, inputs, visiting).astype(jnp.float32).reshape(tokens, model_width)
            while waiting and min(layer for layer, _ in waiting[0][1]) == 0:
                assemble(*waiting.pop(0), count, dense)
            first_weights = tuple(dense[0]) + (packed[0], packed[1], norms[0], 0)
            boundary, _ = layer_forward(start, first_weights, tables, facts)
            ended = ended + (boundary,)
        for index in active:
            if index not in started:
                started.add(index)
                gather = gathers[index]
                fresh = fresh + [(gather.block, part, 1, gather, part, [0]) for part in range(3)]
        extra = []
        if number in (1, 2):
            extra.append((packed[number - 1], sibling))
        if number == 4:
            extra.append((visiting, cross))
        moving = fresh if number >= 2 else []
        there, came, collected, swapped, results = gather_step(
            [gathers[index] for index in active], masks, moving, extra, ended
        )
        fresh = came if moving else fresh + came
        if number == 0:
            packed = list(pack_adapters(trained, swapped_units))
        if number in (1, 2):
            packed[number - 1] = jnp.where(home, packed[number - 1], results[0])
        if number == 4:
            visiting = results[0]
        marks = [assemble(*waiting.pop(0), count, dense)] if waiting and number < len(plan) - 1 else []
        ended = tuple(there) + tuple(results) + tuple(marks)
        if number == 3:
            ended = ended + tuple(packed)
        if moving:
            ended = ended + (swapped,)
            layout = [(gather.layer, part) for _, _, size, gather, part, _ in moving for _ in range(size)]
            places_of = [
                (known ^ low) + bases[gather.which] for _, _, _, gather, _, found in moving for known in found
            ]
            info = jnp.stack([core] + places_of)
            waiting.append((info, layout, collected, swapped))
    for item in waiting:
        assemble(*item, count, dense)
    weights = [tuple(dense[layer]) + (packed[0], packed[1], norms[layer], layer) for layer in range(local_layers)]
    valid = jnp.arange(seq_len)[None, :] < facts[0][:, None]
    end_grad = jnp.where(home, cotangent, visiting).astype(jnp.float32)
    end_grad = jnp.where(stage == 1, end_grad * valid[..., None].astype(jnp.float32), 0.0)
    end_grad = end_grad.reshape(tokens, model_width)
    def stage_forward(residual, after):
        kept = []
        for layer in range(local_layers):
            residual, kept_state = layer_forward(residual, weights[layer], tables, facts, after if layer == 0 else ())
            kept.append(kept_state)
        return residual, kept

    for layer in range(1, local_layers):
        boundary, _ = layer_forward(boundary, weights[layer], tables, facts)
    boundary = boundary.astype(jnp.bfloat16)
    forward_pairs = [(index, index + middle) for index in range(middle)]
    received = lax.ppermute(boundary, "dp", forward_pairs)
    lane = jnp.arange(128)
    counted = (domain[:, None] == lane[None, :]) | (lane == DOMAINS)[None, :]
    counts = jnp.sum(jnp.where(counted, lengths.astype(jnp.float32)[:, None], 0.0), axis=0, keepdims=True)
    for mask in masks + [middle]:
        counts = counts + flip_place(counts, mask)
    counts = jnp.maximum(counts, 1.0) * model_width
    entry = jnp.where(stage == 0, start, received.astype(jnp.float32))
    final, kept = stage_forward(entry, (counts,))
    final = final.astype(jnp.bfloat16)

    gradient = end_grad
    late = [None] * local_layers
    for layer in reversed(range(local_layers)):
        gradient, late[layer] = layer_backward(gradient, kept[layer], weights[layer], tables, facts)
    sent = gradient.astype(jnp.bfloat16)
    came_back = lax.ppermute(sent, "dp", [(after, before) for before, after in forward_pairs])
    late_halves = tie([swap_halves(block, 1, core, count) for block in late], came_back)
    late_piece = sum_halves(late_halves, count)

    gradient = jnp.where(stage == 0, came_back.astype(jnp.float32), 0.0)
    out_pairs = [(count + index + middle, index + middle) for index in range(middle)]
    out_pairs = out_pairs + [(index + middle, count + index) for index in range(middle)]
    visiting = both_axes(jnp.where(core == 0, final, received), out_pairs)
    section_out = jnp.where(home, jnp.where(stage == 0, boundary, final), visiting)
    section_out = section_out.reshape(1, rows_dev, seq_len, model_width)
    pieces = [None] * local_layers
    after = ()
    for layer in reversed(range(local_layers)):
        gradient, block = layer_backward(gradient, kept[layer], weights[layer], tables, facts, after)
        halves = swap_halves(block, 0, core, count)
        if layer == local_layers - 1:
            pieces[layer] = sum_halves([tie(halves, late_piece)], count)
            late_piece = cross_section(late_piece, 1, stage, count)
            after = (late_piece,)
        else:
            if layer == 0:
                late_whole = spread_section(tie(late_piece, pieces[local_layers - 1]), 1, count)
                halves = tie(halves, late_whole[1])
            pieces[layer] = sum_halves([halves], count)
            after = ()
    early_piece = cross_section(jnp.concatenate(pieces, 0), 0, stage, count)
    early_whole = spread_section(early_piece, 0, count)

    grad_pairs = [(index, count + index) for index in range(middle)]
    grad_pairs = grad_pairs + [(count + index, index + middle) for index in range(middle)]
    visiting = both_axes(jnp.where(core == 0, came_back, gradient.astype(jnp.bfloat16)), grad_pairs)
    section_grad = jnp.where(
        home, jnp.where(stage == 0, gradient, sent.astype(jnp.float32)), visiting.astype(jnp.float32)
    )
    section_grad = section_grad.reshape(1, rows_dev, seq_len, model_width)

    rate = peak_rate * (steps_since_reset[0].astype(jnp.float32) + 1.0) / WARM
    outputs = finish(place, core, rate, early_whole, late_whole, counts, trained, frozen)
    *outputs, rms = outputs
    return (section_out, section_grad, *outputs, rms[:, :, : DOMAINS + 1])


def solution(mesh):
    across = P("dp", None, None)
    copied = P("section", None, None)
    split = P("section", "dp", None)
    wide = P("section", "dp", None, None)
    return jax.shard_map(
        shards,
        mesh=mesh,
        in_specs=(across, across, P("dp"), P("dp"), P()) + (split,) * 4 + (copied,) * 10,
        out_specs=(wide, wide) + (copied,) * 10 + (split,) * 4 + (copied,),
        check_vma=False,
    )
```
